128 devices in a mesh: seq: 8 (over y, core), lat: 16 (over z, x).
Axes of the slice: x: 4, y: 4, z: 4, core: 2. Of those that a mesh axis runs over, the one named last changes fastest.
Arguments:
- resid: bfloat16 [1024, 5376], P('seq'), may hold values from -6 to 6
- w_enc: bfloat16 [5376, 65536], P(None, ('seq', 'lat')), may hold values from -0.078125 to 0.078125
- b_enc: float32 [65536], P(('seq', 'lat')), may hold values from -1.5 to 1.5
- threshold: float32 [65536], P(('seq', 'lat')), may hold values from 0.8 to 2
- w_dec: bfloat16 [65536, 5376], P(('seq', 'lat')), may hold values from -0.125 to 0.125
- b_dec: float32 [5376], replicated, may hold values from -3 to 3
- clamp_ids: int32 [16], replicated, may hold values from 0 to 65535, as said below
- clamp_index: int32 [16], replicated, may hold values from 0 to 7
- clamp_table: float32 [8], replicated, may hold values from 2 to 8
- pre_gain: float32 [5376], replicated, may hold values from 0.1 to 1.9
- w_query: bfloat16 [5376, 4096], P(None, 'lat'), may hold values from -0.078125 to 0.078125
- w_key: bfloat16 [5376, 2048], P(None, 'lat'), may hold values from -0.078125 to 0.078125
- w_value: bfloat16 [5376, 2048], P(None, 'lat'), may hold values from -0.078125 to 0.078125
- q_gain: float32 [128], replicated, may hold values from 0.8 to 8
- k_gain: float32 [128], replicated, may hold values from 0.8 to 8
- cache_key: bfloat16 [512, 2048], P('seq', 'lat'), may hold values from -6 to 6
- cache_value: bfloat16 [512, 2048], P('seq', 'lat'), may hold values from -6 to 6
- starts: int32 [1024], P('seq'), may hold values from 0 to 1535, as said below
- w_out: bfloat16 [4096, 5376], P('lat'), may hold values from -0.09375 to 0.09375
- post_gain: float32 [5376], replicated, may hold values from 0.25 to 1.75
Outputs:
- layer_out: bfloat16 [1024, 5376], P(('seq', 'lat'))
The draws below stay inside these ranges and needn't reach their ends.
Inputs may be any that keep to these rules, and one draw needn't show every extreme that they name: `clamp_ids`: distinct latent ids. Never falls along the tokens; starts[t] <= 512 + t; the first new token's document begins at context index 0.
All inputs are finite; a program needn't handle non-finite values.
Results may differ from the reference program's by a relative error of at most 0.028.
Values may be sent and summed in bfloat16 or wider, within the bound.
No kernel may reach another device: no remote copies, remote signals or barrier semaphores. Data moves between devices by JAX's collectives and lax.ppermute only.
A program may use at most 128 MiB of HBM per device.

```python
import math
import jax
import jax.numpy as jnp
from jax import lax

D = 5376
HD = 128
HEADS = 32
KV_HEADS = 16
WINDOW = 1024
LAT_DEV = 512
LATENTS = 65536
TOK_DEV = 128
TOKENS = 1024
PREFIX = 512
NCLAMP = 16
NVALS = 8
N_SEQ = 8
N_LAT = 16


def draw_starts(key, part):
    first_key = jax.random.fold_in(key, 5)
    second_key = jax.random.fold_in(key, 7)
    flags = jax.random.randint(first_key, (TOKENS,), 0, TOK_DEV) == 0
    forced = jax.random.randint(second_key, (), TOKENS // 2, TOKENS)
    flags = flags | (jnp.arange(TOKENS, dtype=jnp.int32) == forced)
    flags = flags.at[0].set(False).at[TOKENS - 1].set(True)
    marks = jnp.where(flags, jnp.arange(TOKENS, dtype=jnp.int32) + PREFIX, 0)
    return lax.cummax(marks).astype(jnp.int32)


def draw_clamp_ids(key, part):
    return jax.random.permutation(key, LATENTS)[:NCLAMP].astype(jnp.int32)


def gain_draw(key):
    low = jnp.log(jnp.float32(0.8))
    high = jnp.log(jnp.float32(4.0))
    return jnp.exp(jax.random.uniform(key, (HD,), jnp.float32, low, high))


def draw_q_gain(key, part):
    return gain_draw(jax.random.fold_in(key, 11))


def draw_k_gain(key, part):
    return gain_draw(jax.random.fold_in(key, 23))


def plant(array, own_key, least, largest):
    dims = array.shape
    spot = [jax.random.randint(jax.random.fold_in(own_key, axis), (), 0, dims[axis]) for axis in range(len(dims))]
    array = array.at[tuple(spot)].set(least)
    longest = dims.index(max(dims))
    spot[longest] = (spot[longest] + 1) % dims[longest]
    return array.at[tuple(spot)].set(largest)


def levels(own_key, dims, split, low, largest):
    level = 1.0
    for dim, shards_of in split:
        draws = jax.random.uniform(jax.random.fold_in(jax.random.fold_in(own_key, 6), dim), (shards_of,), jnp.float32, low / len(split), largest / len(split))
        level = level * jnp.repeat(jnp.exp(draws), dims[dim] // shards_of).reshape((-1,) + (1,) * (len(dims) - 1 - dim))
    return level


def scatter_about(rng, extent, width, limit, pieces=(), held_as=jnp.bfloat16):
    level = levels(rng, extent, pieces, -0.22, 0.18) if pieces else 1.0
    drawn = jax.random.normal(rng, extent, jnp.float32) * width * level
    return jnp.minimum(jnp.maximum(drawn, -limit), limit).astype(held_as)


def setup_inputs(seed: int = 0) -> dict:
    splits = jax.random.split(jax.random.key(seed), 21)
    return {
        "resid": scatter_about(splits[0], (TOKENS, D), 1.0, 6.0, ((0, 8),)),
        "w_enc": scatter_about(splits[1], (D, LATENTS), D ** -0.5, 0.078125, ((1, 128),)),
        "b_enc": scatter_about(splits[2], (LATENTS,), 0.3, 1.5, ((0, 128),), jnp.float32),
        "threshold": jnp.clip(jnp.exp(math.log(2.0) - 0.9162907 * jax.random.uniform(splits[3], (LATENTS,), jnp.float32) ** levels(splits[3], (LATENTS,), ((0, 128),), -0.2, 0.2)), 0.8, 2.0),
        "w_dec": scatter_about(splits[4], (LATENTS, D), 2048 ** -0.5, 0.125, ((0, 128),)),
        "b_dec": scatter_about(splits[5], (D,), 0.5, 3.0, (), jnp.float32),
        "clamp_ids": draw_clamp_ids(jax.random.fold_in(splits[20], 71), 0),
        "clamp_index": plant(jax.random.randint(splits[7], (NCLAMP,), 0, NVALS), jax.random.fold_in(splits[7], 1), 0, NVALS - 1).astype(jnp.int32),
        "clamp_table": jnp.clip(jax.random.uniform(splits[8], (NVALS,), jnp.float32, 2.0, 8.0), 2.0, 8.0),
        "pre_gain": jnp.clip(1.0 + 0.18 * jax.random.normal(splits[9], (D,), jnp.float32), 0.1, 1.9),
        "w_query": scatter_about(splits[10], (D, HEADS * HD), D ** -0.5, 0.078125, ((1, 16),)),
        "w_key": scatter_about(splits[11], (D, KV_HEADS * HD), D ** -0.5, 0.078125, ((1, 16),)),
        "w_value": scatter_about(splits[12], (D, KV_HEADS * HD), D ** -0.5, 0.078125, ((1, 16),)),
        "q_gain": draw_q_gain(jax.random.fold_in(splits[20], 71), 0),
        "k_gain": draw_k_gain(jax.random.fold_in(splits[20], 71), 0),
        "cache_key": scatter_about(splits[15], (PREFIX, KV_HEADS * HD), 1.0, 6.0, ((0, 8), (1, 16))),
        "cache_value": scatter_about(splits[16], (PREFIX, KV_HEADS * HD), 1.0, 6.0, ((0, 8), (1, 16))),
        "starts": draw_starts(jax.random.fold_in(splits[20], 71), 0),
        "w_out": scatter_about(splits[18], (HEADS * HD, D), (HEADS * HD) ** -0.5, 0.09375, ((0, 16),)),
        "post_gain": jnp.clip(1.0 + 0.15 * jax.random.normal(splits[19], (D,), jnp.float32), 0.25, 1.75),
    }


EPS = 1e-06
THETA = 10000.0
QUERY_SCALE = 168.0 ** (-0.5)

def rms_scale(values, gain):
    return values * lax.rsqrt(lax.optimization_barrier(jnp.mean(values * values, axis=-1, keepdims=True)) + EPS) * gain

def rotate(values, positions):
    half = values.shape[-1] // 2
    freq = THETA ** (-(jnp.arange(half, dtype=jnp.float32) * 2.0 / values.shape[-1]))
    angle = positions[:, None] * freq[None, :]
    cosine = jnp.cos(angle)[:, None, :]
    sine = jnp.sin(angle)[:, None, :]
    first = values[..., :half]
    second = values[..., half:]
    return jnp.concatenate([first * cosine - second * sine, second * cosine + first * sine], axis=-1)

def reference(resid, w_enc, b_enc, threshold, w_dec, b_dec, clamp_ids, clamp_index, clamp_table, pre_gain, w_query, w_key, w_value, q_gain, k_gain, cache_key, cache_value, starts, w_out, post_gain):
    table_pick = clamp_index[:, None] == jnp.arange(NVALS, dtype=jnp.int32)[None, :]
    values = lax.optimization_barrier(jnp.sum(jnp.where(table_pick, clamp_table[None, :], 0.0), axis=1))

    def block(recon, index):
        first = (index * LAT_DEV).astype(jnp.int32)
        encoder = lax.dynamic_slice_in_dim(w_enc, first, LAT_DEV, 1)
        pre = jnp.dot(resid, encoder, preferred_element_type=jnp.float32) + lax.dynamic_slice_in_dim(b_enc, first, LAT_DEV, 0)
        act = jnp.maximum(pre - lax.dynamic_slice_in_dim(threshold, first, LAT_DEV, 0), 0.0)
        match = (first + jnp.arange(LAT_DEV, dtype=jnp.int32))[None, :] == clamp_ids[:, None]
        level = lax.optimization_barrier(jnp.sum(jnp.where(match, values[:, None], 0.0), axis=0))
        codes = jnp.where(jnp.any(match, axis=0)[None, :], level[None, :], act).astype(jnp.bfloat16)
        decoder = lax.dynamic_slice_in_dim(w_dec, first, LAT_DEV, 0)
        return (recon + jnp.dot(codes, decoder, preferred_element_type=jnp.float32), None)
    recon, _ = lax.scan(block, jnp.zeros((TOKENS, D), jnp.float32), jnp.arange(N_SEQ * N_LAT, dtype=jnp.int32))
    restored = (recon + b_dec).astype(jnp.bfloat16)
    normed = rms_scale(restored.astype(jnp.float32), pre_gain).astype(jnp.bfloat16)
    positions = PREFIX + jnp.arange(TOKENS, dtype=jnp.int32)
    angles = positions.astype(jnp.float32)
    query = jnp.dot(normed, w_query, preferred_element_type=jnp.float32).reshape(TOKENS, HEADS, HD)
    query = rotate(rms_scale(query, q_gain), angles).astype(jnp.bfloat16)
    key = jnp.dot(normed, w_key, preferred_element_type=jnp.float32).reshape(TOKENS, KV_HEADS, HD)
    key = rotate(rms_scale(key, k_gain), angles).astype(jnp.bfloat16)
    value = jnp.dot(normed, w_value, preferred_element_type=jnp.float32).astype(jnp.bfloat16).reshape(TOKENS, KV_HEADS, HD)
    keys_all = jnp.concatenate([cache_key.reshape(PREFIX, KV_HEADS, HD), key], axis=0)
    values_all = jnp.concatenate([cache_value.reshape(PREFIX, KV_HEADS, HD), value], axis=0)
    context = jnp.arange(PREFIX + TOKENS, dtype=jnp.int32)
    allowed = (context[None, :] <= positions[:, None]) & (context[None, :] > positions[:, None] - WINDOW) & (context[None, :] >= starts[:, None])
    group = HEADS // KV_HEADS
    grouped = query.reshape(TOKENS, KV_HEADS, group, HD).transpose(1, 0, 2, 3)

    def attend(operands):
        q_part, k_part, v_part = operands
        scores = jnp.einsum('tgd,kd->gtk', q_part.astype(jnp.float32), k_part.astype(jnp.float32)) * QUERY_SCALE
        top = lax.optimization_barrier(jnp.max(jnp.where(allowed[None], scores, -1e+30), axis=-1, keepdims=True))
        weights = jnp.where(allowed[None], jnp.exp(scores - top), 0.0)
        total = lax.optimization_barrier(jnp.sum(weights, axis=-1, keepdims=True))
        rounded = lax.optimization_barrier(weights.astype(jnp.bfloat16)).astype(jnp.float32)
        mixed = jnp.einsum('gtk,kd->gtd', rounded, v_part.astype(jnp.float32))
        return mixed / total
    heads_out = lax.map(attend, (grouped, keys_all.transpose(1, 0, 2), values_all.transpose(1, 0, 2)))
    attended = heads_out.transpose(2, 0, 1, 3).reshape(TOKENS, HEADS * HD).astype(jnp.bfloat16)
    mixed = jnp.dot(attended, w_out, preferred_element_type=jnp.float32)
    return (restored.astype(jnp.float32) + rms_scale(mixed, post_gain)).astype(jnp.bfloat16)
```

```python
import functools

import jax
import jax.numpy as jnp
from jax import lax
from jax.experimental import pallas as pl
from jax.experimental.pallas import tpu as pltpu
from jax.sharding import PartitionSpec as P

WINDOW = 1024
PREFIX = 512
EPS = 1e-06
THETA = 10000.0
QUERY_SCALE = 168.0 ** (-0.5)

NY, NC, NZ, NX = 4, 2, 4, 4
AXES = ("seq", "lat")
TILE = 384
F32, BF16 = jnp.float32, jnp.bfloat16


def first_bits(core):
    return 1 if core == 0 else 3


def second_bits(core):
    return 3 if core == 0 else 1


def exchange(value, dim, bits):
    pairs = []
    for y in range(NY):
        for c in range(NC):
            for z in range(NZ):
                for x in range(NX):
                    to = {"y": y, "c": c, "z": z, "x": x}
                    to[dim] ^= bits(c)
                    pairs.append(
                        (
                            (y * NC + c) * NZ * NX + z * NX + x,
                            (to["y"] * NC + to["c"]) * NZ * NX + to["z"] * NX + to["x"],
                        )
                    )
    return lax.ppermute(value, AXES, pairs)


def swap_cores(value):
    return exchange(value, "c", lambda core: 1)


def relative(place, core):
    step = jnp.arange(4, dtype=jnp.int32)
    order0 = jnp.where(step == 1, 3, jnp.where(step == 2, 1, jnp.where(step == 3, 2, 0)))
    order1 = jnp.where(step == 1, 1, jnp.where(step == 2, 3, jnp.where(step == 3, 2, 0)))
    return place ^ jnp.where(core == 0, order0, order1)


def row_order(z, x, core):
    zs, xs = relative(z, core), relative(x, core)
    row = (zs[:, None] * NX + xs[None, :])[:, :, None] * 8 + jnp.arange(8, dtype=jnp.int32)
    return row.reshape(-1)


def rms_scale(values, gain):
    return values * lax.rsqrt(jnp.mean(values * values, axis=-1, keepdims=True) + EPS) * gain


def rotate(values, positions):
    half = values.shape[-1] // 2
    freq = THETA ** (-(jnp.arange(half, dtype=F32) * 2.0 / values.shape[-1]))
    angle = positions[:, None] * freq[None, :]
    cosine = jnp.cos(angle)[:, None, :]
    sine = jnp.sin(angle)[:, None, :]
    first = values[..., :half]
    second = values[..., half:]
    return jnp.concatenate(
        [first * cosine - second * sine, second * cosine + first * sine], axis=-1
    )


def encode_kernel(count, *refs):
    blocks, (own_ref, sib_ref, params_ref, codes_ref, rows_ref) = refs[:count], refs[count:]
    step = pl.program_id(0)
    half = pl.num_programs(0) // 2
    size = blocks[0].shape[0]

    @pl.when(step == 0)
    def _():
        for i in range(count):
            rows_ref[i * size : (i + 1) * size, :] = blocks[i][...]

    def tile(weights_ref):
        pre = jnp.dot(rows_ref[...], weights_ref[...], preferred_element_type=F32)
        pre = pre + params_ref[0:1, :]
        act = jnp.maximum(pre - params_ref[1:2, :], 0.0)
        codes = jnp.where(params_ref[2:3, :] > 0.0, params_ref[3:4, :], act)
        codes_ref[...] = codes.astype(BF16)

    @pl.when(step < half)
    def _():
        tile(own_ref)

    @pl.when(step >= half)
    def _():
        tile(sib_ref)


def encode(blocks, own, sib, params):
    count = len(blocks)
    size, width = blocks[0].shape
    lats = own.shape[1]
    cols = 256
    half = lats // cols
    return pl.pallas_call(
        functools.partial(encode_kernel, count),
        name="encode",
        out_shape=jax.ShapeDtypeStruct((count * size, 2 * lats), BF16),
        grid=(2 * half,),
        in_specs=[pl.BlockSpec((size, width), lambda j: (0, 0), pipeline_mode=pl.Buffered(1))]
        * count
        + [
            pl.BlockSpec((width, cols), lambda j: (0, jnp.minimum(j, half - 1))),
            pl.BlockSpec((width, cols), lambda j: (0, jnp.maximum(j - half, 0))),
            pl.BlockSpec((4, cols), lambda j: (0, j)),
        ],
        out_specs=pl.BlockSpec((count * size, cols), lambda j: (0, j)),
        scratch_shapes=[pltpu.VMEM((count * size, width), BF16)],
        compiler_params=pltpu.CompilerParams(vmem_limit_bytes=32 * 1024 * 1024),
        cost_estimate=pl.CostEstimate(
            flops=4 * count * size * width * lats,
            bytes_accessed=4 * width * lats + 2 * count * size * (width + 2 * lats),
            transcendentals=0,
        ),
    )(*blocks, own, sib, params)


def decode_kernel(group, *refs):
    early_ref, late_ref, own_ref, sib_ref, keep_ref, send_ref, rows_ref = refs
    size = early_ref.shape[0]
    lats = own_ref.shape[0]

    @pl.when(pl.program_id(0) == 0)
    def _():
        rows_ref[:size, :] = early_ref[...]
        rows_ref[size:, :] = late_ref[...]

    total = jnp.dot(rows_ref[:, :lats], own_ref[...], preferred_element_type=F32)
    total += jnp.dot(rows_ref[:, lats:], sib_ref[...], preferred_element_type=F32)
    total = total.astype(BF16)
    half = group // 2
    for i in range(2 * size // group):
        keep_ref[i * half : (i + 1) * half, :] = total[i * group : i * group + half, :]
        send_ref[i * half : (i + 1) * half, :] = total[i * group + half : (i + 1) * group, :]


def decode(early, late, own, sib, part, group):
    size = early.shape[0]
    lats, width = own.shape
    tiles = width // 2 // TILE
    out = jax.ShapeDtypeStruct((size, width // 2), BF16)
    return pl.pallas_call(
        functools.partial(decode_kernel, group),
        name="decode",
        out_shape=(out, out),
        grid=(tiles,),
        in_specs=[pl.BlockSpec(early.shape, lambda j: (0, 0), pipeline_mode=pl.Buffered(1))] * 2
        + [pl.BlockSpec((lats, TILE), lambda j: (0, j + part * tiles))] * 2,
        out_specs=[pl.BlockSpec((size, TILE), lambda j: (0, j))] * 2,
        scratch_shapes=[pltpu.VMEM((2 * size, 2 * lats), BF16)],
        compiler_params=pltpu.CompilerParams(vmem_limit_bytes=32 * 1024 * 1024),
        cost_estimate=pl.CostEstimate(
            flops=4 * size * lats * width,
            bytes_accessed=2 * (lats * width + 2 * size * lats * 2 + size * width),
            transcendentals=0,
        ),
    )(early, late, own, sib)


def split(value, group):
    rows, width = value.shape
    grouped = value.reshape(rows // group, group, width)
    half = group // 2
    return (
        grouped[:, :half].reshape(rows // 2, width),
        grouped[:, half:].reshape(rows // 2, width),
    )


def add(left, right):
    return (left.astype(F32) + right.astype(F32)).astype(BF16)


def reduce_step(value, dim, bits, group):
    keep, send = split(value, group)
    return add(keep, exchange(send, dim, bits))


def swap_halves(value, group):
    keep, send = split(value, group)
    rows, width = value.shape
    half = group // 2
    return jnp.concatenate(
        [send.reshape(-1, half, width), keep.reshape(-1, half, width)], axis=1
    ).reshape(rows, width)


def sum_over(value, dim, unit):
    value = add(value, swap_halves(exchange(value, dim, first_bits), 4 * unit))
    other = swap_halves(exchange(value, dim, second_bits), 2 * unit)
    return value.astype(F32) + other.astype(F32)


def gather_step(value, dim, bits, group):
    other = exchange(value, dim, bits)
    rows, width = value.shape
    return jnp.concatenate(
        [value.reshape(-1, group, width), other.reshape(-1, group, width)], axis=1
    ).reshape(2 * rows, width)


def per_device(
    resid,
    w_enc,
    b_enc,
    threshold,
    w_dec,
    b_dec,
    clamp_ids,
    clamp_index,
    clamp_table,
    pre_gain,
    w_query,
    w_key,
    w_value,
    q_gain,
    k_gain,
    cache_key,
    cache_value,
    starts,
    w_out,
    post_gain,
):
    seq_place = lax.axis_index("seq")
    lat_place = lax.axis_index("lat")
    core = seq_place % NC
    z, x = lat_place // NX, lat_place % NX
    tok_rows, width = resid.shape
    part = width // 2
    lats = w_enc.shape[1]
    head_size = q_gain.shape[0]
    heads_here = w_query.shape[1] // head_size

    order = row_order(z, x, core)
    pick = order[:, None] == jnp.arange(tok_rows, dtype=jnp.int32)[None, :]

    with jax.named_scope("gather_resid"):
        own = jnp.dot(pick.astype(BF16), resid, preferred_element_type=F32).astype(BF16)
        near = exchange(own, "y", first_bits)
        far = exchange(own, "y", second_bits)
        opposite = exchange(near, "y", second_bits)

    with jax.named_scope("swap_weights"):
        offsets = jnp.stack([b_enc, threshold])
        sib_offsets = swap_cores(offsets)
        sib_enc = swap_cores(w_enc)
        sib_dec = swap_cores(w_dec)

    with jax.named_scope("clamp"):
        table_pick = (
            clamp_index[:, None] == jnp.arange(clamp_table.shape[0], dtype=jnp.int32)[None, :]
        )
        values = jnp.sum(jnp.where(table_pick, clamp_table[None, :], 0.0), axis=1)
        spread = jnp.arange(lats, dtype=jnp.int32)
        here = jnp.concatenate(
            [
                (seq_place * NZ * NX + lat_place) * lats + spread,
                ((seq_place ^ 1) * NZ * NX + lat_place) * lats + spread,
            ]
        )
        match = here[None, :] == clamp_ids[:, None]
        clamped = jnp.any(match, axis=0).astype(F32)
        level = jnp.sum(jnp.where(match, values[:, None], 0.0), axis=0)
        params = jnp.concatenate(
            [
                jnp.concatenate([offsets, sib_offsets], axis=1),
                clamped[None, :],
                level[None, :],
            ],
            axis=0,
        )

    with jax.named_scope("codes"):
        early = encode([own, near], w_enc, sib_enc, params)
        late = encode([far, opposite], w_enc, sib_enc, params)

    with jax.named_scope("decode_and_sum"):
        keep_z, send_z = decode(early, late, w_dec, sib_dec, 0, 128)
        keep_x, send_x = decode(early, late, w_dec, sib_dec, 1, 32)
        sum_z = add(keep_z, exchange(send_z, "z", first_bits))
        sum_x = add(keep_x, exchange(send_x, "x", first_bits))
        sum_z = reduce_step(sum_z, "z", second_bits, 64)
        sum_x = reduce_step(sum_x, "x", second_bits, 16)
        both = jnp.concatenate([sum_z, sum_x], axis=1)
        both = reduce_step(both, "y", second_bits, tok_rows)
        both = reduce_step(both, "y", first_bits, tok_rows // 2)
        sum_z = sum_over(both[:, :part], "x", 8)
        sum_x = sum_over(both[:, part:], "z", 8)
        rest_z = (sum_z + b_dec[:part]).astype(BF16)
        rest_x = (sum_x + b_dec[part:]).astype(BF16)
        restored = jnp.concatenate([rest_z[:8], rest_x[:8]], axis=1)

    with jax.named_scope("gather_restored"):
        rest_z = gather_step(rest_z, "z", second_bits, 32)
        rest_x = gather_step(rest_x, "x", second_bits, 8)
        rest_z = gather_step(rest_z, "z", first_bits, 64)
        rest_x = gather_step(rest_x, "x", first_bits, 16)
        shard_rows = jnp.concatenate([rest_z, rest_x], axis=1)

    with jax.named_scope("projections"):
        normed = rms_scale(shard_rows.astype(F32), pre_gain).astype(BF16)
        query_ctx = PREFIX + seq_place * tok_rows + order
        angles = query_ctx.astype(F32)
        query = jnp.dot(normed, w_query, preferred_element_type=F32).reshape(
            tok_rows, heads_here, head_size
        )
        query = rotate(rms_scale(query, q_gain), angles).astype(BF16)
        key_new = jnp.dot(normed, w_key, preferred_element_type=F32).reshape(
            tok_rows, 1, head_size
        )
        key_new = (
            rotate(rms_scale(key_new, k_gain), angles).astype(BF16).reshape(tok_rows, head_size)
        )
        value_new = jnp.dot(normed, w_value, preferred_element_type=F32).astype(BF16)

    with jax.named_scope("attention"):
        pre_rows = cache_key.shape[0]
        own_pairs = jnp.concatenate(
            [
                jnp.concatenate([cache_key, cache_value], axis=1),
                jnp.concatenate([key_new, value_new], axis=1),
            ],
            axis=0,
        )
        pairs = lax.all_gather(own_pairs, "seq", axis=0, tiled=True)
        keys, vals = pairs[:, :head_size], pairs[:, head_size:]
        orders = jnp.stack([row_order(z, x, jnp.int32(i)) for i in range(NC)])
        shard = jnp.arange(NY * NC, dtype=jnp.int32)
        new_ctx = PREFIX + shard[:, None] * tok_rows + jnp.tile(orders, (NY, 1))
        old_ctx = shard[:, None] * pre_rows + jnp.arange(pre_rows, dtype=jnp.int32)[None, :]
        key_ctx = jnp.concatenate([old_ctx, new_ctx], axis=1).reshape(-1)
        first_ctx = jnp.sum(jnp.where(pick, starts[None, :], 0), axis=1)
        scores = (
            jnp.einsum("tgd,kd->gtk", query, keys, preferred_element_type=F32) * QUERY_SCALE
        )
        allowed = (
            (key_ctx[None, :] <= query_ctx[:, None])
            & (key_ctx[None, :] > query_ctx[:, None] - WINDOW)
            & (key_ctx[None, :] >= first_ctx[:, None])
        )
        newest = jnp.max(jnp.where(allowed[None], scores, -1e30), axis=-1)
        weights = jnp.where(allowed[None], jnp.exp(scores - newest[..., None]), 0.0)
        total = jnp.sum(weights, axis=-1)
        accum = jnp.einsum(
            "gtk,kd->gtd", weights.astype(BF16), vals, preferred_element_type=F32
        )
        attended = (
            (accum / total[..., None])
            .transpose(1, 0, 2)
            .reshape(tok_rows, heads_here * head_size)
            .astype(BF16)
        )

    with jax.named_scope("project_out"):
        out_z = jnp.dot(attended, w_out[:, :part], preferred_element_type=F32).astype(BF16)
        out_x = jnp.dot(attended, w_out[:, part:], preferred_element_type=F32).astype(BF16)
        out_z = reduce_step(out_z, "z", first_bits, 128)
        out_x = reduce_step(out_x, "x", first_bits, 32)
        out_z = reduce_step(out_z, "z", second_bits, 64)
        out_x = reduce_step(out_x, "x", second_bits, 16)
        out_z = reduce_step(out_z, "x", first_bits, 32)
        out_x = reduce_step(out_x, "z", first_bits, 32)
        keep_z, send_z = split(out_z, 16)
        keep_x, send_x = split(out_x, 16)
        mine_z = keep_z.astype(F32) + exchange(send_z, "x", second_bits).astype(F32)
        mine_x = keep_x.astype(F32) + exchange(send_x, "z", second_bits).astype(F32)
        mine = jnp.concatenate([mine_z, mine_x], axis=1)
        return (restored.astype(F32) + rms_scale(mine, post_gain)).astype(BF16)


def solution(mesh):
    in_specs = (
        P("seq", None),
        P(None, ("seq", "lat")),
        P(("seq", "lat")),
        P(("seq", "lat")),
        P(("seq", "lat"), None),
        P(),
        P(),
        P(),
        P(),
        P(),
        P(None, "lat"),
        P(None, "lat"),
        P(None, "lat"),
        P(),
        P(),
        P("seq", "lat"),
        P("seq", "lat"),
        P("seq"),
        P("lat", None),
        P(),
    )
    out_specs = P(("seq", "lat"), None)
    return jax.shard_map(
        per_device, mesh=mesh, in_specs=in_specs, out_specs=out_specs, check_vma=False
    )
```

```python
import functools

import jax
import jax.numpy as jnp
from jax import lax
from jax.experimental import pallas as pl
from jax.experimental.pallas import tpu as pltpu
from jax.sharding import PartitionSpec as P

WINDOW = 1024
PREFIX = 512
EPS = 1e-06
THETA = 10000.0
QUERY_SCALE = 168.0 ** (-0.5)

NY, NC, NZ, NX = 4, 2, 4, 4
AXES = ("seq", "lat")
TILE = 896
F32, BF16 = jnp.float32, jnp.bfloat16


def first_bits(core):
    return 1 if core == 0 else 3


def second_bits(core):
    return 3 if core == 0 else 1


def exchange(value, dim, bits):
    pairs = []
    for y in range(NY):
        for c in range(NC):
            for z in range(NZ):
                for x in range(NX):
                    to = {"y": y, "c": c, "z": z, "x": x}
                    to[dim] ^= bits(c)
                    pairs.append(
                        (
                            (y * NC + c) * NZ * NX + z * NX + x,
                            (to["y"] * NC + to["c"]) * NZ * NX + to["z"] * NX + to["x"],
                        )
                    )
    return lax.ppermute(value, AXES, pairs)


def swap_cores(value):
    return exchange(value, "c", lambda core: 1)


def relative(place, core):
    step = jnp.arange(4, dtype=jnp.int32)
    order0 = jnp.where(step == 1, 3, jnp.where(step == 2, 1, jnp.where(step == 3, 2, 0)))
    order1 = jnp.where(step == 1, 1, jnp.where(step == 2, 3, jnp.where(step == 3, 2, 0)))
    return place ^ jnp.where(core == 0, order0, order1)


def row_order(z, x, core):
    zs, xs = relative(z, core), relative(x, core)
    row = (zs[:, None] * NX + xs[None, :])[:, :, None] * 8 + jnp.arange(8, dtype=jnp.int32)
    return row.reshape(-1)


def rms_scale(values, gain):
    return values * lax.rsqrt(jnp.mean(values * values, axis=-1, keepdims=True) + EPS) * gain


def encode_kernel(count, *refs):
    blocks = refs[:count]
    own_ref, sib_ref, params_ref, pick_ref, codes_ref, rows_ref, total_ref = refs[count:]
    step = pl.program_id(0)
    size = blocks[0].shape[0]
    lats = own_ref.shape[1]
    for i in range(count):
        rows_ref[i * size : (i + 1) * size, :] = blocks[i][...]
    left = jnp.dot(rows_ref[...], own_ref[...], preferred_element_type=F32)
    right = jnp.dot(rows_ref[...], sib_ref[...], preferred_element_type=F32)

    @pl.when(step == 0)
    def _():
        total_ref[:, :lats] = left
        total_ref[:, lats:] = right

    @pl.when(step > 0)
    def _():
        total_ref[:, :lats] += left
        total_ref[:, lats:] += right

    @pl.when(step == pl.num_programs(0) - 1)
    def _():
        pre = total_ref[...] + params_ref[0:1, :]
        act = jnp.maximum(pre - params_ref[1:2, :], 0.0)
        codes = jnp.where(params_ref[2:3, :] > 0.0, params_ref[3:4, :], act).astype(BF16)
        for i in range(count):
            moved = jnp.dot(
                pick_ref[...], codes[i * size : (i + 1) * size], preferred_element_type=F32
            )
            codes_ref[i * size : (i + 1) * size, :] = moved.astype(BF16)


def encode(blocks, own, sib, params, pick):
    count = len(blocks)
    size, width = blocks[0].shape
    lats = own.shape[1]
    depth = 768
    return pl.pallas_call(
        functools.partial(encode_kernel, count),
        name="encode",
        out_shape=jax.ShapeDtypeStruct((count * size, 2 * lats), BF16),
        grid=(width // depth,),
        in_specs=[pl.BlockSpec((size, depth), lambda k: (0, k))] * count
        + [pl.BlockSpec((depth, lats), lambda k: (k, 0))] * 2
        + [
            pl.BlockSpec(params.shape, lambda k: (0, 0)),
            pl.BlockSpec(pick.shape, lambda k: (0, 0)),
        ],
        out_specs=pl.BlockSpec((count * size, 2 * lats), lambda k: (0, 0)),
        scratch_shapes=[
            pltpu.VMEM((count * size, depth), BF16),
            pltpu.VMEM((count * size, 2 * lats), F32),
        ],
        compiler_params=pltpu.CompilerParams(vmem_limit_bytes=24 * 1024 * 1024),
        cost_estimate=pl.CostEstimate(
            flops=4 * count * size * width * lats,
            bytes_accessed=(4 * width * lats + 2 * count * size * (width + 2 * lats)),
            transcendentals=0,
        ),
    )(*blocks, own, sib, params, pick)


def decode_kernel(group, codes_ref, own_ref, sib_ref, keep_ref, send_ref):
    size = codes_ref.shape[0]
    lats = own_ref.shape[0]
    total = jnp.dot(codes_ref[:, :lats], own_ref[...], preferred_element_type=F32)
    total += jnp.dot(codes_ref[:, lats:], sib_ref[...], preferred_element_type=F32)
    total = total.astype(BF16)
    half = group // 2
    for i in range(size // group):
        keep_ref[i * half : (i + 1) * half, :] = total[i * group : i * group + half, :]
        send_ref[i * half : (i + 1) * half, :] = total[i * group + half : (i + 1) * group, :]


def decode(codes, own, sib, part, group):
    size = codes.shape[0]
    lats, width = own.shape
    tiles = width // 2 // TILE
    out = jax.ShapeDtypeStruct((size // 2, width // 2), BF16)
    return pl.pallas_call(
        functools.partial(decode_kernel, group),
        name="decode",
        out_shape=(out, out),
        grid=(tiles,),
        in_specs=[pl.BlockSpec(codes.shape, lambda j: (0, 0))]
        + [pl.BlockSpec((lats, TILE), lambda j: (0, j + part * tiles))] * 2,
        out_specs=[pl.BlockSpec((size // 2, TILE), lambda j: (0, j))] * 2,
        compiler_params=pltpu.CompilerParams(vmem_limit_bytes=24 * 1024 * 1024),
        cost_estimate=pl.CostEstimate(
            flops=2 * size * lats * width,
            bytes_accessed=2 * (lats * width + 2 * size * lats + size * width // 2),
            transcendentals=0,
        ),
    )(codes, own, sib)


def project_kernel(
    left_ref,
    right_ref,
    gain_ref,
    query_w,
    key_w,
    value_w,
    head_gains,
    cosine_ref,
    sine_ref,
    cache_key,
    cache_value,
    query_ref,
    pairs_ref,
    normed_ref,
):
    part = left_ref.shape[1]
    hd = key_w.shape[1]
    left, right = left_ref[...].astype(F32), right_ref[...].astype(F32)
    square = jnp.sum(left * left, axis=-1, keepdims=True) + jnp.sum(
        right * right, axis=-1, keepdims=True
    )
    scale = lax.rsqrt(square / (2 * part) + EPS)
    normed_ref[:, :part] = (left * scale * gain_ref[0:1, :part]).astype(BF16)
    normed_ref[:, part:] = (right * scale * gain_ref[0:1, part:]).astype(BF16)
    normed = normed_ref[...]

    def turn(values, gain):
        values = rms_scale(values, gain)
        return (
            values * cosine_ref[...] + pltpu.roll(values, hd // 2, axis=1) * sine_ref[...]
        ).astype(BF16)

    old = cache_key.shape[0]
    pairs_ref[:old, :hd] = cache_key[...]
    pairs_ref[:old, hd:] = cache_value[...]
    key = jnp.dot(normed, key_w[...], preferred_element_type=F32)
    pairs_ref[old:, :hd] = turn(key, head_gains[1:2, :])
    value = jnp.dot(normed, value_w[...], preferred_element_type=F32)
    pairs_ref[old:, hd:] = value.astype(BF16)
    query = jnp.dot(normed, query_w[...], preferred_element_type=F32)
    for h in range(query_ref.shape[1] // hd):
        query_ref[:, h * hd : (h + 1) * hd] = turn(
            query[:, h * hd : (h + 1) * hd], head_gains[0:1, :]
        )


def project(left, right, gain, query_w, key_w, value_w, gains, cosine, sine, old_key, old_value):
    rows, hd = left.shape[0], key_w.shape[1]
    width = query_w.shape[0]
    return pl.pallas_call(
        project_kernel,
        name="project",
        out_shape=(
            jax.ShapeDtypeStruct((rows, query_w.shape[1]), BF16),
            jax.ShapeDtypeStruct((old_key.shape[0] + rows, 2 * hd), BF16),
        ),
        scratch_shapes=[pltpu.VMEM((rows, width), BF16)],
        compiler_params=pltpu.CompilerParams(vmem_limit_bytes=24 * 1024 * 1024),
        cost_estimate=pl.CostEstimate(
            flops=8 * rows * width * hd,
            bytes_accessed=8 * width * hd + 2 * rows * width,
            transcendentals=0,
        ),
    )(left, right, gain, query_w, key_w, value_w, gains, cosine, sine, old_key, old_value)


def attend_kernel(
    query_ref,
    pairs_ref,
    key_ctx,
    query_ctx,
    first_ctx,
    out_w,
    keep_z,
    send_z,
    keep_x,
    send_x,
    attended_ref,
):
    rows, hd = query_ref.shape[0], pairs_ref.shape[1] // 2
    allowed = (
        (key_ctx[...] <= query_ctx[...])
        & (key_ctx[...] > query_ctx[...] - WINDOW)
        & (key_ctx[...] >= first_ctx[...])
    )
    for h in range(query_ref.shape[1] // hd):
        scores = (
            lax.dot_general(
                query_ref[:, h * hd : (h + 1) * hd],
                pairs_ref[:, :hd],
                (((1,), (1,)), ((), ())),
                preferred_element_type=F32,
            )
            * QUERY_SCALE
        )
        scores = jnp.where(allowed, scores, -1e30)
        newest = jnp.max(scores, axis=-1, keepdims=True)
        weights = jnp.where(allowed, jnp.exp(scores - newest), 0.0)
        total = jnp.sum(weights, axis=-1, keepdims=True)
        mixed = jnp.dot(weights.astype(BF16), pairs_ref[:, hd:], preferred_element_type=F32)
        attended_ref[:, h * hd : (h + 1) * hd] = (mixed / total).astype(BF16)
    attended = attended_ref[...]
    part = out_w.shape[1] // 2
    for tile in range(part // TILE):
        here = slice(tile * TILE, (tile + 1) * TILE)
        left = jnp.dot(attended, out_w[:, here], preferred_element_type=F32).astype(BF16)
        keep_z[:, here] = left[: rows // 2]
        send_z[:, here] = left[rows // 2 :]
        there = slice(part + tile * TILE, part + (tile + 1) * TILE)
        right = jnp.dot(attended, out_w[:, there], preferred_element_type=F32).astype(BF16)
        for i in range(4):
            keep_x[i * 16 : (i + 1) * 16, here] = right[i * 32 : i * 32 + 16]
            send_x[i * 16 : (i + 1) * 16, here] = right[i * 32 + 16 : i * 32 + 32]


def attend(query, pairs, key_ctx, query_ctx, first_ctx, out_w):
    rows, width = query.shape[0], out_w.shape[1]
    out = jax.ShapeDtypeStruct((rows // 2, width // 2), BF16)
    return pl.pallas_call(
        attend_kernel,
        name="attend",
        out_shape=(out, out, out, out),
        scratch_shapes=[pltpu.VMEM((rows, query.shape[1]), BF16)],
        compiler_params=pltpu.CompilerParams(vmem_limit_bytes=24 * 1024 * 1024),
        cost_estimate=pl.CostEstimate(
            flops=2 * rows * query.shape[1] * (2 * pairs.shape[0] + width),
            bytes_accessed=2 * (query.shape[1] * width + rows * width + pairs.size),
            transcendentals=2 * rows * pairs.shape[0],
        ),
    )(query, pairs, key_ctx, query_ctx, first_ctx, out_w)


def split(value, group):
    rows, width = value.shape
    grouped = value.reshape(rows // group, group, width)
    half = group // 2
    return (
        grouped[:, :half].reshape(rows // 2, width),
        grouped[:, half:].reshape(rows // 2, width),
    )


def add(left, right):
    return (left.astype(F32) + right.astype(F32)).astype(BF16)


def reduce_step(value, dim, bits, group):
    keep, send = split(value, group)
    return add(keep, exchange(send, dim, bits))


def swap_halves(value, group):
    keep, send = split(value, group)
    rows, width = value.shape
    half = group // 2
    return jnp.concatenate(
        [send.reshape(-1, half, width), keep.reshape(-1, half, width)], axis=1
    ).reshape(rows, width)


def sum_over(value, dim, unit):
    value = add(value, swap_halves(exchange(value, dim, first_bits), 4 * unit))
    other = swap_halves(exchange(value, dim, second_bits), 2 * unit)
    return value.astype(F32) + other.astype(F32)


def gather_step(value, dim, bits, group):
    other = exchange(value, dim, bits)
    rows, width = value.shape
    return jnp.concatenate(
        [value.reshape(-1, group, width), other.reshape(-1, group, width)], axis=1
    ).reshape(2 * rows, width)


def per_device(
    resid,
    w_enc,
    b_enc,
    threshold,
    w_dec,
    b_dec,
    clamp_ids,
    clamp_index,
    clamp_table,
    pre_gain,
    w_query,
    w_key,
    w_value,
    q_gain,
    k_gain,
    cache_key,
    cache_value,
    starts,
    w_out,
    post_gain,
):
    seq_place = lax.axis_index("seq")
    lat_place = lax.axis_index("lat")
    core = seq_place % NC
    z, x = lat_place // NX, lat_place % NX
    tok_rows, width = resid.shape
    part = width // 2
    lats = w_enc.shape[1]
    head_size = q_gain.shape[0]

    order = row_order(z, x, core)
    pick = order[:, None] == jnp.arange(tok_rows, dtype=jnp.int32)[None, :]

    with jax.named_scope("gather_resid"):
        near = exchange(resid, "y", first_bits)
        again, near = lax.optimization_barrier((resid, near))
        far = exchange(again, "y", second_bits)
        opposite = exchange(near, "y", second_bits)

    with jax.named_scope("swap_weights"):
        offsets = jnp.stack([b_enc, threshold])
        sib_offsets = swap_cores(offsets)
        sib_enc = swap_cores(w_enc)
        sib_dec = swap_cores(w_dec)

    with jax.named_scope("clamp"):
        table_pick = (
            clamp_index[:, None] == jnp.arange(clamp_table.shape[0], dtype=jnp.int32)[None, :]
        )
        values = jnp.sum(jnp.where(table_pick, clamp_table[None, :], 0.0), axis=1)
        spread = jnp.arange(lats, dtype=jnp.int32)
        here = jnp.concatenate(
            [
                (seq_place * NZ * NX + lat_place) * lats + spread,
                ((seq_place ^ 1) * NZ * NX + lat_place) * lats + spread,
            ]
        )
        match = here[None, :] == clamp_ids[:, None]
        clamped = jnp.any(match, axis=0).astype(F32)
        level = jnp.sum(jnp.where(match, values[:, None], 0.0), axis=0)
        params = jnp.concatenate(
            [
                jnp.concatenate([offsets, sib_offsets], axis=1),
                clamped[None, :],
                level[None, :],
            ],
            axis=0,
        )

    def codes_of(blocks):
        return encode(blocks, w_enc, sib_enc, params, pick.astype(BF16))

    def terms(codes):
        return (
            decode(codes, w_dec, sib_dec, 0, 128),
            decode(codes, w_dec, sib_dec, 1, 32),
        )

    def first_exchange(terms_z, terms_x):
        return exchange(terms_z[1], "z", first_bits), exchange(terms_x[1], "x", first_bits)

    def plane_sums(terms_z, terms_x, received):
        sum_z = add(terms_z[0], received[0])
        sum_x = add(terms_x[0], received[1])
        sum_z = reduce_step(sum_z, "z", second_bits, 64)
        sum_x = reduce_step(sum_x, "x", second_bits, 16)
        return jnp.concatenate([sum_z, sum_x], axis=1)

    with jax.named_scope("early_tokens"):
        early_terms = terms(codes_of([resid, near]))
        early_received = first_exchange(*early_terms)
        (far, opposite), _ = lax.optimization_barrier(((far, opposite), early_terms))
    with jax.named_scope("late_tokens"):
        late_codes = codes_of([far, opposite])
        late_codes, early_received = lax.optimization_barrier((late_codes, early_received))
        early = plane_sums(*early_terms, early_received)
        late_terms = terms(late_codes)
        late = plane_sums(*late_terms, first_exchange(*late_terms))

    with jax.named_scope("sum_over_chips"):
        both = add(early, exchange(late, "y", second_bits))
        both = reduce_step(both, "y", first_bits, tok_rows // 2)
        sum_z = sum_over(both[:, :part], "x", 8)
        sum_x = sum_over(both[:, part:], "z", 8)
        rest_z = (sum_z + b_dec[:part]).astype(BF16)
        rest_x = (sum_x + b_dec[part:]).astype(BF16)
        restored = jnp.concatenate([rest_z[:8], rest_x[:8]], axis=1)

    with jax.named_scope("gather_restored"):
        rest_z = gather_step(rest_z, "z", second_bits, 32)
        rest_x = gather_step(rest_x, "x", second_bits, 8)
        rest_z = gather_step(rest_z, "z", first_bits, 64)
        rest_x = gather_step(rest_x, "x", first_bits, 16)

    with jax.named_scope("projections"):
        query_ctx = PREFIX + seq_place * tok_rows + order
        freq = THETA ** (-(jnp.arange(head_size // 2, dtype=F32) * 2.0 / head_size))
        angle = query_ctx.astype(F32)[:, None] * freq[None, :]
        cosine, sine = jnp.cos(angle), jnp.sin(angle)
        cosine = jnp.concatenate([cosine, cosine], axis=1)
        sine = jnp.concatenate([-sine, sine], axis=1)
        query, own_pairs = project(
            rest_z,
            rest_x,
            pre_gain[None, :],
            w_query,
            w_key,
            w_value,
            jnp.stack([q_gain, k_gain]),
            cosine,
            sine,
            cache_key,
            cache_value,
        )

    with jax.named_scope("attention"):
        pre_rows = cache_key.shape[0]
        pairs = lax.all_gather(own_pairs, "seq", axis=0, tiled=True)
        orders = jnp.stack([row_order(z, x, jnp.int32(i)) for i in range(NC)])
        shard = jnp.arange(NY * NC, dtype=jnp.int32)
        new_ctx = PREFIX + shard[:, None] * tok_rows + jnp.tile(orders, (NY, 1))
        old_ctx = shard[:, None] * pre_rows + jnp.arange(pre_rows, dtype=jnp.int32)[None, :]
        key_ctx = jnp.concatenate([old_ctx, new_ctx], axis=1).reshape(1, -1)
        first_ctx = jnp.sum(jnp.where(pick, starts[None, :], 0), axis=1)
        keep_z, send_z, keep_x, send_x = attend(
            query, pairs, key_ctx, query_ctx[:, None], first_ctx[:, None], w_out
        )

    with jax.named_scope("sum_over_heads"):
        out_z = add(keep_z, exchange(send_z, "z", first_bits))
        out_x = add(keep_x, exchange(send_x, "x", first_bits))
        out_z = reduce_step(out_z, "z", second_bits, 64)
        out_x = reduce_step(out_x, "x", second_bits, 16)
        out_z = reduce_step(out_z, "x", first_bits, 32)
        out_x = reduce_step(out_x, "z", first_bits, 32)
        keep_z, send_z = split(out_z, 16)
        keep_x, send_x = split(out_x, 16)
        mine_z = keep_z.astype(F32) + exchange(send_z, "x", second_bits).astype(F32)
        mine_x = keep_x.astype(F32) + exchange(send_x, "z", second_bits).astype(F32)
        mine = jnp.concatenate([mine_z, mine_x], axis=1)
        return (restored.astype(F32) + rms_scale(mine, post_gain)).astype(BF16)


def solution(mesh):
    in_specs = (
        P("seq", None),
        P(None, ("seq", "lat")),
        P(("seq", "lat")),
        P(("seq", "lat")),
        P(("seq", "lat"), None),
        P(),
        P(),
        P(),
        P(),
        P(),
        P(None, "lat"),
        P(None, "lat"),
        P(None, "lat"),
        P(),
        P(),
        P("seq", "lat"),
        P("seq", "lat"),
        P("seq"),
        P("lat", None),
        P(),
    )
    out_specs = P(("seq", "lat"), None)
    return jax.shard_map(
        per_device, mesh=mesh, in_specs=in_specs, out_specs=out_specs, check_vma=False
    )
```

```python
import functools

import jax
import jax.numpy as jnp
from jax import lax
from jax.experimental import pallas as pl
from jax.experimental.pallas import tpu as pltpu
from jax.sharding import PartitionSpec as P

WINDOW = 1024
PREFIX = 512
EPS = 1e-06
THETA = 10000.0
QUERY_SCALE = 168.0 ** (-0.5)

NY, NC, NZ, NX = 4, 2, 4, 4
AXES = ("seq", "lat")
TILE = 896
F32, BF16 = jnp.float32, jnp.bfloat16


def first_bits(core):
    return 1 if core == 0 else 3


def second_bits(core):
    return 3 if core == 0 else 1


def exchange(value, dim, bits):
    pairs = []
    for y in range(NY):
        for c in range(NC):
            for z in range(NZ):
                for x in range(NX):
                    to = {"y": y, "c": c, "z": z, "x": x}
                    to[dim] ^= bits(c)
                    pairs.append(
                        (
                            (y * NC + c) * NZ * NX + z * NX + x,
                            (to["y"] * NC + to["c"]) * NZ * NX + to["z"] * NX + to["x"],
                        )
                    )
    return lax.ppermute(value, AXES, pairs)


def swap_cores(value):
    return exchange(value, "c", lambda core: 1)


def relative(place, core):
    step = jnp.arange(4, dtype=jnp.int32)
    order0 = jnp.where(step == 1, 3, jnp.where(step == 2, 1, jnp.where(step == 3, 2, 0)))
    order1 = jnp.where(step == 1, 1, jnp.where(step == 2, 3, jnp.where(step == 3, 2, 0)))
    return place ^ jnp.where(core == 0, order0, order1)


def row_order(z, x, core):
    zs, xs = relative(z, core), relative(x, core)
    row = (zs[:, None] * NX + xs[None, :])[:, :, None] * 8 + jnp.arange(8, dtype=jnp.int32)
    return row.reshape(-1)


def rms_scale(values, gain):
    return values * lax.rsqrt(jnp.mean(values * values, axis=-1, keepdims=True) + EPS) * gain


def encode_kernel(count, *refs):
    blocks = refs[:count]
    own_ref, sib_ref, params_ref, pick_ref, codes_ref, rows_ref = refs[count:]
    size = blocks[0].shape[0]
    lats = own_ref.shape[1]
    for i in range(count):
        rows_ref[i * size : (i + 1) * size, :] = blocks[i][...]
    for side, weights_ref in enumerate((own_ref, sib_ref)):
        for tile in range(lats // 256):
            here = slice(tile * 256, (tile + 1) * 256)
            there = slice(side * lats + tile * 256, side * lats + (tile + 1) * 256)
            pre = jnp.dot(rows_ref[...], weights_ref[:, here], preferred_element_type=F32)
            act = jnp.maximum(pre + params_ref[0:1, there] - params_ref[1:2, there], 0.0)
            codes = jnp.where(params_ref[2:3, there] > 0.0, params_ref[3:4, there], act)
            codes = codes.astype(BF16)
            for i in range(count):
                moved = jnp.dot(
                    pick_ref[...], codes[i * size : (i + 1) * size], preferred_element_type=F32
                )
                codes_ref[i * size : (i + 1) * size, there] = moved.astype(BF16)


def encode(blocks, own, sib, params, pick):
    count = len(blocks)
    size, width = blocks[0].shape
    lats = own.shape[1]
    return pl.pallas_call(
        functools.partial(encode_kernel, count),
        name="encode",
        out_shape=jax.ShapeDtypeStruct((count * size, 2 * lats), BF16),
        scratch_shapes=[pltpu.VMEM((count * size, width), BF16)],
        compiler_params=pltpu.CompilerParams(vmem_limit_bytes=12 * 1024 * 1024),
        cost_estimate=pl.CostEstimate(
            flops=4 * count * size * width * lats,
            bytes_accessed=4 * width * lats + 2 * count * size * (width + 2 * lats),
            transcendentals=0,
        ),
    )(*blocks, own, sib, params, pick)


def decode_kernel(part, group, codes_ref, own_ref, sib_ref, keep_ref, send_ref):
    size = codes_ref.shape[0]
    lats, width = own_ref.shape
    half = group // 2
    for tile in range(width // 2 // TILE):
        here = slice(tile * TILE, (tile + 1) * TILE)
        there = slice(part * (width // 2) + tile * TILE, part * (width // 2) + (tile + 1) * TILE)
        total = jnp.dot(codes_ref[:, :lats], own_ref[:, there], preferred_element_type=F32)
        total += jnp.dot(codes_ref[:, lats:], sib_ref[:, there], preferred_element_type=F32)
        total = total.astype(BF16)
        for i in range(size // group):
            keep_ref[i * half : (i + 1) * half, here] = total[i * group : i * group + half, :]
            send_ref[i * half : (i + 1) * half, here] = total[i * group + half : (i + 1) * group, :]


def decode(codes, own, sib, part, group):
    size = codes.shape[0]
    lats, width = own.shape
    out = jax.ShapeDtypeStruct((size // 2, width // 2), BF16)
    return pl.pallas_call(
        functools.partial(decode_kernel, part, group),
        name="decode",
        out_shape=(out, out),
        compiler_params=pltpu.CompilerParams(vmem_limit_bytes=12 * 1024 * 1024),
        cost_estimate=pl.CostEstimate(
            flops=2 * size * lats * width,
            bytes_accessed=2 * (lats * width + 2 * size * lats + size * width // 2),
            transcendentals=0,
        ),
    )(codes, own, sib)


def project_kernel(
    left_ref,
    right_ref,
    gain_ref,
    query_w,
    key_w,
    value_w,
    head_gains,
    cosine_ref,
    sine_ref,
    cache_key,
    cache_value,
    query_ref,
    pairs_ref,
    normed_ref,
):
    part = left_ref.shape[1]
    hd = key_w.shape[1]
    left, right = left_ref[...].astype(F32), right_ref[...].astype(F32)
    square = jnp.sum(left * left, axis=-1, keepdims=True) + jnp.sum(
        right * right, axis=-1, keepdims=True
    )
    scale = lax.rsqrt(square / (2 * part) + EPS)
    normed_ref[:, :part] = (left * scale * gain_ref[0:1, :part]).astype(BF16)
    normed_ref[:, part:] = (right * scale * gain_ref[0:1, part:]).astype(BF16)
    normed = normed_ref[...]

    def turn(values, gain):
        values = rms_scale(values, gain)
        return (
            values * cosine_ref[...] + pltpu.roll(values, hd // 2, axis=1) * sine_ref[...]
        ).astype(BF16)

    old = cache_key.shape[0]
    pairs_ref[:old, :hd] = cache_key[...]
    pairs_ref[:old, hd:] = cache_value[...]
    key = jnp.dot(normed, key_w[...], preferred_element_type=F32)
    pairs_ref[old:, :hd] = turn(key, head_gains[1:2, :])
    value = jnp.dot(normed, value_w[...], preferred_element_type=F32)
    pairs_ref[old:, hd:] = value.astype(BF16)
    query = jnp.dot(normed, query_w[...], preferred_element_type=F32)
    for h in range(query_ref.shape[1] // hd):
        query_ref[:, h * hd : (h + 1) * hd] = turn(
            query[:, h * hd : (h + 1) * hd], head_gains[0:1, :]
        )


def project(left, right, gain, query_w, key_w, value_w, gains, cosine, sine, old_key, old_value):
    rows, hd = left.shape[0], key_w.shape[1]
    width = query_w.shape[0]
    return pl.pallas_call(
        project_kernel,
        name="project",
        out_shape=(
            jax.ShapeDtypeStruct((rows, query_w.shape[1]), BF16),
            jax.ShapeDtypeStruct((old_key.shape[0] + rows, 2 * hd), BF16),
        ),
        scratch_shapes=[pltpu.VMEM((rows, width), BF16)],
        compiler_params=pltpu.CompilerParams(vmem_limit_bytes=12 * 1024 * 1024),
        cost_estimate=pl.CostEstimate(
            flops=8 * rows * width * hd,
            bytes_accessed=8 * width * hd + 2 * rows * width,
            transcendentals=0,
        ),
    )(left, right, gain, query_w, key_w, value_w, gains, cosine, sine, old_key, old_value)


def attend_kernel(
    query_ref,
    pairs_ref,
    key_ctx,
    query_ctx,
    first_ctx,
    out_w,
    keep_z,
    send_z,
    keep_x,
    send_x,
    attended_ref,
):
    rows, hd = query_ref.shape[0], pairs_ref.shape[1] // 2
    allowed = (
        (key_ctx[...] <= query_ctx[...])
        & (key_ctx[...] > query_ctx[...] - WINDOW)
        & (key_ctx[...] >= first_ctx[...])
    )
    for h in range(query_ref.shape[1] // hd):
        scores = (
            lax.dot_general(
                query_ref[:, h * hd : (h + 1) * hd],
                pairs_ref[:, :hd],
                (((1,), (1,)), ((), ())),
                preferred_element_type=F32,
            )
            * QUERY_SCALE
        )
        scores = jnp.where(allowed, scores, -1e30)
        newest = jnp.max(scores, axis=-1, keepdims=True)
        weights = jnp.where(allowed, jnp.exp(scores - newest), 0.0)
        total = jnp.sum(weights, axis=-1, keepdims=True)
        mixed = jnp.dot(weights.astype(BF16), pairs_ref[:, hd:], preferred_element_type=F32)
        attended_ref[:, h * hd : (h + 1) * hd] = (mixed / total).astype(BF16)
    attended = attended_ref[...]
    part = out_w.shape[1] // 2
    for tile in range(part // TILE):
        here = slice(tile * TILE, (tile + 1) * TILE)
        left = jnp.dot(attended, out_w[:, here], preferred_element_type=F32).astype(BF16)
        keep_z[:, here] = left[: rows // 2]
        send_z[:, here] = left[rows // 2 :]
        there = slice(part + tile * TILE, part + (tile + 1) * TILE)
        right = jnp.dot(attended, out_w[:, there], preferred_element_type=F32).astype(BF16)
        for i in range(4):
            keep_x[i * 16 : (i + 1) * 16, here] = right[i * 32 : i * 32 + 16]
            send_x[i * 16 : (i + 1) * 16, here] = right[i * 32 + 16 : i * 32 + 32]


def attend(query, pairs, key_ctx, query_ctx, first_ctx, out_w):
    rows, width = query.shape[0], out_w.shape[1]
    out = jax.ShapeDtypeStruct((rows // 2, width // 2), BF16)
    return pl.pallas_call(
        attend_kernel,
        name="attend",
        out_shape=(out, out, out, out),
        scratch_shapes=[pltpu.VMEM((rows, query.shape[1]), BF16)],
        compiler_params=pltpu.CompilerParams(vmem_limit_bytes=12 * 1024 * 1024),
        cost_estimate=pl.CostEstimate(
            flops=2 * rows * query.shape[1] * (2 * pairs.shape[0] + width),
            bytes_accessed=2 * (query.shape[1] * width + rows * width + pairs.size),
            transcendentals=2 * rows * pairs.shape[0],
        ),
    )(query, pairs, key_ctx, query_ctx, first_ctx, out_w)


def split(value, group):
    rows, width = value.shape
    grouped = value.reshape(rows // group, group, width)
    half = group // 2
    return (
        grouped[:, :half].reshape(rows // 2, width),
        grouped[:, half:].reshape(rows // 2, width),
    )


def add(left, right):
    return (left.astype(F32) + right.astype(F32)).astype(BF16)


def reduce_step(value, dim, bits, group):
    keep, send = split(value, group)
    return add(keep, exchange(send, dim, bits))


def swap_halves(value, group):
    keep, send = split(value, group)
    rows, width = value.shape
    half = group // 2
    return jnp.concatenate(
        [send.reshape(-1, half, width), keep.reshape(-1, half, width)], axis=1
    ).reshape(rows, width)


def gather_step(value, dim, bits, group):
    other = exchange(value, dim, bits)
    rows, width = value.shape
    return jnp.concatenate(
        [value.reshape(-1, group, width), other.reshape(-1, group, width)], axis=1
    ).reshape(2 * rows, width)


def per_device(
    resid,
    w_enc,
    b_enc,
    threshold,
    w_dec,
    b_dec,
    clamp_ids,
    clamp_index,
    clamp_table,
    pre_gain,
    w_query,
    w_key,
    w_value,
    q_gain,
    k_gain,
    cache_key,
    cache_value,
    starts,
    w_out,
    post_gain,
):
    seq_place = lax.axis_index("seq")
    lat_place = lax.axis_index("lat")
    core = seq_place % NC
    z, x = lat_place // NX, lat_place % NX
    tok_rows, width = resid.shape
    part = width // 2
    lats = w_enc.shape[1]
    head_size = q_gain.shape[0]

    order = row_order(z, x, core)
    pick = order[:, None] == jnp.arange(tok_rows, dtype=jnp.int32)[None, :]

    with jax.named_scope("gather_resid"):
        near = exchange(resid, "y", first_bits)
        again, near = lax.optimization_barrier((resid, near))
        far = exchange(again, "y", second_bits)
        opposite = exchange(near, "y", second_bits)

    with jax.named_scope("swap_weights"):
        offsets = jnp.stack([b_enc, threshold])
        sib_offsets = swap_cores(offsets)
        sib_enc = swap_cores(w_enc)
        sib_dec = swap_cores(w_dec)

    with jax.named_scope("clamp"):
        table_pick = (
            clamp_index[:, None] == jnp.arange(clamp_table.shape[0], dtype=jnp.int32)[None, :]
        )
        values = jnp.sum(jnp.where(table_pick, clamp_table[None, :], 0.0), axis=1)
        spread = jnp.arange(lats, dtype=jnp.int32)
        here = jnp.concatenate(
            [
                (seq_place * NZ * NX + lat_place) * lats + spread,
                ((seq_place ^ 1) * NZ * NX + lat_place) * lats + spread,
            ]
        )
        match = here[None, :] == clamp_ids[:, None]
        clamped = jnp.any(match, axis=0).astype(F32)
        level = jnp.sum(jnp.where(match, values[:, None], 0.0), axis=0)
        params = jnp.concatenate(
            [
                jnp.concatenate([offsets, sib_offsets], axis=1),
                clamped[None, :],
                level[None, :],
            ],
            axis=0,
        )

    def codes_of(blocks):
        return encode(blocks, w_enc, sib_enc, params, pick.astype(BF16))

    def terms(codes):
        return (
            decode(codes, w_dec, sib_dec, 0, 128),
            decode(codes, w_dec, sib_dec, 1, 32),
        )

    def first_exchange(terms_z, terms_x):
        return exchange(terms_z[1], "z", first_bits), exchange(terms_x[1], "x", first_bits)

    def plane_sums(terms_z, terms_x, received):
        sum_z = add(terms_z[0], received[0])
        sum_x = add(terms_x[0], received[1])
        sum_z = reduce_step(sum_z, "x", first_bits, 32)
        sum_x = reduce_step(sum_x, "z", first_bits, 64)
        return jnp.concatenate([sum_z, sum_x], axis=1)

    with jax.named_scope("early_tokens"):
        early_terms = terms(codes_of([resid, near]))
        early_received = first_exchange(*early_terms)
        (far, opposite), _ = lax.optimization_barrier(((far, opposite), early_terms))
    with jax.named_scope("late_tokens"):
        late_codes = codes_of([far, opposite])
        late_codes, early_received = lax.optimization_barrier((late_codes, early_received))
        early = plane_sums(*early_terms, early_received)
        late_terms = terms(late_codes)
        late = plane_sums(*late_terms, first_exchange(*late_terms))

    with jax.named_scope("sum_over_chips"):
        quarter = tok_rows // 4
        near_sums = exchange(early[quarter:], "y", first_bits)
        far_sums = exchange(late[:quarter], "y", second_bits)
        opposite_sums = exchange(late[quarter:], "y", lambda core: 2)
        total = early[:quarter].astype(F32) + near_sums.astype(F32)
        total = (total + far_sums.astype(F32) + opposite_sums.astype(F32)).astype(BF16)
        total = add(total, swap_halves(exchange(total, "z", second_bits), 32))
        other = swap_halves(exchange(total, "x", second_bits), 16)
        total = total.astype(F32) + other.astype(F32)
        rest = (total + b_dec).astype(BF16)
        restored = rest[:8]

    with jax.named_scope("gather_restored"):
        rest_z = gather_step(rest[:, :part], "x", first_bits, 16)
        rest_x = gather_step(rest[:, part:], "z", first_bits, 32)
        rest_z = gather_step(rest_z, "z", first_bits, 64)
        rest_x = gather_step(rest_x, "x", first_bits, 16)

    with jax.named_scope("projections"):
        query_ctx = PREFIX + seq_place * tok_rows + order
        freq = THETA ** (-(jnp.arange(head_size // 2, dtype=F32) * 2.0 / head_size))
        angle = query_ctx.astype(F32)[:, None] * freq[None, :]
        cosine, sine = jnp.cos(angle), jnp.sin(angle)
        cosine = jnp.concatenate([cosine, cosine], axis=1)
        sine = jnp.concatenate([-sine, sine], axis=1)
        query, own_pairs = project(
            rest_z,
            rest_x,
            pre_gain[None, :],
            w_query,
            w_key,
            w_value,
            jnp.stack([q_gain, k_gain]),
            cosine,
            sine,
            cache_key,
            cache_value,
        )

    with jax.named_scope("attention"):
        pre_rows = cache_key.shape[0]
        pairs = lax.all_gather(own_pairs, "seq", axis=0, tiled=True)
        orders = jnp.stack([row_order(z, x, jnp.int32(i)) for i in range(NC)])
        shard = jnp.arange(NY * NC, dtype=jnp.int32)
        new_ctx = PREFIX + shard[:, None] * tok_rows + jnp.tile(orders, (NY, 1))
        old_ctx = shard[:, None] * pre_rows + jnp.arange(pre_rows, dtype=jnp.int32)[None, :]
        key_ctx = jnp.concatenate([old_ctx, new_ctx], axis=1).reshape(1, -1)
        first_ctx = jnp.sum(jnp.where(pick, starts[None, :], 0), axis=1)
        keep_z, send_z, keep_x, send_x = attend(
            query, pairs, key_ctx, query_ctx[:, None], first_ctx[:, None], w_out
        )

    with jax.named_scope("sum_over_heads"):
        out_z = add(keep_z, exchange(send_z, "z", first_bits))
        out_x = add(keep_x, exchange(send_x, "x", first_bits))
        out_z = reduce_step(out_z, "x", first_bits, 32)
        out_x = reduce_step(out_x, "z", first_bits, 64)
        both = jnp.concatenate([out_z, out_x], axis=1)
        both = reduce_step(both, "z", second_bits, 32)
        keep, send = split(both, 16)
        mine = keep.astype(F32) + exchange(send, "x", second_bits).astype(F32)
        return (restored.astype(F32) + rms_scale(mine, post_gain)).astype(BF16)


def solution(mesh):
    in_specs = (
        P("seq", None),
        P(None, ("seq", "lat")),
        P(("seq", "lat")),
        P(("seq", "lat")),
        P(("seq", "lat"), None),
        P(),
        P(),
        P(),
        P(),
        P(),
        P(None, "lat"),
        P(None, "lat"),
        P(None, "lat"),
        P(),
        P(),
        P("seq", "lat"),
        P("seq", "lat"),
        P("seq"),
        P("lat", None),
        P(),
    )
    out_specs = P(("seq", "lat"), None)
    return jax.shard_map(
        per_device, mesh=mesh, in_specs=in_specs, out_specs=out_specs, check_vma=False
    )
```

```python
import functools

import jax
import jax.numpy as jnp
from jax import lax
from jax.experimental import pallas as pl
from jax.experimental.pallas import tpu as pltpu
from jax.sharding import PartitionSpec as P

WINDOW = 1024
PREFIX = 512
EPS = 1e-06
THETA = 10000.0
QUERY_SCALE = 168.0 ** (-0.5)

NY, NC, NZ, NX = 4, 2, 4, 4
AXES = ("seq", "lat")
TILE = 896
F32, BF16 = jnp.float32, jnp.bfloat16


def first_bits(core):
    return 1 if core == 0 else 3


def second_bits(core):
    return 3 if core == 0 else 1


def exchange(value, dim, bits):
    pairs = []
    for y in range(NY):
        for c in range(NC):
            for z in range(NZ):
                for x in range(NX):
                    to = {"y": y, "c": c, "z": z, "x": x}
                    to[dim] ^= bits(c)
                    pairs.append(
                        (
                            (y * NC + c) * NZ * NX + z * NX + x,
                            (to["y"] * NC + to["c"]) * NZ * NX + to["z"] * NX + to["x"],
                        )
                    )
    return lax.ppermute(value, AXES, pairs)


def swap_cores(value):
    return exchange(value, "c", lambda core: 1)


def relative(place, core):
    step = jnp.arange(4, dtype=jnp.int32)
    order0 = jnp.where(step == 1, 3, jnp.where(step == 2, 1, jnp.where(step == 3, 2, 0)))
    order1 = jnp.where(step == 1, 1, jnp.where(step == 2, 3, jnp.where(step == 3, 2, 0)))
    return place ^ jnp.where(core == 0, order0, order1)


def row_order(z, x, core):
    zs, xs = relative(z, core), relative(x, core)
    row = (zs[:, None] * NX + xs[None, :])[:, :, None] * 8 + jnp.arange(8, dtype=jnp.int32)
    return row.reshape(-1)


def rms_scale(values, gain):
    return values * lax.rsqrt(jnp.mean(values * values, axis=-1, keepdims=True) + EPS) * gain


def stage_kernel(source_ref, target_ref, sem):
    copy = pltpu.make_async_copy(source_ref, target_ref, sem)
    copy.start()
    copy.wait()


def stage(value):
    return pl.pallas_call(
        stage_kernel,
        name="stage",
        out_shape=jax.ShapeDtypeStruct(value.shape, value.dtype),
        in_specs=[pl.BlockSpec(memory_space=pl.ANY)],
        out_specs=pl.BlockSpec(memory_space=pltpu.VMEM),
        scratch_shapes=[pltpu.SemaphoreType.DMA],
        compiler_params=pltpu.CompilerParams(vmem_limit_bytes=6 * 1024 * 1024),
        cost_estimate=pl.CostEstimate(flops=0, bytes_accessed=2 * value.size, transcendentals=0),
    )(value)


def encode_kernel(count, *refs):
    blocks = refs[:count]
    own_ref, sib_ref, params_ref, pick_ref, codes_ref, rows_ref = refs[count:]
    size = blocks[0].shape[0]
    lats = own_ref.shape[1]
    for i in range(count):
        rows_ref[i * size : (i + 1) * size, :] = blocks[i][...]
    for side, weights_ref in enumerate((own_ref, sib_ref)):
        there = slice(side * lats, (side + 1) * lats)
        pre = jnp.dot(rows_ref[...], weights_ref[...], preferred_element_type=F32)
        act = jnp.maximum(pre + params_ref[0:1, there] - params_ref[1:2, there], 0.0)
        codes = jnp.where(params_ref[2:3, there] > 0.0, params_ref[3:4, there], act)
        codes = codes.astype(BF16)
        for i in range(count):
            moved = jnp.dot(
                pick_ref[...], codes[i * size : (i + 1) * size], preferred_element_type=F32
            )
            codes_ref[i * size : (i + 1) * size, there] = moved.astype(BF16)


def encode(blocks, own, sib, params, pick):
    count = len(blocks)
    size, width = blocks[0].shape
    lats = own.shape[1]
    return pl.pallas_call(
        functools.partial(encode_kernel, count),
        name="encode",
        out_shape=jax.ShapeDtypeStruct((count * size, 2 * lats), BF16),
        scratch_shapes=[pltpu.VMEM((count * size, width), BF16)],
        compiler_params=pltpu.CompilerParams(vmem_limit_bytes=12 * 1024 * 1024),
        cost_estimate=pl.CostEstimate(
            flops=4 * count * size * width * lats,
            bytes_accessed=4 * width * lats + 2 * count * size * (width + 2 * lats),
            transcendentals=0,
        ),
    )(*blocks, own, sib, params, pick)


def decode_kernel(part, group, codes_ref, own_ref, sib_ref, keep_ref, send_ref):
    size = codes_ref.shape[0]
    lats, width = own_ref.shape
    half = group // 2
    for tile in range(width // 2 // TILE):
        here = slice(tile * TILE, (tile + 1) * TILE)
        there = slice(part * (width // 2) + tile * TILE, part * (width // 2) + (tile + 1) * TILE)
        total = jnp.dot(codes_ref[:, :lats], own_ref[:, there], preferred_element_type=F32)
        total += jnp.dot(codes_ref[:, lats:], sib_ref[:, there], preferred_element_type=F32)
        total = total.astype(BF16)
        for i in range(size // group):
            keep_ref[i * half : (i + 1) * half, here] = total[i * group : i * group + half, :]
            send_ref[i * half : (i + 1) * half, here] = total[i * group + half : (i + 1) * group, :]


def decode(codes, own, sib, part, group):
    size = codes.shape[0]
    lats, width = own.shape
    out = jax.ShapeDtypeStruct((size // 2, width // 2), BF16)
    return pl.pallas_call(
        functools.partial(decode_kernel, part, group),
        name="decode",
        out_shape=(out, out),
        compiler_params=pltpu.CompilerParams(vmem_limit_bytes=12 * 1024 * 1024),
        cost_estimate=pl.CostEstimate(
            flops=2 * size * lats * width,
            bytes_accessed=2 * (lats * width + 2 * size * lats + size * width // 2),
            transcendentals=0,
        ),
    )(codes, own, sib)


def project_kernel(
    left_ref,
    right_ref,
    gain_ref,
    query_w,
    key_w,
    value_w,
    head_gains,
    cosine_ref,
    sine_ref,
    cache_key,
    cache_value,
    query_ref,
    pairs_ref,
    normed_ref,
):
    part = left_ref.shape[1]
    hd = key_w.shape[1]
    left, right = left_ref[...].astype(F32), right_ref[...].astype(F32)
    square = jnp.sum(left * left, axis=-1, keepdims=True) + jnp.sum(
        right * right, axis=-1, keepdims=True
    )
    scale = lax.rsqrt(square / (2 * part) + EPS)
    normed_ref[:, :part] = (left * scale * gain_ref[0:1, :part]).astype(BF16)
    normed_ref[:, part:] = (right * scale * gain_ref[0:1, part:]).astype(BF16)
    normed = normed_ref[...]

    def turn(values, gain):
        values = rms_scale(values, gain)
        return (
            values * cosine_ref[...] + pltpu.roll(values, hd // 2, axis=1) * sine_ref[...]
        ).astype(BF16)

    old = cache_key.shape[0]
    pairs_ref[:old, :hd] = cache_key[...]
    pairs_ref[:old, hd:] = cache_value[...]
    key = jnp.dot(normed, key_w[...], preferred_element_type=F32)
    pairs_ref[old:, :hd] = turn(key, head_gains[1:2, :])
    value = jnp.dot(normed, value_w[...], preferred_element_type=F32)
    pairs_ref[old:, hd:] = value.astype(BF16)
    query = jnp.dot(normed, query_w[...], preferred_element_type=F32)
    for h in range(query_ref.shape[1] // hd):
        query_ref[:, h * hd : (h + 1) * hd] = turn(
            query[:, h * hd : (h + 1) * hd], head_gains[0:1, :]
        )


def project(left, right, gain, query_w, key_w, value_w, gains, cosine, sine, old_key, old_value):
    rows, hd = left.shape[0], key_w.shape[1]
    width = query_w.shape[0]
    return pl.pallas_call(
        project_kernel,
        name="project",
        out_shape=(
            jax.ShapeDtypeStruct((rows, query_w.shape[1]), BF16),
            jax.ShapeDtypeStruct((old_key.shape[0] + rows, 2 * hd), BF16),
        ),
        scratch_shapes=[pltpu.VMEM((rows, width), BF16)],
        compiler_params=pltpu.CompilerParams(vmem_limit_bytes=12 * 1024 * 1024),
        cost_estimate=pl.CostEstimate(
            flops=8 * rows * width * hd,
            bytes_accessed=8 * width * hd + 2 * rows * width,
            transcendentals=0,
        ),
    )(left, right, gain, query_w, key_w, value_w, gains, cosine, sine, old_key, old_value)


def attend_kernel(
    query_ref,
    pairs_ref,
    key_ctx,
    query_ctx,
    first_ctx,
    out_w,
    keep_z,
    send_z,
    keep_x,
    send_x,
    attended_ref,
):
    rows, hd = query_ref.shape[0], pairs_ref.shape[1] // 2
    allowed = (
        (key_ctx[...] <= query_ctx[...])
        & (key_ctx[...] > query_ctx[...] - WINDOW)
        & (key_ctx[...] >= first_ctx[...])
    )
    for h in range(query_ref.shape[1] // hd):
        scores = (
            lax.dot_general(
                query_ref[:, h * hd : (h + 1) * hd],
                pairs_ref[:, :hd],
                (((1,), (1,)), ((), ())),
                preferred_element_type=F32,
            )
            * QUERY_SCALE
        )
        scores = jnp.where(allowed, scores, -1e30)
        newest = jnp.max(scores, axis=-1, keepdims=True)
        weights = jnp.where(allowed, jnp.exp(scores - newest), 0.0)
        total = jnp.sum(weights, axis=-1, keepdims=True)
        mixed = jnp.dot(weights.astype(BF16), pairs_ref[:, hd:], preferred_element_type=F32)
        attended_ref[:, h * hd : (h + 1) * hd] = (mixed / total).astype(BF16)
    attended = attended_ref[...]
    part = out_w.shape[1] // 2
    for tile in range(part // TILE):
        here = slice(tile * TILE, (tile + 1) * TILE)
        left = jnp.dot(attended, out_w[:, here], preferred_element_type=F32).astype(BF16)
        keep_z[:, here] = left[: rows // 2]
        send_z[:, here] = left[rows // 2 :]
        there = slice(part + tile * TILE, part + (tile + 1) * TILE)
        right = jnp.dot(attended, out_w[:, there], preferred_element_type=F32).astype(BF16)
        for i in range(4):
            keep_x[i * 16 : (i + 1) * 16, here] = right[i * 32 : i * 32 + 16]
            send_x[i * 16 : (i + 1) * 16, here] = right[i * 32 + 16 : i * 32 + 32]


def attend(query, pairs, key_ctx, query_ctx, first_ctx, out_w):
    rows, width = query.shape[0], out_w.shape[1]
    out = jax.ShapeDtypeStruct((rows // 2, width // 2), BF16)
    return pl.pallas_call(
        attend_kernel,
        name="attend",
        out_shape=(out, out, out, out),
        scratch_shapes=[pltpu.VMEM((rows, query.shape[1]), BF16)],
        compiler_params=pltpu.CompilerParams(vmem_limit_bytes=12 * 1024 * 1024),
        cost_estimate=pl.CostEstimate(
            flops=2 * rows * query.shape[1] * (2 * pairs.shape[0] + width),
            bytes_accessed=2 * (query.shape[1] * width + rows * width + pairs.size),
            transcendentals=2 * rows * pairs.shape[0],
        ),
    )(query, pairs, key_ctx, query_ctx, first_ctx, out_w)


def split(value, group):
    rows, width = value.shape
    grouped = value.reshape(rows // group, group, width)
    half = group // 2
    return (
        grouped[:, :half].reshape(rows // 2, width),
        grouped[:, half:].reshape(rows // 2, width),
    )


def add(left, right):
    return (left.astype(F32) + right.astype(F32)).astype(BF16)


def reduce_step(value, dim, bits, group):
    keep, send = split(value, group)
    return add(keep, exchange(send, dim, bits))


def swap_halves(value, group):
    keep, send = split(value, group)
    rows, width = value.shape
    half = group // 2
    return jnp.concatenate(
        [send.reshape(-1, half, width), keep.reshape(-1, half, width)], axis=1
    ).reshape(rows, width)


def gather_step(value, dim, bits, group):
    other = exchange(value, dim, bits)
    rows, width = value.shape
    return jnp.concatenate(
        [value.reshape(-1, group, width), other.reshape(-1, group, width)], axis=1
    ).reshape(2 * rows, width)


def per_device(
    resid,
    w_enc,
    b_enc,
    threshold,
    w_dec,
    b_dec,
    clamp_ids,
    clamp_index,
    clamp_table,
    pre_gain,
    w_query,
    w_key,
    w_value,
    q_gain,
    k_gain,
    cache_key,
    cache_value,
    starts,
    w_out,
    post_gain,
):
    seq_place = lax.axis_index("seq")
    lat_place = lax.axis_index("lat")
    core = seq_place % NC
    z, x = lat_place // NX, lat_place % NX
    tok_rows, width = resid.shape
    part = width // 2
    lats = w_enc.shape[1]
    head_size = q_gain.shape[0]

    order = row_order(z, x, core)
    pick = order[:, None] == jnp.arange(tok_rows, dtype=jnp.int32)[None, :]

    with jax.named_scope("gather_resid"):
        near = exchange(resid, "y", first_bits)
        again, near = lax.optimization_barrier((resid, near))
        far = exchange(again, "y", second_bits)
        opposite = exchange(near, "y", second_bits)

    with jax.named_scope("swap_weights"):
        offsets = jnp.stack([b_enc, threshold])
        sib_offsets = swap_cores(offsets)
        sib_enc = stage(swap_cores(w_enc))
        sib_dec = stage(swap_cores(w_dec))

    with jax.named_scope("clamp"):
        table_pick = (
            clamp_index[:, None] == jnp.arange(clamp_table.shape[0], dtype=jnp.int32)[None, :]
        )
        values = jnp.sum(jnp.where(table_pick, clamp_table[None, :], 0.0), axis=1)
        spread = jnp.arange(lats, dtype=jnp.int32)
        here = jnp.concatenate(
            [
                (seq_place * NZ * NX + lat_place) * lats + spread,
                ((seq_place ^ 1) * NZ * NX + lat_place) * lats + spread,
            ]
        )
        match = here[None, :] == clamp_ids[:, None]
        clamped = jnp.any(match, axis=0).astype(F32)
        level = jnp.sum(jnp.where(match, values[:, None], 0.0), axis=0)
        params = jnp.concatenate(
            [
                jnp.concatenate([offsets, sib_offsets], axis=1),
                clamped[None, :],
                level[None, :],
            ],
            axis=0,
        )

    def codes_of(blocks):
        return encode(blocks, w_enc, sib_enc, params, pick.astype(BF16))

    def terms(codes):
        return (
            decode(codes, w_dec, sib_dec, 0, 128),
            decode(codes, w_dec, sib_dec, 1, 32),
        )

    def first_exchange(terms_z, terms_x):
        return exchange(terms_z[1], "z", first_bits), exchange(terms_x[1], "x", first_bits)

    def plane_sums(terms_z, terms_x, received):
        sum_z = add(terms_z[0], received[0])
        sum_x = add(terms_x[0], received[1])
        sum_z = reduce_step(sum_z, "x", first_bits, 32)
        sum_x = reduce_step(sum_x, "z", first_bits, 64)
        return jnp.concatenate([sum_z, sum_x], axis=1)

    with jax.named_scope("early_tokens"):
        early_terms = terms(codes_of([resid, near]))
        early_received = first_exchange(*early_terms)
        (far, opposite), _ = lax.optimization_barrier(((far, opposite), early_terms))
    with jax.named_scope("late_tokens"):
        late_terms = terms(codes_of([far, opposite]))
        late_received = first_exchange(*late_terms)
        (early_received, _) = lax.optimization_barrier((early_received, late_terms))
        early = plane_sums(*early_terms, early_received)
        late = plane_sums(*late_terms, late_received)

    with jax.named_scope("sum_over_chips"):
        quarter = tok_rows // 4
        near_sums = exchange(early[quarter:], "y", first_bits)
        far_sums = exchange(late[:quarter], "y", second_bits)
        opposite_sums = exchange(late[quarter:], "y", lambda core: 2)
        total = early[:quarter].astype(F32) + near_sums.astype(F32)
        total = (total + far_sums.astype(F32) + opposite_sums.astype(F32)).astype(BF16)
        total = add(total, swap_halves(exchange(total, "z", second_bits), 32))
        other = swap_halves(exchange(total, "x", second_bits), 16)
        total = total.astype(F32) + other.astype(F32)
        rest = (total + b_dec).astype(BF16)
        restored = rest[:8]

    with jax.named_scope("gather_restored"):
        rest_z = gather_step(rest[:, :part], "x", first_bits, 16)
        rest_x = gather_step(rest[:, part:], "z", first_bits, 32)
        rest_z = gather_step(rest_z, "z", first_bits, 64)
        rest_x = gather_step(rest_x, "x", first_bits, 16)

    with jax.named_scope("projections"):
        query_ctx = PREFIX + seq_place * tok_rows + order
        freq = THETA ** (-(jnp.arange(head_size // 2, dtype=F32) * 2.0 / head_size))
        angle = query_ctx.astype(F32)[:, None] * freq[None, :]
        cosine, sine = jnp.cos(angle), jnp.sin(angle)
        cosine = jnp.concatenate([cosine, cosine], axis=1)
        sine = jnp.concatenate([-sine, sine], axis=1)
        query, own_pairs = project(
            rest_z,
            rest_x,
            pre_gain[None, :],
            w_query,
            w_key,
            w_value,
            jnp.stack([q_gain, k_gain]),
            cosine,
            sine,
            cache_key,
            cache_value,
        )

    with jax.named_scope("attention"):
        pre_rows = cache_key.shape[0]
        pairs = lax.all_gather(own_pairs, "seq", axis=0, tiled=True)
        orders = jnp.stack([row_order(z, x, jnp.int32(i)) for i in range(NC)])
        shard = jnp.arange(NY * NC, dtype=jnp.int32)
        new_ctx = PREFIX + shard[:, None] * tok_rows + jnp.tile(orders, (NY, 1))
        old_ctx = shard[:, None] * pre_rows + jnp.arange(pre_rows, dtype=jnp.int32)[None, :]
        key_ctx = jnp.concatenate([old_ctx, new_ctx], axis=1).reshape(1, -1)
        first_ctx = jnp.sum(jnp.where(pick, starts[None, :], 0), axis=1)
        keep_z, send_z, keep_x, send_x = attend(
            query, pairs, key_ctx, query_ctx[:, None], first_ctx[:, None], w_out
        )

    with jax.named_scope("sum_over_heads"):
        out_z = add(keep_z, exchange(send_z, "z", first_bits))
        out_x = add(keep_x, exchange(send_x, "x", first_bits))
        out_z = reduce_step(out_z, "x", first_bits, 32)
        out_x = reduce_step(out_x, "z", first_bits, 64)
        both = jnp.concatenate([out_z, out_x], axis=1)
        both = reduce_step(both, "z", second_bits, 32)
        keep, send = split(both, 16)
        mine = keep.astype(F32) + exchange(send, "x", second_bits).astype(F32)
        return (restored.astype(F32) + rms_scale(mine, post_gain)).astype(BF16)


def solution(mesh):
    in_specs = (
        P("seq", None),
        P(None, ("seq", "lat")),
        P(("seq", "lat")),
        P(("seq", "lat")),
        P(("seq", "lat"), None),
        P(),
        P(),
        P(),
        P(),
        P(),
        P(None, "lat"),
        P(None, "lat"),
        P(None, "lat"),
        P(),
        P(),
        P("seq", "lat"),
        P("seq", "lat"),
        P("seq"),
        P("lat", None),
        P(),
    )
    out_specs = P(("seq", "lat"), None)
    return jax.shard_map(
        per_device, mesh=mesh, in_specs=in_specs, out_specs=out_specs, check_vma=False
    )
```

```python
import functools

import jax
import jax.numpy as jnp
from jax import lax
from jax.experimental import pallas as pl
from jax.experimental.pallas import tpu as pltpu
from jax.sharding import PartitionSpec as P

WINDOW = 1024
PREFIX = 512
EPS = 1e-06
THETA = 10000.0
QUERY_SCALE = 168.0 ** (-0.5)

NY, NC, NZ, NX = 4, 2, 4, 4
AXES = ("seq", "lat")
TILE = 896
F32, BF16 = jnp.float32, jnp.bfloat16


def first_bits(core):
    return 1 if core == 0 else 3


def second_bits(core):
    return 3 if core == 0 else 1


def exchange(value, dim, bits):
    pairs = []
    for y in range(NY):
        for c in range(NC):
            for z in range(NZ):
                for x in range(NX):
                    to = {"y": y, "c": c, "z": z, "x": x}
                    to[dim] ^= bits(c)
                    pairs.append(
                        (
                            (y * NC + c) * NZ * NX + z * NX + x,
                            (to["y"] * NC + to["c"]) * NZ * NX + to["z"] * NX + to["x"],
                        )
                    )
    return lax.ppermute(value, AXES, pairs)


def swap_cores(value):
    return exchange(value, "c", lambda core: 1)


def relative(place, core):
    step = jnp.arange(4, dtype=jnp.int32)
    order0 = jnp.where(step == 1, 3, jnp.where(step == 2, 1, jnp.where(step == 3, 2, 0)))
    order1 = jnp.where(step == 1, 1, jnp.where(step == 2, 3, jnp.where(step == 3, 2, 0)))
    return place ^ jnp.where(core == 0, order0, order1)


def row_order(z, x, core):
    zs, xs = relative(z, core), relative(x, core)
    row = (zs[:, None] * NX + xs[None, :])[:, :, None] * 8 + jnp.arange(8, dtype=jnp.int32)
    return row.reshape(-1)


def rms_scale(values, gain):
    return values * lax.rsqrt(jnp.mean(values * values, axis=-1, keepdims=True) + EPS) * gain


def stage_kernel(source_ref, target_ref, sem):
    copy = pltpu.make_async_copy(source_ref, target_ref, sem)
    copy.start()
    copy.wait()


def stage(value):
    return pl.pallas_call(
        stage_kernel,
        name="stage",
        out_shape=jax.ShapeDtypeStruct(value.shape, value.dtype),
        in_specs=[pl.BlockSpec(memory_space=pl.ANY)],
        out_specs=pl.BlockSpec(memory_space=pltpu.VMEM),
        scratch_shapes=[pltpu.SemaphoreType.DMA],
        compiler_params=pltpu.CompilerParams(vmem_limit_bytes=6 * 1024 * 1024),
        cost_estimate=pl.CostEstimate(flops=0, bytes_accessed=2 * value.size, transcendentals=0),
    )(value)


def encode_kernel(count, *refs):
    blocks = refs[:count]
    picks = refs[count : 2 * count]
    own_ref, sib_ref, params_ref, codes_ref, rows_ref = refs[2 * count :]
    size = blocks[0].shape[0]
    lats = own_ref.shape[1]
    for i in range(count):
        rows_ref[i * size : (i + 1) * size, :] = blocks[i][...]
    for side, weights_ref in enumerate((own_ref, sib_ref)):
        there = slice(side * lats, (side + 1) * lats)
        pre = jnp.dot(rows_ref[...], weights_ref[...], preferred_element_type=F32)
        act = jnp.maximum(pre + params_ref[0:1, there] - params_ref[1:2, there], 0.0)
        codes = jnp.where(params_ref[2:3, there] > 0.0, params_ref[3:4, there], act)
        codes = codes.astype(BF16)
        for i in range(count):
            moved = jnp.dot(
                picks[i][...], codes[i * size : (i + 1) * size], preferred_element_type=F32
            )
            codes_ref[i * size : (i + 1) * size, there] = moved.astype(BF16)


def encode(blocks, picks, own, sib, params):
    count = len(blocks)
    size, width = blocks[0].shape
    lats = own.shape[1]
    return pl.pallas_call(
        functools.partial(encode_kernel, count),
        name="encode",
        out_shape=jax.ShapeDtypeStruct((count * size, 2 * lats), BF16),
        scratch_shapes=[pltpu.VMEM((count * size, width), BF16)],
        compiler_params=pltpu.CompilerParams(vmem_limit_bytes=12 * 1024 * 1024),
        cost_estimate=pl.CostEstimate(
            flops=4 * count * size * width * lats,
            bytes_accessed=4 * width * lats + 2 * count * size * (width + 2 * lats),
            transcendentals=0,
        ),
    )(*blocks, *picks, own, sib, params)


def decode_kernel(part, group, codes_ref, own_ref, sib_ref, keep_ref, send_ref):
    size = codes_ref.shape[0]
    lats, width = own_ref.shape
    half = group // 2
    for tile in range(width // 2 // TILE):
        here = slice(tile * TILE, (tile + 1) * TILE)
        there = slice(part * (width // 2) + tile * TILE, part * (width // 2) + (tile + 1) * TILE)
        total = jnp.dot(codes_ref[:, :lats], own_ref[:, there], preferred_element_type=F32)
        total += jnp.dot(codes_ref[:, lats:], sib_ref[:, there], preferred_element_type=F32)
        total = total.astype(BF16)
        for i in range(size // group):
            keep_ref[i * half : (i + 1) * half, here] = total[i * group : i * group + half, :]
            send_ref[i * half : (i + 1) * half, here] = total[i * group + half : (i + 1) * group, :]


def decode(codes, own, sib, part, group):
    size = codes.shape[0]
    lats, width = own.shape
    out = jax.ShapeDtypeStruct((size // 2, width // 2), BF16)
    return pl.pallas_call(
        functools.partial(decode_kernel, part, group),
        name="decode",
        out_shape=(out, out),
        compiler_params=pltpu.CompilerParams(vmem_limit_bytes=12 * 1024 * 1024),
        cost_estimate=pl.CostEstimate(
            flops=2 * size * lats * width,
            bytes_accessed=2 * (lats * width + 2 * size * lats + size * width // 2),
            transcendentals=0,
        ),
    )(codes, own, sib)


def project_kernel(
    left_ref,
    right_ref,
    gain_ref,
    query_w,
    key_w,
    value_w,
    head_gains,
    cosine_ref,
    sine_ref,
    cache_key,
    cache_value,
    query_ref,
    pairs_ref,
    normed_ref,
):
    part = left_ref.shape[1]
    hd = key_w.shape[1]
    left, right = left_ref[...].astype(F32), right_ref[...].astype(F32)
    square = jnp.sum(left * left, axis=-1, keepdims=True) + jnp.sum(
        right * right, axis=-1, keepdims=True
    )
    scale = lax.rsqrt(square / (2 * part) + EPS)
    normed_ref[:, :part] = (left * scale * gain_ref[0:1, :part]).astype(BF16)
    normed_ref[:, part:] = (right * scale * gain_ref[0:1, part:]).astype(BF16)
    normed = normed_ref[...]

    def turn(values, gain):
        values = rms_scale(values, gain)
        return (
            values * cosine_ref[...] + pltpu.roll(values, hd // 2, axis=1) * sine_ref[...]
        ).astype(BF16)

    old = cache_key.shape[0]
    pairs_ref[:old, :hd] = cache_key[...]
    pairs_ref[:old, hd:] = cache_value[...]
    key = jnp.dot(normed, key_w[...], preferred_element_type=F32)
    pairs_ref[old:, :hd] = turn(key, head_gains[1:2, :])
    value = jnp.dot(normed, value_w[...], preferred_element_type=F32)
    pairs_ref[old:, hd:] = value.astype(BF16)
    query = jnp.dot(normed, query_w[...], preferred_element_type=F32)
    for h in range(query_ref.shape[1] // hd):
        query_ref[:, h * hd : (h + 1) * hd] = turn(
            query[:, h * hd : (h + 1) * hd], head_gains[0:1, :]
        )


def project(left, right, gain, query_w, key_w, value_w, gains, cosine, sine, old_key, old_value):
    rows, hd = left.shape[0], key_w.shape[1]
    width = query_w.shape[0]
    return pl.pallas_call(
        project_kernel,
        name="project",
        out_shape=(
            jax.ShapeDtypeStruct((rows, query_w.shape[1]), BF16),
            jax.ShapeDtypeStruct((old_key.shape[0] + rows, 2 * hd), BF16),
        ),
        scratch_shapes=[pltpu.VMEM((rows, width), BF16)],
        compiler_params=pltpu.CompilerParams(vmem_limit_bytes=12 * 1024 * 1024),
        cost_estimate=pl.CostEstimate(
            flops=8 * rows * width * hd,
            bytes_accessed=8 * width * hd + 2 * rows * width,
            transcendentals=0,
        ),
    )(left, right, gain, query_w, key_w, value_w, gains, cosine, sine, old_key, old_value)


def attend_kernel(
    query_ref,
    pairs_ref,
    key_ctx,
    query_ctx,
    first_ctx,
    out_w,
    keep_z,
    send_z,
    keep_x,
    send_x,
    attended_ref,
):
    rows, hd = query_ref.shape[0], pairs_ref.shape[1] // 2
    allowed = (
        (key_ctx[...] <= query_ctx[...])
        & (key_ctx[...] > query_ctx[...] - WINDOW)
        & (key_ctx[...] >= first_ctx[...])
    )
    for h in range(query_ref.shape[1] // hd):
        scores = (
            lax.dot_general(
                query_ref[:, h * hd : (h + 1) * hd],
                pairs_ref[:, :hd],
                (((1,), (1,)), ((), ())),
                preferred_element_type=F32,
            )
            * QUERY_SCALE
        )
        scores = jnp.where(allowed, scores, -1e30)
        newest = jnp.max(scores, axis=-1, keepdims=True)
        weights = jnp.where(allowed, jnp.exp(scores - newest), 0.0)
        total = jnp.sum(weights, axis=-1, keepdims=True)
        mixed = jnp.dot(weights.astype(BF16), pairs_ref[:, hd:], preferred_element_type=F32)
        attended_ref[:, h * hd : (h + 1) * hd] = (mixed / total).astype(BF16)
    attended = attended_ref[...]
    part = out_w.shape[1] // 2
    for tile in range(part // TILE):
        here = slice(tile * TILE, (tile + 1) * TILE)
        left = jnp.dot(attended, out_w[:, here], preferred_element_type=F32).astype(BF16)
        keep_z[:, here] = left[: rows // 2]
        send_z[:, here] = left[rows // 2 :]
        there = slice(part + tile * TILE, part + (tile + 1) * TILE)
        right = jnp.dot(attended, out_w[:, there], preferred_element_type=F32).astype(BF16)
        for i in range(4):
            keep_x[i * 16 : (i + 1) * 16, here] = right[i * 32 : i * 32 + 16]
            send_x[i * 16 : (i + 1) * 16, here] = right[i * 32 + 16 : i * 32 + 32]


def attend(query, pairs, key_ctx, query_ctx, first_ctx, out_w):
    rows, width = query.shape[0], out_w.shape[1]
    out = jax.ShapeDtypeStruct((rows // 2, width // 2), BF16)
    return pl.pallas_call(
        attend_kernel,
        name="attend",
        out_shape=(out, out, out, out),
        scratch_shapes=[pltpu.VMEM((rows, query.shape[1]), BF16)],
        compiler_params=pltpu.CompilerParams(vmem_limit_bytes=12 * 1024 * 1024),
        cost_estimate=pl.CostEstimate(
            flops=2 * rows * query.shape[1] * (2 * pairs.shape[0] + width),
            bytes_accessed=2 * (query.shape[1] * width + rows * width + pairs.size),
            transcendentals=2 * rows * pairs.shape[0],
        ),
    )(query, pairs, key_ctx, query_ctx, first_ctx, out_w)


def split(value, group):
    rows, width = value.shape
    grouped = value.reshape(rows // group, group, width)
    half = group // 2
    return (
        grouped[:, :half].reshape(rows // 2, width),
        grouped[:, half:].reshape(rows // 2, width),
    )


def add(left, right):
    return (left.astype(F32) + right.astype(F32)).astype(BF16)


def reduce_step(value, dim, bits, group):
    keep, send = split(value, group)
    return add(keep, exchange(send, dim, bits))


def swap_halves(value, group):
    keep, send = split(value, group)
    rows, width = value.shape
    half = group // 2
    return jnp.concatenate(
        [send.reshape(-1, half, width), keep.reshape(-1, half, width)], axis=1
    ).reshape(rows, width)


def gather_step(value, dim, bits, group):
    other = exchange(value, dim, bits)
    rows, width = value.shape
    return jnp.concatenate(
        [value.reshape(-1, group, width), other.reshape(-1, group, width)], axis=1
    ).reshape(2 * rows, width)


def per_device(
    resid,
    w_enc,
    b_enc,
    threshold,
    w_dec,
    b_dec,
    clamp_ids,
    clamp_index,
    clamp_table,
    pre_gain,
    w_query,
    w_key,
    w_value,
    q_gain,
    k_gain,
    cache_key,
    cache_value,
    starts,
    w_out,
    post_gain,
):
    seq_place = lax.axis_index("seq")
    lat_place = lax.axis_index("lat")
    core = seq_place % NC
    z, x = lat_place // NX, lat_place % NX
    tok_rows, width = resid.shape
    part = width // 2
    lats = w_enc.shape[1]
    head_size = q_gain.shape[0]

    order = row_order(z, x, core)
    pick = order[:, None] == jnp.arange(tok_rows, dtype=jnp.int32)[None, :]

    with jax.named_scope("gather_resid"):
        quarter = tok_rows // 4
        piece = 2 * (z % 2) + x % 2
        mine = lax.dynamic_slice_in_dim(resid, piece * quarter, quarter, 0)
        mine = exchange(mine, "y", lambda core: 2)
        near = exchange(resid, "y", first_bits)
        left, right = mine[:, :part], mine[:, part:]
        left = jnp.concatenate([left, exchange(left, "x", first_bits)])
        right = jnp.concatenate([right, exchange(right, "z", first_bits)])
        left = jnp.concatenate([left, exchange(left, "z", first_bits)])
        more = exchange(right, "x", first_bits)
        right = jnp.concatenate(
            [right[:quarter], more[:quarter], right[quarter:], more[quarter:]]
        )
        opposite = jnp.concatenate([left, right], axis=1)
        again, near = lax.optimization_barrier((resid, near))
        far = exchange(again, "y", second_bits)
        spot = jnp.arange(tok_rows, dtype=jnp.int32)
        spot = (piece ^ (spot // quarter)) * quarter + spot % quarter
        pick_opposite = (order[:, None] == spot[None, :]).astype(BF16)

    with jax.named_scope("swap_weights"):
        offsets = jnp.stack([b_enc, threshold])
        sib_offsets = swap_cores(offsets)
        sib_enc = stage(swap_cores(w_enc))
        sib_dec = stage(swap_cores(w_dec))

    with jax.named_scope("clamp"):
        table_pick = (
            clamp_index[:, None] == jnp.arange(clamp_table.shape[0], dtype=jnp.int32)[None, :]
        )
        values = jnp.sum(jnp.where(table_pick, clamp_table[None, :], 0.0), axis=1)
        spread = jnp.arange(lats, dtype=jnp.int32)
        here = jnp.concatenate(
            [
                (seq_place * NZ * NX + lat_place) * lats + spread,
                ((seq_place ^ 1) * NZ * NX + lat_place) * lats + spread,
            ]
        )
        match = here[None, :] == clamp_ids[:, None]
        clamped = jnp.any(match, axis=0).astype(F32)
        level = jnp.sum(jnp.where(match, values[:, None], 0.0), axis=0)
        params = jnp.concatenate(
            [
                jnp.concatenate([offsets, sib_offsets], axis=1),
                clamped[None, :],
                level[None, :],
            ],
            axis=0,
        )

    def terms(codes):
        return (
            decode(codes, w_dec, sib_dec, 0, 128),
            decode(codes, w_dec, sib_dec, 1, 32),
        )

    def first_exchange(terms_z, terms_x):
        return exchange(terms_z[1], "z", first_bits), exchange(terms_x[1], "x", first_bits)

    def plane_sums(terms_z, terms_x, received):
        sum_z = add(terms_z[0], received[0])
        sum_x = add(terms_x[0], received[1])
        sum_z = reduce_step(sum_z, "x", first_bits, 32)
        sum_x = reduce_step(sum_x, "z", first_bits, 64)
        return jnp.concatenate([sum_z, sum_x], axis=1)

    with jax.named_scope("early_tokens"):
        pick_rows = pick.astype(BF16)
        early_terms = terms(
            encode([near, opposite], [pick_rows, pick_opposite], w_enc, sib_enc, params)
        )
        early_received = first_exchange(*early_terms)
        far, _ = lax.optimization_barrier((far, early_terms))
    with jax.named_scope("late_tokens"):
        late_codes = encode([resid, far], [pick_rows, pick_rows], w_enc, sib_enc, params)
        late_codes, early_received = lax.optimization_barrier((late_codes, early_received))
        early = plane_sums(*early_terms, early_received)
        late_terms = terms(late_codes)
        late = plane_sums(*late_terms, first_exchange(*late_terms))

    with jax.named_scope("sum_over_chips"):
        total = add(late, exchange(early, "y", first_bits))
        total = add(total[:quarter], exchange(total[quarter:], "y", second_bits))
        total = add(total, swap_halves(exchange(total, "z", second_bits), 32))
        other = swap_halves(exchange(total, "x", second_bits), 16)
        total = total.astype(F32) + other.astype(F32)
        rest = (total + b_dec).astype(BF16)
        restored = rest[:8]

    with jax.named_scope("gather_restored"):
        rest_z = gather_step(rest[:, :part], "x", first_bits, 16)
        rest_x = gather_step(rest[:, part:], "z", first_bits, 32)
        rest_z = gather_step(rest_z, "z", first_bits, 64)
        rest_x = gather_step(rest_x, "x", first_bits, 16)

    with jax.named_scope("projections"):
        query_ctx = PREFIX + seq_place * tok_rows + order
        freq = THETA ** (-(jnp.arange(head_size // 2, dtype=F32) * 2.0 / head_size))
        angle = query_ctx.astype(F32)[:, None] * freq[None, :]
        cosine, sine = jnp.cos(angle), jnp.sin(angle)
        cosine = jnp.concatenate([cosine, cosine], axis=1)
        sine = jnp.concatenate([-sine, sine], axis=1)
        query, own_pairs = project(
            rest_z,
            rest_x,
            pre_gain[None, :],
            w_query,
            w_key,
            w_value,
            jnp.stack([q_gain, k_gain]),
            cosine,
            sine,
            cache_key,
            cache_value,
        )

    with jax.named_scope("attention"):
        pre_rows = cache_key.shape[0]
        pairs = lax.all_gather(own_pairs, "seq", axis=0, tiled=True)
        orders = jnp.stack([row_order(z, x, jnp.int32(i)) for i in range(NC)])
        shard = jnp.arange(NY * NC, dtype=jnp.int32)
        new_ctx = PREFIX + shard[:, None] * tok_rows + jnp.tile(orders, (NY, 1))
        old_ctx = shard[:, None] * pre_rows + jnp.arange(pre_rows, dtype=jnp.int32)[None, :]
        key_ctx = jnp.concatenate([old_ctx, new_ctx], axis=1).reshape(1, -1)
        first_ctx = jnp.sum(jnp.where(pick, starts[None, :], 0), axis=1)
        keep_z, send_z, keep_x, send_x = attend(
            query, pairs, key_ctx, query_ctx[:, None], first_ctx[:, None], w_out
        )

    with jax.named_scope("sum_over_heads"):
        out_z = add(keep_z, exchange(send_z, "z", first_bits))
        out_x = add(keep_x, exchange(send_x, "x", first_bits))
        out_z = reduce_step(out_z, "x", first_bits, 32)
        out_x = reduce_step(out_x, "z", first_bits, 64)
        both = jnp.concatenate([out_z, out_x], axis=1)
        both = reduce_step(both, "z", second_bits, 32)
        keep, send = split(both, 16)
        mine = keep.astype(F32) + exchange(send, "x", second_bits).astype(F32)
        return (restored.astype(F32) + rms_scale(mine, post_gain)).astype(BF16)


def solution(mesh):
    in_specs = (
        P("seq", None),
        P(None, ("seq", "lat")),
        P(("seq", "lat")),
        P(("seq", "lat")),
        P(("seq", "lat"), None),
        P(),
        P(),
        P(),
        P(),
        P(),
        P(None, "lat"),
        P(None, "lat"),
        P(None, "lat"),
        P(),
        P(),
        P("seq", "lat"),
        P("seq", "lat"),
        P("seq"),
        P("lat", None),
        P(),
    )
    out_specs = P(("seq", "lat"), None)
    return jax.shard_map(
        per_device, mesh=mesh, in_specs=in_specs, out_specs=out_specs, check_vma=False
    )
```

```python
import functools

import jax
import jax.numpy as jnp
from jax import lax
from jax.experimental import pallas as pl
from jax.experimental.pallas import tpu as pltpu
from jax.sharding import PartitionSpec as P

WINDOW = 1024
PREFIX = 512
EPS = 1e-06
THETA = 10000.0
QUERY_SCALE = 168.0 ** (-0.5)

NY, NC, NZ, NX = 4, 2, 4, 4
AXES = ("seq", "lat")
TILE = 896
F32, BF16 = jnp.float32, jnp.bfloat16


def first_bits(core):
    return 1 if core == 0 else 3


def second_bits(core):
    return 3 if core == 0 else 1


def exchange(value, dim, bits):
    pairs = []
    for y in range(NY):
        for c in range(NC):
            for z in range(NZ):
                for x in range(NX):
                    to = {"y": y, "c": c, "z": z, "x": x}
                    to[dim] ^= bits(c)
                    pairs.append(
                        (
                            (y * NC + c) * NZ * NX + z * NX + x,
                            (to["y"] * NC + to["c"]) * NZ * NX + to["z"] * NX + to["x"],
                        )
                    )
    return lax.ppermute(value, AXES, pairs)


def swap_cores(value):
    return exchange(value, "c", lambda core: 1)


def relative(place, core):
    step = jnp.arange(4, dtype=jnp.int32)
    order0 = jnp.where(step == 1, 3, jnp.where(step == 2, 1, jnp.where(step == 3, 2, 0)))
    order1 = jnp.where(step == 1, 1, jnp.where(step == 2, 3, jnp.where(step == 3, 2, 0)))
    return place ^ jnp.where(core == 0, order0, order1)


def row_order(z, x, core):
    zs, xs = relative(z, core), relative(x, core)
    row = (zs[:, None] * NX + xs[None, :])[:, :, None] * 8 + jnp.arange(8, dtype=jnp.int32)
    return row.reshape(-1)


def rms_scale(values, gain):
    return values * lax.rsqrt(jnp.mean(values * values, axis=-1, keepdims=True) + EPS) * gain


def stage_kernel(source_ref, target_ref, sem):
    copy = pltpu.make_async_copy(source_ref, target_ref, sem)
    copy.start()
    copy.wait()


def stage(value):
    return pl.pallas_call(
        stage_kernel,
        name="stage",
        out_shape=jax.ShapeDtypeStruct(value.shape, value.dtype),
        in_specs=[pl.BlockSpec(memory_space=pl.ANY)],
        out_specs=pl.BlockSpec(memory_space=pltpu.VMEM),
        scratch_shapes=[pltpu.SemaphoreType.DMA],
        compiler_params=pltpu.CompilerParams(vmem_limit_bytes=6 * 1024 * 1024),
        cost_estimate=pl.CostEstimate(flops=0, bytes_accessed=2 * value.size, transcendentals=0),
    )(value)


def encode_kernel(count, *refs):
    blocks = refs[:count]
    picks = refs[count : 2 * count]
    own_ref, sib_ref, params_ref, codes_ref, rows_ref = refs[2 * count :]
    size = blocks[0].shape[0]
    lats = own_ref.shape[1]
    for i in range(count):
        rows_ref[i * size : (i + 1) * size, :] = blocks[i][...]
    for side, weights_ref in enumerate((own_ref, sib_ref)):
        there = slice(side * lats, (side + 1) * lats)
        pre = jnp.dot(rows_ref[...], weights_ref[...], preferred_element_type=F32)
        act = jnp.maximum(pre + params_ref[0:1, there] - params_ref[1:2, there], 0.0)
        codes = jnp.where(params_ref[2:3, there] > 0.0, params_ref[3:4, there], act)
        codes = codes.astype(BF16)
        for i in range(count):
            moved = jnp.dot(
                picks[i][...], codes[i * size : (i + 1) * size], preferred_element_type=F32
            )
            codes_ref[i * size : (i + 1) * size, there] = moved.astype(BF16)


def encode(blocks, picks, own, sib, params):
    count = len(blocks)
    size, width = blocks[0].shape
    lats = own.shape[1]
    return pl.pallas_call(
        functools.partial(encode_kernel, count),
        name="encode",
        out_shape=jax.ShapeDtypeStruct((count * size, 2 * lats), BF16),
        scratch_shapes=[pltpu.VMEM((count * size, width), BF16)],
        compiler_params=pltpu.CompilerParams(vmem_limit_bytes=12 * 1024 * 1024),
        cost_estimate=pl.CostEstimate(
            flops=4 * count * size * width * lats,
            bytes_accessed=4 * width * lats + 2 * count * size * (width + 2 * lats),
            transcendentals=0,
        ),
    )(*blocks, *picks, own, sib, params)


def decode_kernel(part, group, codes_ref, own_ref, sib_ref, keep_ref, send_ref):
    size = codes_ref.shape[0]
    lats, width = own_ref.shape
    half = group // 2
    for tile in range(width // 2 // TILE):
        here = slice(tile * TILE, (tile + 1) * TILE)
        there = slice(part * (width // 2) + tile * TILE, part * (width // 2) + (tile + 1) * TILE)
        total = jnp.dot(codes_ref[:, :lats], own_ref[:, there], preferred_element_type=F32)
        total += jnp.dot(codes_ref[:, lats:], sib_ref[:, there], preferred_element_type=F32)
        total = total.astype(BF16)
        for i in range(size // group):
            keep_ref[i * half : (i + 1) * half, here] = total[i * group : i * group + half, :]
            send_ref[i * half : (i + 1) * half, here] = total[i * group + half : (i + 1) * group, :]


def decode(codes, own, sib, part, group):
    size = codes.shape[0]
    lats, width = own.shape
    out = jax.ShapeDtypeStruct((size // 2, width // 2), BF16)
    return pl.pallas_call(
        functools.partial(decode_kernel, part, group),
        name="decode",
        out_shape=(out, out),
        compiler_params=pltpu.CompilerParams(vmem_limit_bytes=12 * 1024 * 1024),
        cost_estimate=pl.CostEstimate(
            flops=2 * size * lats * width,
            bytes_accessed=2 * (lats * width + 2 * size * lats + size * width // 2),
            transcendentals=0,
        ),
    )(codes, own, sib)


def project_kernel(
    left_ref,
    right_ref,
    gain_ref,
    query_w,
    key_w,
    value_w,
    head_gains,
    cosine_ref,
    sine_ref,
    cache_key,
    cache_value,
    query_ref,
    pairs_ref,
    normed_ref,
):
    part = left_ref.shape[1]
    hd = key_w.shape[1]
    left, right = left_ref[...].astype(F32), right_ref[...].astype(F32)
    square = jnp.sum(left * left, axis=-1, keepdims=True) + jnp.sum(
        right * right, axis=-1, keepdims=True
    )
    scale = lax.rsqrt(square / (2 * part) + EPS)
    normed_ref[:, :part] = (left * scale * gain_ref[0:1, :part]).astype(BF16)
    normed_ref[:, part:] = (right * scale * gain_ref[0:1, part:]).astype(BF16)
    normed = normed_ref[...]

    def turn(values, gain):
        values = rms_scale(values, gain)
        return (
            values * cosine_ref[...] + pltpu.roll(values, hd // 2, axis=1) * sine_ref[...]
        ).astype(BF16)

    old = cache_key.shape[0]
    pairs_ref[:old, :hd] = cache_key[...]
    pairs_ref[:old, hd:] = cache_value[...]
    key = jnp.dot(normed, key_w[...], preferred_element_type=F32)
    pairs_ref[old:, :hd] = turn(key, head_gains[1:2, :])
    value = jnp.dot(normed, value_w[...], preferred_element_type=F32)
    pairs_ref[old:, hd:] = value.astype(BF16)
    query = jnp.dot(normed, query_w[...], preferred_element_type=F32)
    for h in range(query_ref.shape[1] // hd):
        query_ref[:, h * hd : (h + 1) * hd] = turn(
            query[:, h * hd : (h + 1) * hd], head_gains[0:1, :]
        )


def project(left, right, gain, query_w, key_w, value_w, gains, cosine, sine, old_key, old_value):
    rows, hd = left.shape[0], key_w.shape[1]
    width = query_w.shape[0]
    return pl.pallas_call(
        project_kernel,
        name="project",
        out_shape=(
            jax.ShapeDtypeStruct((rows, query_w.shape[1]), BF16),
            jax.ShapeDtypeStruct((old_key.shape[0] + rows, 2 * hd), BF16),
        ),
        scratch_shapes=[pltpu.VMEM((rows, width), BF16)],
        compiler_params=pltpu.CompilerParams(vmem_limit_bytes=12 * 1024 * 1024),
        cost_estimate=pl.CostEstimate(
            flops=8 * rows * width * hd,
            bytes_accessed=8 * width * hd + 2 * rows * width,
            transcendentals=0,
        ),
    )(left, right, gain, query_w, key_w, value_w, gains, cosine, sine, old_key, old_value)


def attend_kernel(
    query_ref,
    pairs_ref,
    key_ctx,
    query_ctx,
    first_ctx,
    out_w,
    keep_z,
    send_z,
    keep_x,
    send_x,
    attended_ref,
):
    rows, hd = query_ref.shape[0], pairs_ref.shape[1] // 2
    allowed = (
        (key_ctx[...] <= query_ctx[...])
        & (key_ctx[...] > query_ctx[...] - WINDOW)
        & (key_ctx[...] >= first_ctx[...])
    )
    for h in range(query_ref.shape[1] // hd):
        scores = (
            lax.dot_general(
                query_ref[:, h * hd : (h + 1) * hd],
                pairs_ref[:, :hd],
                (((1,), (1,)), ((), ())),
                preferred_element_type=F32,
            )
            * QUERY_SCALE
        )
        scores = jnp.where(allowed, scores, -1e30)
        newest = jnp.max(scores, axis=-1, keepdims=True)
        weights = jnp.where(allowed, jnp.exp(scores - newest), 0.0)
        total = jnp.sum(weights, axis=-1, keepdims=True)
        mixed = jnp.dot(weights.astype(BF16), pairs_ref[:, hd:], preferred_element_type=F32)
        attended_ref[:, h * hd : (h + 1) * hd] = (mixed / total).astype(BF16)
    attended = attended_ref[...]
    part = out_w.shape[1] // 2
    for tile in range(part // TILE):
        here = slice(tile * TILE, (tile + 1) * TILE)
        left = jnp.dot(attended, out_w[:, here], preferred_element_type=F32).astype(BF16)
        keep_z[:, here] = left[: rows // 2]
        send_z[:, here] = left[rows // 2 :]
        there = slice(part + tile * TILE, part + (tile + 1) * TILE)
        right = jnp.dot(attended, out_w[:, there], preferred_element_type=F32).astype(BF16)
        for i in range(4):
            keep_x[i * 16 : (i + 1) * 16, here] = right[i * 32 : i * 32 + 16]
            send_x[i * 16 : (i + 1) * 16, here] = right[i * 32 + 16 : i * 32 + 32]


def attend(query, pairs, key_ctx, query_ctx, first_ctx, out_w):
    rows, width = query.shape[0], out_w.shape[1]
    out = jax.ShapeDtypeStruct((rows // 2, width // 2), BF16)
    return pl.pallas_call(
        attend_kernel,
        name="attend",
        out_shape=(out, out, out, out),
        scratch_shapes=[pltpu.VMEM((rows, query.shape[1]), BF16)],
        compiler_params=pltpu.CompilerParams(vmem_limit_bytes=12 * 1024 * 1024),
        cost_estimate=pl.CostEstimate(
            flops=2 * rows * query.shape[1] * (2 * pairs.shape[0] + width),
            bytes_accessed=2 * (query.shape[1] * width + rows * width + pairs.size),
            transcendentals=2 * rows * pairs.shape[0],
        ),
    )(query, pairs, key_ctx, query_ctx, first_ctx, out_w)


def split(value, group):
    rows, width = value.shape
    grouped = value.reshape(rows // group, group, width)
    half = group // 2
    return (
        grouped[:, :half].reshape(rows // 2, width),
        grouped[:, half:].reshape(rows // 2, width),
    )


def add(left, right):
    return (left.astype(F32) + right.astype(F32)).astype(BF16)


def reduce_step(value, dim, bits, group):
    keep, send = split(value, group)
    return add(keep, exchange(send, dim, bits))


def swap_halves(value, group):
    keep, send = split(value, group)
    rows, width = value.shape
    half = group // 2
    return jnp.concatenate(
        [send.reshape(-1, half, width), keep.reshape(-1, half, width)], axis=1
    ).reshape(rows, width)


def gather_step(value, dim, bits, group):
    other = exchange(value, dim, bits)
    rows, width = value.shape
    return jnp.concatenate(
        [value.reshape(-1, group, width), other.reshape(-1, group, width)], axis=1
    ).reshape(2 * rows, width)


def per_device(
    resid,
    w_enc,
    b_enc,
    threshold,
    w_dec,
    b_dec,
    clamp_ids,
    clamp_index,
    clamp_table,
    pre_gain,
    w_query,
    w_key,
    w_value,
    q_gain,
    k_gain,
    cache_key,
    cache_value,
    starts,
    w_out,
    post_gain,
):
    seq_place = lax.axis_index("seq")
    lat_place = lax.axis_index("lat")
    core = seq_place % NC
    z, x = lat_place // NX, lat_place % NX
    tok_rows, width = resid.shape
    part = width // 2
    lats = w_enc.shape[1]
    head_size = q_gain.shape[0]

    order = row_order(z, x, core)
    pick = order[:, None] == jnp.arange(tok_rows, dtype=jnp.int32)[None, :]

    with jax.named_scope("gather_resid"):
        quarter = tok_rows // 4
        piece = 2 * (z % 2) + x % 2
        near = exchange(resid, "y", first_bits)
        mine = lax.dynamic_slice_in_dim(near, piece * quarter, quarter, 0)
        again, mine = lax.optimization_barrier((resid, mine))
        mine = exchange(mine, "y", second_bits)
        far = exchange(again, "y", second_bits)
        near, mine = lax.optimization_barrier((near, mine))
        left, right = mine[:, :part], mine[:, part:]
        left_more = exchange(left, "x", first_bits)
        right_more = exchange(right, "z", first_bits)
        spot = jnp.arange(tok_rows, dtype=jnp.int32)
        spot = (piece ^ (spot // quarter)) * quarter + spot % quarter
        pick_opposite = (order[:, None] == spot[None, :]).astype(BF16)
        pick_rows = pick.astype(BF16)

    with jax.named_scope("swap_weights"):
        offsets = jnp.stack([b_enc, threshold])
        sib_offsets = swap_cores(offsets)
        sib_enc = stage(swap_cores(w_enc))
        sib_dec = stage(swap_cores(w_dec))

    with jax.named_scope("clamp"):
        table_pick = (
            clamp_index[:, None] == jnp.arange(clamp_table.shape[0], dtype=jnp.int32)[None, :]
        )
        values = jnp.sum(jnp.where(table_pick, clamp_table[None, :], 0.0), axis=1)
        spread = jnp.arange(lats, dtype=jnp.int32)
        here = jnp.concatenate(
            [
                (seq_place * NZ * NX + lat_place) * lats + spread,
                ((seq_place ^ 1) * NZ * NX + lat_place) * lats + spread,
            ]
        )
        match = here[None, :] == clamp_ids[:, None]
        clamped = jnp.any(match, axis=0).astype(F32)
        level = jnp.sum(jnp.where(match, values[:, None], 0.0), axis=0)
        params = jnp.concatenate(
            [
                jnp.concatenate([offsets, sib_offsets], axis=1),
                clamped[None, :],
                level[None, :],
            ],
            axis=0,
        )

    def terms(codes):
        return (
            decode(codes, w_dec, sib_dec, 0, 128),
            decode(codes, w_dec, sib_dec, 1, 32),
        )

    def first_exchange(terms_z, terms_x):
        return exchange(terms_z[1], "z", first_bits), exchange(terms_x[1], "x", first_bits)

    def plane_sums(terms_z, terms_x, received):
        sum_z = add(terms_z[0], received[0])
        sum_x = add(terms_x[0], received[1])
        sum_z = reduce_step(sum_z, "x", first_bits, 32)
        sum_x = reduce_step(sum_x, "z", first_bits, 64)
        return jnp.concatenate([sum_z, sum_x], axis=1)

    with jax.named_scope("early_tokens"):
        early_codes = encode([resid, near], [pick_rows, pick_rows], w_enc, sib_enc, params)
        early_codes, left_more, right_more = lax.optimization_barrier(
            (early_codes, left_more, right_more)
        )
        left = jnp.concatenate([left, left_more])
        right = jnp.concatenate([right, right_more])
        left = jnp.concatenate([left, exchange(left, "z", first_bits)])
        more = exchange(right, "x", first_bits)
        right = jnp.concatenate(
            [right[:quarter], more[:quarter], right[quarter:], more[quarter:]]
        )
        opposite = jnp.concatenate([left, right], axis=1)
        early_terms = terms(early_codes)
        early_received = first_exchange(*early_terms)
        (far, opposite), _ = lax.optimization_barrier(((far, opposite), early_terms))
    with jax.named_scope("late_tokens"):
        late_terms = terms(
            encode([far, opposite], [pick_rows, pick_opposite], w_enc, sib_enc, params)
        )
        late_received = first_exchange(*late_terms)
        (early_received, _) = lax.optimization_barrier((early_received, late_terms))
        early = plane_sums(*early_terms, early_received)
        late = plane_sums(*late_terms, late_received)

    with jax.named_scope("sum_over_chips"):
        quarter = tok_rows // 4
        near_sums = exchange(early[quarter:], "y", first_bits)
        far_sums = exchange(late[:quarter], "y", second_bits)
        opposite_sums = exchange(late[quarter:], "y", lambda core: 2)
        total = early[:quarter].astype(F32) + near_sums.astype(F32)
        total = (total + far_sums.astype(F32) + opposite_sums.astype(F32)).astype(BF16)
        total = add(total, swap_halves(exchange(total, "z", second_bits), 32))
        other = swap_halves(exchange(total, "x", second_bits), 16)
        total = total.astype(F32) + other.astype(F32)
        rest = (total + b_dec).astype(BF16)
        restored = rest[:8]

    with jax.named_scope("gather_restored"):
        rest_z = gather_step(rest[:, :part], "x", first_bits, 16)
        rest_x = gather_step(rest[:, part:], "z", first_bits, 32)
        rest_z = gather_step(rest_z, "z", first_bits, 64)
        rest_x = gather_step(rest_x, "x", first_bits, 16)

    with jax.named_scope("projections"):
        query_ctx = PREFIX + seq_place * tok_rows + order
        freq = THETA ** (-(jnp.arange(head_size // 2, dtype=F32) * 2.0 / head_size))
        angle = query_ctx.astype(F32)[:, None] * freq[None, :]
        cosine, sine = jnp.cos(angle), jnp.sin(angle)
        cosine = jnp.concatenate([cosine, cosine], axis=1)
        sine = jnp.concatenate([-sine, sine], axis=1)
        query, own_pairs = project(
            rest_z,
            rest_x,
            pre_gain[None, :],
            w_query,
            w_key,
            w_value,
            jnp.stack([q_gain, k_gain]),
            cosine,
            sine,
            cache_key,
            cache_value,
        )

    with jax.named_scope("attention"):
        pre_rows = cache_key.shape[0]
        pairs = lax.all_gather(own_pairs, "seq", axis=0, tiled=True)
        orders = jnp.stack([row_order(z, x, jnp.int32(i)) for i in range(NC)])
        shard = jnp.arange(NY * NC, dtype=jnp.int32)
        new_ctx = PREFIX + shard[:, None] * tok_rows + jnp.tile(orders, (NY, 1))
        old_ctx = shard[:, None] * pre_rows + jnp.arange(pre_rows, dtype=jnp.int32)[None, :]
        key_ctx = jnp.concatenate([old_ctx, new_ctx], axis=1).reshape(1, -1)
        first_ctx = jnp.sum(jnp.where(pick, starts[None, :], 0), axis=1)
        keep_z, send_z, keep_x, send_x = attend(
            query, pairs, key_ctx, query_ctx[:, None], first_ctx[:, None], w_out
        )

    with jax.named_scope("sum_over_heads"):
        out_z = add(keep_z, exchange(send_z, "z", first_bits))
        out_x = add(keep_x, exchange(send_x, "x", first_bits))
        out_z = reduce_step(out_z, "x", first_bits, 32)
        out_x = reduce_step(out_x, "z", first_bits, 64)
        both = jnp.concatenate([out_z, out_x], axis=1)
        both = reduce_step(both, "z", second_bits, 32)
        keep, send = split(both, 16)
        mine = keep.astype(F32) + exchange(send, "x", second_bits).astype(F32)
        return (restored.astype(F32) + rms_scale(mine, post_gain)).astype(BF16)


def solution(mesh):
    in_specs = (
        P("seq", None),
        P(None, ("seq", "lat")),
        P(("seq", "lat")),
        P(("seq", "lat")),
        P(("seq", "lat"), None),
        P(),
        P(),
        P(),
        P(),
        P(),
        P(None, "lat"),
        P(None, "lat"),
        P(None, "lat"),
        P(),
        P(),
        P("seq", "lat"),
        P("seq", "lat"),
        P("seq"),
        P("lat", None),
        P(),
    )
    out_specs = P(("seq", "lat"), None)
    return jax.shard_map(
        per_device, mesh=mesh, in_specs=in_specs, out_specs=out_specs, check_vma=False
    )
```

```python
import functools

import jax
import jax.numpy as jnp
from jax import lax
from jax.experimental import pallas as pl
from jax.experimental.pallas import tpu as pltpu
from jax.sharding import PartitionSpec as P

WINDOW = 1024
PREFIX = 512
EPS = 1e-06
THETA = 10000.0
QUERY_SCALE = 168.0 ** (-0.5)

NY, NC, NZ, NX = 4, 2, 4, 4
AXES = ("seq", "lat")
TILE = 896
F32, BF16 = jnp.float32, jnp.bfloat16


def first_bits(core):
    return 1 if core == 0 else 3


def second_bits(core):
    return 3 if core == 0 else 1


def exchange(value, dim, bits):
    pairs = []
    for y in range(NY):
        for c in range(NC):
            for z in range(NZ):
                for x in range(NX):
                    to = {"y": y, "c": c, "z": z, "x": x}
                    for axis in dim:
                        to[axis] ^= bits(c)
                    pairs.append(
                        (
                            (y * NC + c) * NZ * NX + z * NX + x,
                            (to["y"] * NC + to["c"]) * NZ * NX + to["z"] * NX + to["x"],
                        )
                    )
    return lax.ppermute(value, AXES, pairs)


def swap_cores(value):
    return exchange(value, "c", lambda core: 1)


def relative(place, core):
    step = jnp.arange(4, dtype=jnp.int32)
    order0 = jnp.where(step == 1, 3, jnp.where(step == 2, 1, jnp.where(step == 3, 2, 0)))
    order1 = jnp.where(step == 1, 1, jnp.where(step == 2, 3, jnp.where(step == 3, 2, 0)))
    return place ^ jnp.where(core == 0, order0, order1)


def row_order(z, x, core):
    zs, xs = relative(z, core), relative(x, core)
    row = (zs[:, None] * NX + xs[None, :])[:, :, None] * 8 + jnp.arange(8, dtype=jnp.int32)
    return row.reshape(-1)


def rms_scale(values, gain):
    return values * lax.rsqrt(jnp.mean(values * values, axis=-1, keepdims=True) + EPS) * gain


def stage_kernel(source_ref, target_ref, sem):
    copy = pltpu.make_async_copy(source_ref, target_ref, sem)
    copy.start()
    copy.wait()


def stage(value):
    return pl.pallas_call(
        stage_kernel,
        name="stage",
        out_shape=jax.ShapeDtypeStruct(value.shape, value.dtype),
        in_specs=[pl.BlockSpec(memory_space=pl.ANY)],
        out_specs=pl.BlockSpec(memory_space=pltpu.VMEM),
        scratch_shapes=[pltpu.SemaphoreType.DMA],
        compiler_params=pltpu.CompilerParams(vmem_limit_bytes=6 * 1024 * 1024),
        cost_estimate=pl.CostEstimate(flops=0, bytes_accessed=2 * value.size, transcendentals=0),
    )(value)


def encode_kernel(count, *refs):
    blocks = refs[:count]
    picks = refs[count : 2 * count]
    own_ref, sib_ref, params_ref, codes_ref, rows_ref = refs[2 * count :]
    size = blocks[0].shape[0]
    lats = own_ref.shape[1]
    for i in range(count):
        rows_ref[i * size : (i + 1) * size, :] = blocks[i][...]
    for side, weights_ref in enumerate((own_ref, sib_ref)):
        there = slice(side * lats, (side + 1) * lats)
        pre = jnp.dot(rows_ref[...], weights_ref[...], preferred_element_type=F32)
        act = jnp.maximum(pre + params_ref[0:1, there] - params_ref[1:2, there], 0.0)
        codes = jnp.where(params_ref[2:3, there] > 0.0, params_ref[3:4, there], act)
        codes = codes.astype(BF16)
        for i in range(count):
            moved = jnp.dot(
                picks[i][...], codes[i * size : (i + 1) * size], preferred_element_type=F32
            )
            codes_ref[i * size : (i + 1) * size, there] = moved.astype(BF16)


def encode(blocks, picks, own, sib, params):
    count = len(blocks)
    size, width = blocks[0].shape
    lats = own.shape[1]
    return pl.pallas_call(
        functools.partial(encode_kernel, count),
        name="encode",
        out_shape=jax.ShapeDtypeStruct((count * size, 2 * lats), BF16),
        scratch_shapes=[pltpu.VMEM((count * size, width), BF16)],
        compiler_params=pltpu.CompilerParams(vmem_limit_bytes=12 * 1024 * 1024),
        cost_estimate=pl.CostEstimate(
            flops=4 * count * size * width * lats,
            bytes_accessed=4 * width * lats + 2 * count * size * (width + 2 * lats),
            transcendentals=0,
        ),
    )(*blocks, *picks, own, sib, params)


def decode_kernel(part, group, codes_ref, own_ref, sib_ref, keep_ref, send_ref):
    size = codes_ref.shape[0]
    lats, width = own_ref.shape
    half = group // 2
    for tile in range(width // 2 // TILE):
        here = slice(tile * TILE, (tile + 1) * TILE)
        there = slice(part * (width // 2) + tile * TILE, part * (width // 2) + (tile + 1) * TILE)
        total = jnp.dot(codes_ref[:, :lats], own_ref[:, there], preferred_element_type=F32)
        total += jnp.dot(codes_ref[:, lats:], sib_ref[:, there], preferred_element_type=F32)
        total = total.astype(BF16)
        for i in range(size // group):
            keep_ref[i * half : (i + 1) * half, here] = total[i * group : i * group + half, :]
            send_ref[i * half : (i + 1) * half, here] = total[i * group + half : (i + 1) * group, :]


def decode(codes, own, sib, part, group):
    size = codes.shape[0]
    lats, width = own.shape
    out = jax.ShapeDtypeStruct((size // 2, width // 2), BF16)
    return pl.pallas_call(
        functools.partial(decode_kernel, part, group),
        name="decode",
        out_shape=(out, out),
        compiler_params=pltpu.CompilerParams(vmem_limit_bytes=12 * 1024 * 1024),
        cost_estimate=pl.CostEstimate(
            flops=2 * size * lats * width,
            bytes_accessed=2 * (lats * width + 2 * size * lats + size * width // 2),
            transcendentals=0,
        ),
    )(codes, own, sib)


def project_kernel(
    left_ref,
    right_ref,
    gain_ref,
    query_w,
    key_w,
    value_w,
    head_gains,
    cosine_ref,
    sine_ref,
    cache_key,
    cache_value,
    query_ref,
    pairs_ref,
    normed_ref,
):
    part = left_ref.shape[1]
    hd = key_w.shape[1]
    left, right = left_ref[...].astype(F32), right_ref[...].astype(F32)
    square = jnp.sum(left * left, axis=-1, keepdims=True) + jnp.sum(
        right * right, axis=-1, keepdims=True
    )
    scale = lax.rsqrt(square / (2 * part) + EPS)
    normed_ref[:, :part] = (left * scale * gain_ref[0:1, :part]).astype(BF16)
    normed_ref[:, part:] = (right * scale * gain_ref[0:1, part:]).astype(BF16)
    normed = normed_ref[...]

    def turn(values, gain):
        values = rms_scale(values, gain)
        return (
            values * cosine_ref[...] + pltpu.roll(values, hd // 2, axis=1) * sine_ref[...]
        ).astype(BF16)

    old = cache_key.shape[0]
    pairs_ref[:old, :hd] = cache_key[...]
    pairs_ref[:old, hd:] = cache_value[...]
    key = jnp.dot(normed, key_w[...], preferred_element_type=F32)
    pairs_ref[old:, :hd] = turn(key, head_gains[1:2, :])
    value = jnp.dot(normed, value_w[...], preferred_element_type=F32)
    pairs_ref[old:, hd:] = value.astype(BF16)
    query = jnp.dot(normed, query_w[...], preferred_element_type=F32)
    for h in range(query_ref.shape[1] // hd):
        query_ref[:, h * hd : (h + 1) * hd] = turn(
            query[:, h * hd : (h + 1) * hd], head_gains[0:1, :]
        )


def project(left, right, gain, query_w, key_w, value_w, gains, cosine, sine, old_key, old_value):
    rows, hd = left.shape[0], key_w.shape[1]
    width = query_w.shape[0]
    return pl.pallas_call(
        project_kernel,
        name="project",
        out_shape=(
            jax.ShapeDtypeStruct((rows, query_w.shape[1]), BF16),
            jax.ShapeDtypeStruct((old_key.shape[0] + rows, 2 * hd), BF16),
        ),
        scratch_shapes=[pltpu.VMEM((rows, width), BF16)],
        compiler_params=pltpu.CompilerParams(vmem_limit_bytes=12 * 1024 * 1024),
        cost_estimate=pl.CostEstimate(
            flops=8 * rows * width * hd,
            bytes_accessed=8 * width * hd + 2 * rows * width,
            transcendentals=0,
        ),
    )(left, right, gain, query_w, key_w, value_w, gains, cosine, sine, old_key, old_value)


def attend_kernel(
    query_ref,
    pairs_ref,
    key_ctx,
    query_ctx,
    first_ctx,
    out_w,
    keep_z,
    send_z,
    keep_x,
    send_x,
    attended_ref,
):
    rows, hd = query_ref.shape[0], pairs_ref.shape[1] // 2
    allowed = (
        (key_ctx[...] <= query_ctx[...])
        & (key_ctx[...] > query_ctx[...] - WINDOW)
        & (key_ctx[...] >= first_ctx[...])
    )
    for h in range(query_ref.shape[1] // hd):
        scores = (
            lax.dot_general(
                query_ref[:, h * hd : (h + 1) * hd],
                pairs_ref[:, :hd],
                (((1,), (1,)), ((), ())),
                preferred_element_type=F32,
            )
            * QUERY_SCALE
        )
        scores = jnp.where(allowed, scores, -1e30)
        newest = jnp.max(scores, axis=-1, keepdims=True)
        weights = jnp.where(allowed, jnp.exp(scores - newest), 0.0)
        total = jnp.sum(weights, axis=-1, keepdims=True)
        mixed = jnp.dot(weights.astype(BF16), pairs_ref[:, hd:], preferred_element_type=F32)
        attended_ref[:, h * hd : (h + 1) * hd] = (mixed / total).astype(BF16)
    attended = attended_ref[...]
    part = out_w.shape[1] // 2
    for tile in range(part // TILE):
        here = slice(tile * TILE, (tile + 1) * TILE)
        left = jnp.dot(attended, out_w[:, here], preferred_element_type=F32).astype(BF16)
        keep_z[:, here] = left[: rows // 2]
        send_z[:, here] = left[rows // 2 :]
        there = slice(part + tile * TILE, part + (tile + 1) * TILE)
        right = jnp.dot(attended, out_w[:, there], preferred_element_type=F32).astype(BF16)
        for i in range(4):
            keep_x[i * 16 : (i + 1) * 16, here] = right[i * 32 : i * 32 + 16]
            send_x[i * 16 : (i + 1) * 16, here] = right[i * 32 + 16 : i * 32 + 32]


def attend(query, pairs, key_ctx, query_ctx, first_ctx, out_w):
    rows, width = query.shape[0], out_w.shape[1]
    out = jax.ShapeDtypeStruct((rows // 2, width // 2), BF16)
    return pl.pallas_call(
        attend_kernel,
        name="attend",
        out_shape=(out, out, out, out),
        scratch_shapes=[pltpu.VMEM((rows, query.shape[1]), BF16)],
        compiler_params=pltpu.CompilerParams(vmem_limit_bytes=12 * 1024 * 1024),
        cost_estimate=pl.CostEstimate(
            flops=2 * rows * query.shape[1] * (2 * pairs.shape[0] + width),
            bytes_accessed=2 * (query.shape[1] * width + rows * width + pairs.size),
            transcendentals=2 * rows * pairs.shape[0],
        ),
    )(query, pairs, key_ctx, query_ctx, first_ctx, out_w)


def split(value, group):
    rows, width = value.shape
    grouped = value.reshape(rows // group, group, width)
    half = group // 2
    return (
        grouped[:, :half].reshape(rows // 2, width),
        grouped[:, half:].reshape(rows // 2, width),
    )


def add(left, right):
    return (left.astype(F32) + right.astype(F32)).astype(BF16)


def reduce_step(value, dim, bits, group):
    keep, send = split(value, group)
    return add(keep, exchange(send, dim, bits))


def swap_halves(value, group):
    keep, send = split(value, group)
    rows, width = value.shape
    half = group // 2
    return jnp.concatenate(
        [send.reshape(-1, half, width), keep.reshape(-1, half, width)], axis=1
    ).reshape(rows, width)


def gather_step(value, dim, bits, group):
    other = exchange(value, dim, bits)
    rows, width = value.shape
    return jnp.concatenate(
        [value.reshape(-1, group, width), other.reshape(-1, group, width)], axis=1
    ).reshape(2 * rows, width)


def per_device(
    resid,
    w_enc,
    b_enc,
    threshold,
    w_dec,
    b_dec,
    clamp_ids,
    clamp_index,
    clamp_table,
    pre_gain,
    w_query,
    w_key,
    w_value,
    q_gain,
    k_gain,
    cache_key,
    cache_value,
    starts,
    w_out,
    post_gain,
):
    seq_place = lax.axis_index("seq")
    lat_place = lax.axis_index("lat")
    core = seq_place % NC
    z, x = lat_place // NX, lat_place % NX
    tok_rows, width = resid.shape
    part = width // 2
    lats = w_enc.shape[1]
    head_size = q_gain.shape[0]

    order = row_order(z, x, core)
    pick = order[:, None] == jnp.arange(tok_rows, dtype=jnp.int32)[None, :]

    with jax.named_scope("swap_weights"):
        offsets = jnp.stack([b_enc, threshold])
        sib_offsets = swap_cores(offsets)
        sib_enc = stage(swap_cores(w_enc))
        sib_dec = stage(swap_cores(w_dec))

    with jax.named_scope("gather_resid"):
        quarter = tok_rows // 4
        piece = 2 * (z % 2) + x % 2
        near = exchange(resid, "y", first_bits)
        near, sib_enc = lax.optimization_barrier((near, sib_enc))
        mine = lax.dynamic_slice_in_dim(near, piece * quarter, quarter, 0)
        again, mine = lax.optimization_barrier((resid, mine))
        mine = exchange(mine, "y", second_bits)
        far = exchange(again, "y", second_bits)
        near, mine = lax.optimization_barrier((near, mine))
        left, right = mine[:, :part], mine[:, part:]
        left_more = exchange(left, "x", first_bits)
        right_more = exchange(right, "z", first_bits)
        spot = jnp.arange(tok_rows, dtype=jnp.int32)
        spot = (piece ^ (spot // quarter)) * quarter + spot % quarter
        pick_opposite = (order[:, None] == spot[None, :]).astype(BF16)
        pick_rows = pick.astype(BF16)

    with jax.named_scope("clamp"):
        table_pick = (
            clamp_index[:, None] == jnp.arange(clamp_table.shape[0], dtype=jnp.int32)[None, :]
        )
        values = jnp.sum(jnp.where(table_pick, clamp_table[None, :], 0.0), axis=1)
        spread = jnp.arange(lats, dtype=jnp.int32)
        here = jnp.concatenate(
            [
                (seq_place * NZ * NX + lat_place) * lats + spread,
                ((seq_place ^ 1) * NZ * NX + lat_place) * lats + spread,
            ]
        )
        match = here[None, :] == clamp_ids[:, None]
        clamped = jnp.any(match, axis=0).astype(F32)
        level = jnp.sum(jnp.where(match, values[:, None], 0.0), axis=0)
        params = jnp.concatenate(
            [
                jnp.concatenate([offsets, sib_offsets], axis=1),
                clamped[None, :],
                level[None, :],
            ],
            axis=0,
        )

    def terms(codes):
        return (
            decode(codes, w_dec, sib_dec, 0, 128),
            decode(codes, w_dec, sib_dec, 1, 32),
        )

    def first_exchange(terms_z, terms_x):
        return exchange(terms_z[1], "z", first_bits), exchange(terms_x[1], "x", first_bits)

    def halves(terms_z, terms_x, received):
        sum_z = add(terms_z[0], received[0])
        sum_x = add(terms_x[0], received[1])
        return split(sum_z, 32), split(sum_x, 64)

    def second_exchange(halves_z, halves_x):
        return (
            exchange(halves_z[1], "x", first_bits),
            exchange(halves_x[1], "z", first_bits),
        )

    def plane_sums(halves_z, halves_x, received):
        return jnp.concatenate(
            [add(halves_z[0], received[0]), add(halves_x[0], received[1])], axis=1
        )

    with jax.named_scope("early_tokens"):
        early_codes = encode([resid, near], [pick_rows, pick_rows], w_enc, sib_enc, params)
        early_codes, left_more, right_more = lax.optimization_barrier(
            (early_codes, left_more, right_more)
        )
        left = jnp.concatenate([left, left_more])
        right = jnp.concatenate([right, right_more])
        left = jnp.concatenate([left, exchange(left, "z", first_bits)])
        more = exchange(right, "x", first_bits)
        right = jnp.concatenate(
            [right[:quarter], more[:quarter], right[quarter:], more[quarter:]]
        )
        opposite = jnp.concatenate([left, right], axis=1)
        early_terms = terms(early_codes)
        early_received = first_exchange(*early_terms)
        (far, opposite), _ = lax.optimization_barrier(((far, opposite), early_terms))
    with jax.named_scope("late_tokens"):
        late_terms = terms(
            encode([far, opposite], [pick_rows, pick_opposite], w_enc, sib_enc, params)
        )
        late_received = first_exchange(*late_terms)
        (early_received, _) = lax.optimization_barrier((early_received, late_terms))
        early_halves = halves(*early_terms, early_received)
        early_received = second_exchange(*early_halves)
        late_halves = halves(*late_terms, late_received)
        late_received = second_exchange(*late_halves)
        early_received, _ = lax.optimization_barrier((early_received, late_halves))
        early = plane_sums(*early_halves, early_received)
        late = plane_sums(*late_halves, late_received)

    with jax.named_scope("sum_over_chips"):
        quarter = tok_rows // 4
        near_sums = exchange(early[quarter:], "y", first_bits)
        far_sums = exchange(late[:quarter], "y", second_bits)
        opposite_sums = exchange(late[quarter:], "y", lambda core: 2)
        total = early[:quarter].astype(F32) + near_sums.astype(F32)
        total = (total + far_sums.astype(F32) + opposite_sums.astype(F32)).astype(BF16)
        total = add(total, swap_halves(exchange(total, "z", second_bits), 32))
        other = swap_halves(exchange(total, "x", second_bits), 16)
        total = total.astype(F32) + other.astype(F32)
        rest = (total + b_dec).astype(BF16)
        restored = rest[:8]

    with jax.named_scope("gather_restored"):
        rest_z = gather_step(rest[:, :part], "x", first_bits, 16)
        rest_x = gather_step(rest[:, part:], "z", first_bits, 32)
        rest_z = gather_step(rest_z, "z", first_bits, 64)
        rest_x = gather_step(rest_x, "x", first_bits, 16)

    with jax.named_scope("projections"):
        query_ctx = PREFIX + seq_place * tok_rows + order
        freq = THETA ** (-(jnp.arange(head_size // 2, dtype=F32) * 2.0 / head_size))
        angle = query_ctx.astype(F32)[:, None] * freq[None, :]
        cosine, sine = jnp.cos(angle), jnp.sin(angle)
        cosine = jnp.concatenate([cosine, cosine], axis=1)
        sine = jnp.concatenate([-sine, sine], axis=1)
        query, own_pairs = project(
            rest_z,
            rest_x,
            pre_gain[None, :],
            w_query,
            w_key,
            w_value,
            jnp.stack([q_gain, k_gain]),
            cosine,
            sine,
            cache_key,
            cache_value,
        )

    with jax.named_scope("attention"):
        pre_rows = cache_key.shape[0]
        pairs = lax.all_gather(own_pairs, "seq", axis=0, tiled=True)
        orders = jnp.stack([row_order(z, x, jnp.int32(i)) for i in range(NC)])
        shard = jnp.arange(NY * NC, dtype=jnp.int32)
        new_ctx = PREFIX + shard[:, None] * tok_rows + jnp.tile(orders, (NY, 1))
        old_ctx = shard[:, None] * pre_rows + jnp.arange(pre_rows, dtype=jnp.int32)[None, :]
        key_ctx = jnp.concatenate([old_ctx, new_ctx], axis=1).reshape(1, -1)
        first_ctx = jnp.sum(jnp.where(pick, starts[None, :], 0), axis=1)
        keep_z, send_z, keep_x, send_x = attend(
            query, pairs, key_ctx, query_ctx[:, None], first_ctx[:, None], w_out
        )

    with jax.named_scope("sum_over_heads"):
        out_z = add(keep_z, exchange(send_z, "z", first_bits))
        out_x = add(keep_x, exchange(send_x, "x", first_bits))
        out_z = reduce_step(out_z, "x", first_bits, 32)
        out_x = reduce_step(out_x, "z", first_bits, 64)
        both = jnp.concatenate([out_z, out_x], axis=1)
        mine = both[:8].astype(F32)
        for place, axes in enumerate(("x", "z", "zx")):
            rows = both[8 * place + 8 : 8 * place + 16]
            mine = mine + exchange(rows, axes, second_bits).astype(F32)
        return (restored.astype(F32) + rms_scale(mine, post_gain)).astype(BF16)


def solution(mesh):
    in_specs = (
        P("seq", None),
        P(None, ("seq", "lat")),
        P(("seq", "lat")),
        P(("seq", "lat")),
        P(("seq", "lat"), None),
        P(),
        P(),
        P(),
        P(),
        P(),
        P(None, "lat"),
        P(None, "lat"),
        P(None, "lat"),
        P(),
        P(),
        P("seq", "lat"),
        P("seq", "lat"),
        P("seq"),
        P("lat", None),
        P(),
    )
    out_specs = P(("seq", "lat"), None)
    return jax.shard_map(
        per_device, mesh=mesh, in_specs=in_specs, out_specs=out_specs, check_vma=False
    )
```

```python
import functools

import jax
import jax.numpy as jnp
from jax import lax
from jax.experimental import pallas as pl
from jax.experimental.pallas import tpu as pltpu
from jax.sharding import PartitionSpec as P

WINDOW = 1024
PREFIX = 512
EPS = 1e-06
THETA = 10000.0
QUERY_SCALE = 168.0 ** (-0.5)

NY, NC, NZ, NX = 4, 2, 4, 4
AXES = ("seq", "lat")
TILE = 896
F32, BF16 = jnp.float32, jnp.bfloat16


def first_bits(core):
    return 1 if core == 0 else 3


def second_bits(core):
    return 3 if core == 0 else 1


def exchange(value, dim, bits):
    pairs = []
    for y in range(NY):
        for c in range(NC):
            for z in range(NZ):
                for x in range(NX):
                    to = {"y": y, "c": c, "z": z, "x": x}
                    for axis in dim:
                        to[axis] ^= bits(c)
                    pairs.append(
                        (
                            (y * NC + c) * NZ * NX + z * NX + x,
                            (to["y"] * NC + to["c"]) * NZ * NX + to["z"] * NX + to["x"],
                        )
                    )
    return lax.ppermute(value, AXES, pairs)


def swap_cores(value):
    return exchange(value, "c", lambda core: 1)


def relative(place, core):
    step = jnp.arange(4, dtype=jnp.int32)
    order0 = jnp.where(step == 1, 3, jnp.where(step == 2, 1, jnp.where(step == 3, 2, 0)))
    order1 = jnp.where(step == 1, 1, jnp.where(step == 2, 3, jnp.where(step == 3, 2, 0)))
    return place ^ jnp.where(core == 0, order0, order1)


def row_order(z, x, core):
    zs, xs = relative(z, core), relative(x, core)
    row = (zs[:, None] * NX + xs[None, :])[:, :, None] * 8 + jnp.arange(8, dtype=jnp.int32)
    return row.reshape(-1)


def rms_scale(values, gain):
    return values * lax.rsqrt(jnp.mean(values * values, axis=-1, keepdims=True) + EPS) * gain


def stage_kernel(source_ref, target_ref, sem):
    copy = pltpu.make_async_copy(source_ref, target_ref, sem)
    copy.start()
    copy.wait()


def stage(value):
    return pl.pallas_call(
        stage_kernel,
        name="stage",
        out_shape=jax.ShapeDtypeStruct(value.shape, value.dtype),
        in_specs=[pl.BlockSpec(memory_space=pl.ANY)],
        out_specs=pl.BlockSpec(memory_space=pltpu.VMEM),
        scratch_shapes=[pltpu.SemaphoreType.DMA],
        compiler_params=pltpu.CompilerParams(vmem_limit_bytes=6 * 1024 * 1024),
        cost_estimate=pl.CostEstimate(flops=0, bytes_accessed=2 * value.size, transcendentals=0),
    )(value)


def encode_kernel(count, *refs):
    blocks = refs[:count]
    picks = refs[count : 2 * count]
    own_ref, sib_ref, params_ref, codes_ref, rows_ref = refs[2 * count :]
    size = blocks[0].shape[0]
    lats = own_ref.shape[1]
    for i in range(count):
        rows_ref[i * size : (i + 1) * size, :] = blocks[i][...]
    for side, weights_ref in enumerate((own_ref, sib_ref)):
        there = slice(side * lats, (side + 1) * lats)
        pre = jnp.dot(rows_ref[...], weights_ref[...], preferred_element_type=F32)
        act = jnp.maximum(pre + params_ref[0:1, there] - params_ref[1:2, there], 0.0)
        codes = jnp.where(params_ref[2:3, there] > 0.0, params_ref[3:4, there], act)
        codes = codes.astype(BF16)
        for i in range(count):
            moved = jnp.dot(
                picks[i][...], codes[i * size : (i + 1) * size], preferred_element_type=F32
            )
            codes_ref[i * size : (i + 1) * size, there] = moved.astype(BF16)


def encode(blocks, picks, own, sib, params):
    count = len(blocks)
    size, width = blocks[0].shape
    lats = own.shape[1]
    return pl.pallas_call(
        functools.partial(encode_kernel, count),
        name="encode",
        out_shape=jax.ShapeDtypeStruct((count * size, 2 * lats), BF16),
        scratch_shapes=[pltpu.VMEM((count * size, width), BF16)],
        compiler_params=pltpu.CompilerParams(vmem_limit_bytes=12 * 1024 * 1024),
        cost_estimate=pl.CostEstimate(
            flops=4 * count * size * width * lats,
            bytes_accessed=4 * width * lats + 2 * count * size * (width + 2 * lats),
            transcendentals=0,
        ),
    )(*blocks, *picks, own, sib, params)


def decode_kernel(part, group, codes_ref, own_ref, sib_ref, keep_ref, send_ref):
    size = codes_ref.shape[0]
    lats, width = own_ref.shape
    half = group // 2
    for tile in range(width // 2 // TILE):
        here = slice(tile * TILE, (tile + 1) * TILE)
        there = slice(part * (width // 2) + tile * TILE, part * (width // 2) + (tile + 1) * TILE)
        total = jnp.dot(codes_ref[:, :lats], own_ref[:, there], preferred_element_type=F32)
        total += jnp.dot(codes_ref[:, lats:], sib_ref[:, there], preferred_element_type=F32)
        total = total.astype(BF16)
        for i in range(size // group):
            keep_ref[i * half : (i + 1) * half, here] = total[i * group : i * group + half, :]
            send_ref[i * half : (i + 1) * half, here] = total[i * group + half : (i + 1) * group, :]


def decode(codes, own, sib, part, group):
    size = codes.shape[0]
    lats, width = own.shape
    out = jax.ShapeDtypeStruct((size // 2, width // 2), BF16)
    return pl.pallas_call(
        functools.partial(decode_kernel, part, group),
        name="decode",
        out_shape=(out, out),
        compiler_params=pltpu.CompilerParams(vmem_limit_bytes=12 * 1024 * 1024),
        cost_estimate=pl.CostEstimate(
            flops=2 * size * lats * width,
            bytes_accessed=2 * (lats * width + 2 * size * lats + size * width // 2),
            transcendentals=0,
        ),
    )(codes, own, sib)


def project_kernel(
    left_ref,
    right_ref,
    gain_ref,
    query_w,
    key_w,
    value_w,
    head_gains,
    cosine_ref,
    sine_ref,
    cache_key,
    cache_value,
    query_ref,
    pairs_ref,
    normed_ref,
):
    part = left_ref.shape[1]
    hd = key_w.shape[1]
    left, right = left_ref[...].astype(F32), right_ref[...].astype(F32)
    square = jnp.sum(left * left, axis=-1, keepdims=True) + jnp.sum(
        right * right, axis=-1, keepdims=True
    )
    scale = lax.rsqrt(square / (2 * part) + EPS)
    normed_ref[:, :part] = (left * scale * gain_ref[0:1, :part]).astype(BF16)
    normed_ref[:, part:] = (right * scale * gain_ref[0:1, part:]).astype(BF16)
    normed = normed_ref[...]

    def turn(values, gain):
        values = rms_scale(values, gain)
        return (
            values * cosine_ref[...] + pltpu.roll(values, hd // 2, axis=1) * sine_ref[...]
        ).astype(BF16)

    old = cache_key.shape[0]
    pairs_ref[:old, :hd] = cache_key[...]
    pairs_ref[:old, hd:] = cache_value[...]
    key = jnp.dot(normed, key_w[...], preferred_element_type=F32)
    pairs_ref[old:, :hd] = turn(key, head_gains[1:2, :])
    value = jnp.dot(normed, value_w[...], preferred_element_type=F32)
    pairs_ref[old:, hd:] = value.astype(BF16)
    query = jnp.dot(normed, query_w[...], preferred_element_type=F32)
    for h in range(query_ref.shape[1] // hd):
        query_ref[:, h * hd : (h + 1) * hd] = turn(
            query[:, h * hd : (h + 1) * hd], head_gains[0:1, :]
        )


def project(left, right, gain, query_w, key_w, value_w, gains, cosine, sine, old_key, old_value):
    rows, hd = left.shape[0], key_w.shape[1]
    width = query_w.shape[0]
    return pl.pallas_call(
        project_kernel,
        name="project",
        out_shape=(
            jax.ShapeDtypeStruct((rows, query_w.shape[1]), BF16),
            jax.ShapeDtypeStruct((old_key.shape[0] + rows, 2 * hd), BF16),
        ),
        scratch_shapes=[pltpu.VMEM((rows, width), BF16)],
        compiler_params=pltpu.CompilerParams(vmem_limit_bytes=12 * 1024 * 1024),
        cost_estimate=pl.CostEstimate(
            flops=8 * rows * width * hd,
            bytes_accessed=8 * width * hd + 2 * rows * width,
            transcendentals=0,
        ),
    )(left, right, gain, query_w, key_w, value_w, gains, cosine, sine, old_key, old_value)


def attend_kernel(
    query_ref,
    own_ref,
    sib_ref,
    key_ctx,
    query_ctx,
    first_ctx,
    out_w,
    keep_z,
    send_z,
    keep_x,
    send_x,
    attended_ref,
    pairs_ref,
):
    rows, hd = query_ref.shape[0], pairs_ref.shape[1] // 2
    pairs_ref[: own_ref.shape[0], :] = own_ref[...]
    pairs_ref[own_ref.shape[0] :, :] = sib_ref[...]
    allowed = (
        (key_ctx[...] <= query_ctx[...])
        & (key_ctx[...] > query_ctx[...] - WINDOW)
        & (key_ctx[...] >= first_ctx[...])
    )
    for h in range(query_ref.shape[1] // hd):
        scores = (
            lax.dot_general(
                query_ref[:, h * hd : (h + 1) * hd],
                pairs_ref[:, :hd],
                (((1,), (1,)), ((), ())),
                preferred_element_type=F32,
            )
            * QUERY_SCALE
        )
        scores = jnp.where(allowed, scores, -1e30)
        newest = jnp.max(scores, axis=-1, keepdims=True)
        weights = jnp.where(allowed, jnp.exp(scores - newest), 0.0)
        total = jnp.sum(weights, axis=-1, keepdims=True)
        mixed = jnp.dot(weights.astype(BF16), pairs_ref[:, hd:], preferred_element_type=F32)
        attended_ref[:, h * hd : (h + 1) * hd] = (mixed / total).astype(BF16)
    attended = attended_ref[...]
    part = out_w.shape[1] // 2
    for tile in range(part // TILE):
        here = slice(tile * TILE, (tile + 1) * TILE)
        left = jnp.dot(attended, out_w[:, here], preferred_element_type=F32).astype(BF16)
        keep_z[:, here] = left[: rows // 2]
        send_z[:, here] = left[rows // 2 :]
        there = slice(part + tile * TILE, part + (tile + 1) * TILE)
        right = jnp.dot(attended, out_w[:, there], preferred_element_type=F32).astype(BF16)
        for i in range(4):
            keep_x[i * 16 : (i + 1) * 16, here] = right[i * 32 : i * 32 + 16]
            send_x[i * 16 : (i + 1) * 16, here] = right[i * 32 + 16 : i * 32 + 32]


def attend(query, own, sib, key_ctx, query_ctx, first_ctx, out_w):
    rows, width = query.shape[0], out_w.shape[1]
    out = jax.ShapeDtypeStruct((rows // 2, width // 2), BF16)
    return pl.pallas_call(
        attend_kernel,
        name="attend",
        out_shape=(out, out, out, out),
        scratch_shapes=[
            pltpu.VMEM((rows, query.shape[1]), BF16),
            pltpu.VMEM((2 * own.shape[0], own.shape[1]), BF16),
        ],
        compiler_params=pltpu.CompilerParams(vmem_limit_bytes=12 * 1024 * 1024),
        cost_estimate=pl.CostEstimate(
            flops=2 * rows * query.shape[1] * (4 * own.shape[0] + width),
            bytes_accessed=2 * (query.shape[1] * width + rows * width + 2 * own.size),
            transcendentals=4 * rows * own.shape[0],
        ),
    )(query, own, sib, key_ctx, query_ctx, first_ctx, out_w)


def split(value, group):
    rows, width = value.shape
    grouped = value.reshape(rows // group, group, width)
    half = group // 2
    return (
        grouped[:, :half].reshape(rows // 2, width),
        grouped[:, half:].reshape(rows // 2, width),
    )


def add(left, right):
    return (left.astype(F32) + right.astype(F32)).astype(BF16)


def reduce_step(value, dim, bits, group):
    keep, send = split(value, group)
    return add(keep, exchange(send, dim, bits))


def swap_halves(value, group):
    keep, send = split(value, group)
    rows, width = value.shape
    half = group // 2
    return jnp.concatenate(
        [send.reshape(-1, half, width), keep.reshape(-1, half, width)], axis=1
    ).reshape(rows, width)


def gather_step(value, dim, bits, group):
    other = exchange(value, dim, bits)
    rows, width = value.shape
    return jnp.concatenate(
        [value.reshape(-1, group, width), other.reshape(-1, group, width)], axis=1
    ).reshape(2 * rows, width)


def per_device(
    resid,
    w_enc,
    b_enc,
    threshold,
    w_dec,
    b_dec,
    clamp_ids,
    clamp_index,
    clamp_table,
    pre_gain,
    w_query,
    w_key,
    w_value,
    q_gain,
    k_gain,
    cache_key,
    cache_value,
    starts,
    w_out,
    post_gain,
):
    seq_place = lax.axis_index("seq")
    lat_place = lax.axis_index("lat")
    core = seq_place % NC
    z, x = lat_place // NX, lat_place % NX
    tok_rows, width = resid.shape
    part = width // 2
    lats = w_enc.shape[1]
    head_size = q_gain.shape[0]

    order = row_order(z, x, core)
    pick = order[:, None] == jnp.arange(tok_rows, dtype=jnp.int32)[None, :]

    with jax.named_scope("swap_weights"):
        offsets = jnp.stack([b_enc, threshold])
        sib_offsets = swap_cores(offsets)
        sib_enc = stage(swap_cores(w_enc))
        sib_dec = stage(swap_cores(w_dec))

    with jax.named_scope("gather_resid"):
        quarter = tok_rows // 4
        piece = 2 * (z % 2) + x % 2
        near = exchange(resid, "y", first_bits)
        near, sib_enc = lax.optimization_barrier((near, sib_enc))
        mine = lax.dynamic_slice_in_dim(near, piece * quarter, quarter, 0)
        again, mine = lax.optimization_barrier((resid, mine))
        mine = exchange(mine, "y", second_bits)
        far = exchange(again, "y", second_bits)
        near, mine = lax.optimization_barrier((near, mine))
        left, right = mine[:, :part], mine[:, part:]
        left_more = exchange(left, "x", first_bits)
        right_more = exchange(right, "z", first_bits)
        spot = jnp.arange(tok_rows, dtype=jnp.int32)
        spot = (piece ^ (spot // quarter)) * quarter + spot % quarter
        pick_opposite = (order[:, None] == spot[None, :]).astype(BF16)
        pick_rows = pick.astype(BF16)

    with jax.named_scope("clamp"):
        table_pick = (
            clamp_index[:, None] == jnp.arange(clamp_table.shape[0], dtype=jnp.int32)[None, :]
        )
        values = jnp.sum(jnp.where(table_pick, clamp_table[None, :], 0.0), axis=1)
        spread = jnp.arange(lats, dtype=jnp.int32)
        here = jnp.concatenate(
            [
                (seq_place * NZ * NX + lat_place) * lats + spread,
                ((seq_place ^ 1) * NZ * NX + lat_place) * lats + spread,
            ]
        )
        match = here[None, :] == clamp_ids[:, None]
        clamped = jnp.any(match, axis=0).astype(F32)
        level = jnp.sum(jnp.where(match, values[:, None], 0.0), axis=0)
        params = jnp.concatenate(
            [
                jnp.concatenate([offsets, sib_offsets], axis=1),
                clamped[None, :],
                level[None, :],
            ],
            axis=0,
        )

    def terms(codes):
        return (
            decode(codes, w_dec, sib_dec, 0, 128),
            decode(codes, w_dec, sib_dec, 1, 32),
        )

    def first_exchange(terms_z, terms_x):
        return exchange(terms_z[1], "z", first_bits), exchange(terms_x[1], "x", first_bits)

    def halves(terms_z, terms_x, received):
        sum_z = add(terms_z[0], received[0])
        sum_x = add(terms_x[0], received[1])
        return split(sum_z, 32), split(sum_x, 64)

    def second_exchange(halves_z, halves_x):
        return (
            exchange(halves_z[1], "x", first_bits),
            exchange(halves_x[1], "z", first_bits),
        )

    def plane_sums(halves_z, halves_x, received):
        return jnp.concatenate(
            [add(halves_z[0], received[0]), add(halves_x[0], received[1])], axis=1
        )

    with jax.named_scope("early_tokens"):
        early_codes = encode([resid, near], [pick_rows, pick_rows], w_enc, sib_enc, params)
        early_codes, left_more, right_more = lax.optimization_barrier(
            (early_codes, left_more, right_more)
        )
        left = jnp.concatenate([left, left_more])
        right = jnp.concatenate([right, right_more])
        left = jnp.concatenate([left, exchange(left, "z", first_bits)])
        more = exchange(right, "x", first_bits)
        right = jnp.concatenate(
            [right[:quarter], more[:quarter], right[quarter:], more[quarter:]]
        )
        opposite = jnp.concatenate([left, right], axis=1)
        early_terms = terms(early_codes)
        early_received = first_exchange(*early_terms)
        (far, opposite), _ = lax.optimization_barrier(((far, opposite), early_terms))
    with jax.named_scope("late_tokens"):
        late_terms = terms(
            encode([far, opposite], [pick_rows, pick_opposite], w_enc, sib_enc, params)
        )
        late_received = first_exchange(*late_terms)
        (early_received, _) = lax.optimization_barrier((early_received, late_terms))
        early_halves = halves(*early_terms, early_received)
        early_received = second_exchange(*early_halves)
        late_halves = halves(*late_terms, late_received)
        late_received = second_exchange(*late_halves)
        early_received, _ = lax.optimization_barrier((early_received, late_halves[0]))
        early = plane_sums(*early_halves, early_received)
        late = plane_sums(*late_halves, late_received)

    with jax.named_scope("sum_over_chips"):
        quarter = tok_rows // 4
        near_sums = exchange(early[quarter:], "y", first_bits)
        far_sums = exchange(late[:quarter], "y", second_bits)
        opposite_sums = exchange(late[quarter:], "y", lambda core: 2)
        total = early[:quarter].astype(F32) + near_sums.astype(F32)
        total = (total + far_sums.astype(F32) + opposite_sums.astype(F32)).astype(BF16)
        total = add(total, swap_halves(exchange(total, "z", second_bits), 32))
        other = swap_halves(exchange(total, "x", second_bits), 16)
        total = total.astype(F32) + other.astype(F32)
        rest = (total + b_dec).astype(BF16)
        restored = rest[:8]

    with jax.named_scope("gather_restored"):
        rest_z = gather_step(rest[:, :part], "x", first_bits, 16)
        rest_x = gather_step(rest[:, part:], "z", first_bits, 32)
        rest_z = gather_step(rest_z, "z", first_bits, 64)
        rest_x = gather_step(rest_x, "x", first_bits, 16)

    with jax.named_scope("projections"):
        query_ctx = PREFIX + seq_place * tok_rows + order
        freq = THETA ** (-(jnp.arange(head_size // 2, dtype=F32) * 2.0 / head_size))
        angle = query_ctx.astype(F32)[:, None] * freq[None, :]
        cosine, sine = jnp.cos(angle), jnp.sin(angle)
        cosine = jnp.concatenate([cosine, cosine], axis=1)
        sine = jnp.concatenate([-sine, sine], axis=1)
        query, own_pairs = project(
            rest_z,
            rest_x,
            pre_gain[None, :],
            w_query,
            w_key,
            w_value,
            jnp.stack([q_gain, k_gain]),
            cosine,
            sine,
            cache_key,
            cache_value,
        )

    with jax.named_scope("attention"):
        pre_rows = cache_key.shape[0]
        pairs = jnp.concatenate(
            [
                own_pairs,
                exchange(own_pairs, "y", first_bits),
                exchange(own_pairs, "y", second_bits),
                exchange(own_pairs, "y", lambda place: 2),
            ]
        )
        sib_pairs = swap_cores(pairs)
        y = seq_place // NC
        key_ctx = []
        for side in (core, 1 - core):
            first = jnp.where(side == 0, 1, 3)
            shard = jnp.stack([y, y ^ first, y ^ first ^ 2, y ^ 2]) * NC + side
            old_ctx = shard[:, None] * pre_rows + jnp.arange(pre_rows, dtype=jnp.int32)[None, :]
            new_ctx = PREFIX + shard[:, None] * tok_rows + row_order(z, x, side)[None, :]
            key_ctx.append(jnp.concatenate([old_ctx, new_ctx], axis=1).reshape(-1))
        key_ctx = jnp.concatenate(key_ctx).reshape(1, -1)
        first_ctx = jnp.sum(jnp.where(pick, starts[None, :], 0), axis=1)
        keep_z, send_z, keep_x, send_x = attend(
            query, pairs, sib_pairs, key_ctx, query_ctx[:, None], first_ctx[:, None], w_out
        )

    with jax.named_scope("sum_over_heads"):
        out_z = add(keep_z, exchange(send_z, "z", first_bits))
        out_x = add(keep_x, exchange(send_x, "x", first_bits))
        out_z = reduce_step(out_z, "x", first_bits, 32)
        out_x = reduce_step(out_x, "z", first_bits, 64)
        both = jnp.concatenate([out_z, out_x], axis=1)
        mine = both[:8].astype(F32)
        for place, axes in enumerate(("x", "z", "zx")):
            rows = both[8 * place + 8 : 8 * place + 16]
            mine = mine + exchange(rows, axes, second_bits).astype(F32)
        return (restored.astype(F32) + rms_scale(mine, post_gain)).astype(BF16)


def solution(mesh):
    in_specs = (
        P("seq", None),
        P(None, ("seq", "lat")),
        P(("seq", "lat")),
        P(("seq", "lat")),
        P(("seq", "lat"), None),
        P(),
        P(),
        P(),
        P(),
        P(),
        P(None, "lat"),
        P(None, "lat"),
        P(None, "lat"),
        P(),
        P(),
        P("seq", "lat"),
        P("seq", "lat"),
        P("seq"),
        P("lat", None),
        P(),
    )
    out_specs = P(("seq", "lat"), None)
    return jax.shard_map(
        per_device, mesh=mesh, in_specs=in_specs, out_specs=out_specs, check_vma=False
    )
```

```python
import functools

import jax
import jax.numpy as jnp
from jax import lax
from jax.experimental import pallas as pl
from jax.experimental.pallas import tpu as pltpu
from jax.sharding import PartitionSpec as P

WINDOW = 1024
PREFIX = 512
EPS = 1e-06
THETA = 10000.0
QUERY_SCALE = 168.0 ** (-0.5)

NY, NC, NZ, NX = 4, 2, 4, 4
AXES = ("seq", "lat")
TILE = 896
F32, BF16 = jnp.float32, jnp.bfloat16


def first_bits(core):
    return 1 if core == 0 else 3


def second_bits(core):
    return 3 if core == 0 else 1


def exchange(value, dim, bits):
    pairs = []
    for y in range(NY):
        for c in range(NC):
            for z in range(NZ):
                for x in range(NX):
                    to = {"y": y, "c": c, "z": z, "x": x}
                    for axis in dim:
                        to[axis] ^= bits(c)
                    pairs.append(
                        (
                            (y * NC + c) * NZ * NX + z * NX + x,
                            (to["y"] * NC + to["c"]) * NZ * NX + to["z"] * NX + to["x"],
                        )
                    )
    return lax.ppermute(value, AXES, pairs)


def swap_cores(value):
    return exchange(value, "c", lambda core: 1)


def relative(place, core):
    step = jnp.arange(4, dtype=jnp.int32)
    order0 = jnp.where(step == 1, 3, jnp.where(step == 2, 1, jnp.where(step == 3, 2, 0)))
    order1 = jnp.where(step == 1, 1, jnp.where(step == 2, 3, jnp.where(step == 3, 2, 0)))
    return place ^ jnp.where(core == 0, order0, order1)


def row_order(z, x, core):
    zs, xs = relative(z, core), relative(x, core)
    row = (zs[:, None] * NX + xs[None, :])[:, :, None] * 8 + jnp.arange(8, dtype=jnp.int32)
    return row.reshape(-1)


def key_positions(y, core, z, x, old_rows, new_rows):
    block = old_rows + new_rows
    spot = lax.broadcasted_iota(jnp.int32, (1, NC * NY * block), 1)
    side = core ^ (spot // (NY * block))
    first = jnp.where(side == 0, 1, 3)

    def near(index, one, two):
        return jnp.where(index == 0, 0, jnp.where(index == 1, one, jnp.where(index == 2, two, 2)))

    shard = (y ^ near(spot // block % NY, first, first ^ 2)) * NC + side
    within = spot % block
    fresh = within - old_rows
    at_z = z ^ near(fresh // 32, first ^ 2, first)
    at_x = x ^ near(fresh // 8 % 4, first ^ 2, first)
    new = PREFIX + shard * new_rows + (at_z * NX + at_x) * 8 + fresh % 8
    return jnp.where(within < old_rows, shard * old_rows + within, new)


def rms_scale(values, gain):
    return values * lax.rsqrt(jnp.mean(values * values, axis=-1, keepdims=True) + EPS) * gain


def stage_kernel(source_ref, target_ref, sem):
    copy = pltpu.make_async_copy(source_ref, target_ref, sem)
    copy.start()
    copy.wait()


def stage(value):
    return pl.pallas_call(
        stage_kernel,
        name="stage",
        out_shape=jax.ShapeDtypeStruct(value.shape, value.dtype),
        in_specs=[pl.BlockSpec(memory_space=pl.ANY)],
        out_specs=pl.BlockSpec(memory_space=pltpu.VMEM),
        scratch_shapes=[pltpu.SemaphoreType.DMA],
        compiler_params=pltpu.CompilerParams(vmem_limit_bytes=6 * 1024 * 1024),
        cost_estimate=pl.CostEstimate(flops=0, bytes_accessed=2 * value.size, transcendentals=0),
    )(value)


def encode_kernel(count, *refs):
    blocks = refs[:count]
    picks = refs[count : 2 * count]
    own_ref, sib_ref, params_ref, codes_ref, rows_ref = refs[2 * count :]
    size = blocks[0].shape[0]
    lats = own_ref.shape[1]
    for i in range(count):
        rows_ref[i * size : (i + 1) * size, :] = blocks[i][...]
    for side, weights_ref in enumerate((own_ref, sib_ref)):
        there = slice(side * lats, (side + 1) * lats)
        pre = jnp.dot(rows_ref[...], weights_ref[...], preferred_element_type=F32)
        act = jnp.maximum(pre + params_ref[0:1, there] - params_ref[1:2, there], 0.0)
        codes = jnp.where(params_ref[2:3, there] > 0.0, params_ref[3:4, there], act)
        codes = codes.astype(BF16)
        for i in range(count):
            moved = jnp.dot(
                picks[i][...], codes[i * size : (i + 1) * size], preferred_element_type=F32
            )
            codes_ref[i * size : (i + 1) * size, there] = moved.astype(BF16)


def encode(blocks, picks, own, sib, params):
    count = len(blocks)
    size, width = blocks[0].shape
    lats = own.shape[1]
    return pl.pallas_call(
        functools.partial(encode_kernel, count),
        name="encode",
        out_shape=jax.ShapeDtypeStruct((count * size, 2 * lats), BF16),
        scratch_shapes=[pltpu.VMEM((count * size, width), BF16)],
        compiler_params=pltpu.CompilerParams(vmem_limit_bytes=12 * 1024 * 1024),
        cost_estimate=pl.CostEstimate(
            flops=4 * count * size * width * lats,
            bytes_accessed=4 * width * lats + 2 * count * size * (width + 2 * lats),
            transcendentals=0,
        ),
    )(*blocks, *picks, own, sib, params)


def decode_kernel(part, group, codes_ref, own_ref, sib_ref, keep_ref, send_ref):
    size = codes_ref.shape[0]
    lats, width = own_ref.shape
    half = group // 2
    for tile in range(width // 2 // TILE):
        here = slice(tile * TILE, (tile + 1) * TILE)
        there = slice(part * (width // 2) + tile * TILE, part * (width // 2) + (tile + 1) * TILE)
        total = jnp.dot(codes_ref[:, :lats], own_ref[:, there], preferred_element_type=F32)
        total += jnp.dot(codes_ref[:, lats:], sib_ref[:, there], preferred_element_type=F32)
        total = total.astype(BF16)
        for i in range(size // group):
            keep_ref[i * half : (i + 1) * half, here] = total[i * group : i * group + half, :]
            send_ref[i * half : (i + 1) * half, here] = total[i * group + half : (i + 1) * group, :]


def decode(codes, own, sib, part, group):
    size = codes.shape[0]
    lats, width = own.shape
    out = jax.ShapeDtypeStruct((size // 2, width // 2), BF16)
    return pl.pallas_call(
        functools.partial(decode_kernel, part, group),
        name="decode",
        out_shape=(out, out),
        compiler_params=pltpu.CompilerParams(vmem_limit_bytes=12 * 1024 * 1024),
        cost_estimate=pl.CostEstimate(
            flops=2 * size * lats * width,
            bytes_accessed=2 * (lats * width + 2 * size * lats + size * width // 2),
            transcendentals=0,
        ),
    )(codes, own, sib)


def project_kernel(
    left_ref,
    right_ref,
    gain_ref,
    query_w,
    key_w,
    value_w,
    head_gains,
    cosine_ref,
    sine_ref,
    cache_key,
    cache_value,
    query_ref,
    pairs_ref,
    normed_ref,
):
    part = left_ref.shape[1]
    hd = key_w.shape[1]
    left, right = left_ref[...].astype(F32), right_ref[...].astype(F32)
    square = jnp.sum(left * left, axis=-1, keepdims=True) + jnp.sum(
        right * right, axis=-1, keepdims=True
    )
    scale = lax.rsqrt(square / (2 * part) + EPS)
    normed_ref[:, :part] = (left * scale * gain_ref[0:1, :part]).astype(BF16)
    normed_ref[:, part:] = (right * scale * gain_ref[0:1, part:]).astype(BF16)
    normed = normed_ref[...]

    def turn(values, gain):
        values = rms_scale(values, gain)
        return (
            values * cosine_ref[...] + pltpu.roll(values, hd // 2, axis=1) * sine_ref[...]
        ).astype(BF16)

    old = cache_key.shape[0]
    pairs_ref[:old, :hd] = cache_key[...]
    pairs_ref[:old, hd:] = cache_value[...]
    key = jnp.dot(normed, key_w[...], preferred_element_type=F32)
    pairs_ref[old:, :hd] = turn(key, head_gains[1:2, :])
    value = jnp.dot(normed, value_w[...], preferred_element_type=F32)
    pairs_ref[old:, hd:] = value.astype(BF16)
    query = jnp.dot(normed, query_w[...], preferred_element_type=F32)
    for h in range(query_ref.shape[1] // hd):
        query_ref[:, h * hd : (h + 1) * hd] = turn(
            query[:, h * hd : (h + 1) * hd], head_gains[0:1, :]
        )


def project(left, right, gain, query_w, key_w, value_w, gains, cosine, sine, old_key, old_value):
    rows, hd = left.shape[0], key_w.shape[1]
    width = query_w.shape[0]
    return pl.pallas_call(
        project_kernel,
        name="project",
        out_shape=(
            jax.ShapeDtypeStruct((rows, query_w.shape[1]), BF16),
            jax.ShapeDtypeStruct((old_key.shape[0] + rows, 2 * hd), BF16),
        ),
        scratch_shapes=[pltpu.VMEM((rows, width), BF16)],
        compiler_params=pltpu.CompilerParams(vmem_limit_bytes=12 * 1024 * 1024),
        cost_estimate=pl.CostEstimate(
            flops=8 * rows * width * hd,
            bytes_accessed=8 * width * hd + 2 * rows * width,
            transcendentals=0,
        ),
    )(left, right, gain, query_w, key_w, value_w, gains, cosine, sine, old_key, old_value)


def attend_kernel(
    query_ref,
    own_ref,
    sib_ref,
    key_ctx,
    query_ctx,
    first_ctx,
    out_w,
    keep_z,
    send_z,
    keep_x,
    send_x,
    attended_ref,
    pairs_ref,
):
    rows, hd = query_ref.shape[0], pairs_ref.shape[1] // 2
    pairs_ref[: own_ref.shape[0], :] = own_ref[...]
    pairs_ref[own_ref.shape[0] :, :] = sib_ref[...]
    allowed = (
        (key_ctx[...] <= query_ctx[:, 0:1])
        & (key_ctx[...] > query_ctx[:, 0:1] - WINDOW)
        & (key_ctx[...] >= first_ctx[:, 0:1])
    )
    for h in range(query_ref.shape[1] // hd):
        scores = (
            lax.dot_general(
                query_ref[:, h * hd : (h + 1) * hd],
                pairs_ref[:, :hd],
                (((1,), (1,)), ((), ())),
                preferred_element_type=F32,
            )
            * QUERY_SCALE
        )
        scores = jnp.where(allowed, scores, -1e30)
        newest = jnp.max(scores, axis=-1, keepdims=True)
        weights = jnp.where(allowed, jnp.exp(scores - newest), 0.0)
        total = jnp.sum(weights, axis=-1, keepdims=True)
        mixed = jnp.dot(weights.astype(BF16), pairs_ref[:, hd:], preferred_element_type=F32)
        attended_ref[:, h * hd : (h + 1) * hd] = (mixed / total).astype(BF16)
    attended = attended_ref[...]
    part = out_w.shape[1] // 2
    for tile in range(part // TILE):
        here = slice(tile * TILE, (tile + 1) * TILE)
        left = jnp.dot(attended, out_w[:, here], preferred_element_type=F32).astype(BF16)
        keep_z[:, here] = left[: rows // 2]
        send_z[:, here] = left[rows // 2 :]
        there = slice(part + tile * TILE, part + (tile + 1) * TILE)
        right = jnp.dot(attended, out_w[:, there], preferred_element_type=F32).astype(BF16)
        for i in range(4):
            keep_x[i * 16 : (i + 1) * 16, here] = right[i * 32 : i * 32 + 16]
            send_x[i * 16 : (i + 1) * 16, here] = right[i * 32 + 16 : i * 32 + 32]


def attend(query, own, sib, key_ctx, query_ctx, first_ctx, out_w):
    rows, width = query.shape[0], out_w.shape[1]
    out = jax.ShapeDtypeStruct((rows // 2, width // 2), BF16)
    return pl.pallas_call(
        attend_kernel,
        name="attend",
        out_shape=(out, out, out, out),
        scratch_shapes=[
            pltpu.VMEM((rows, query.shape[1]), BF16),
            pltpu.VMEM((2 * own.shape[0], own.shape[1]), BF16),
        ],
        compiler_params=pltpu.CompilerParams(vmem_limit_bytes=12 * 1024 * 1024),
        cost_estimate=pl.CostEstimate(
            flops=2 * rows * query.shape[1] * (4 * own.shape[0] + width),
            bytes_accessed=2 * (query.shape[1] * width + rows * width + 2 * own.size),
            transcendentals=4 * rows * own.shape[0],
        ),
    )(query, own, sib, key_ctx, query_ctx, first_ctx, out_w)


def split(value, group):
    rows, width = value.shape
    grouped = value.reshape(rows // group, group, width)
    half = group // 2
    return (
        grouped[:, :half].reshape(rows // 2, width),
        grouped[:, half:].reshape(rows // 2, width),
    )


def add(left, right):
    return (left.astype(F32) + right.astype(F32)).astype(BF16)


def reduce_step(value, dim, bits, group):
    keep, send = split(value, group)
    return add(keep, exchange(send, dim, bits))


def swap_halves(value, group):
    keep, send = split(value, group)
    rows, width = value.shape
    half = group // 2
    return jnp.concatenate(
        [send.reshape(-1, half, width), keep.reshape(-1, half, width)], axis=1
    ).reshape(rows, width)


def gather_step(value, dim, bits, group):
    other = exchange(value, dim, bits)
    rows, width = value.shape
    return jnp.concatenate(
        [value.reshape(-1, group, width), other.reshape(-1, group, width)], axis=1
    ).reshape(2 * rows, width)


def per_device(
    resid,
    w_enc,
    b_enc,
    threshold,
    w_dec,
    b_dec,
    clamp_ids,
    clamp_index,
    clamp_table,
    pre_gain,
    w_query,
    w_key,
    w_value,
    q_gain,
    k_gain,
    cache_key,
    cache_value,
    starts,
    w_out,
    post_gain,
):
    seq_place = lax.axis_index("seq")
    lat_place = lax.axis_index("lat")
    core = seq_place % NC
    z, x = lat_place // NX, lat_place % NX
    tok_rows, width = resid.shape
    part = width // 2
    lats = w_enc.shape[1]
    head_size = q_gain.shape[0]

    order = row_order(z, x, core)
    pick = order[:, None] == jnp.arange(tok_rows, dtype=jnp.int32)[None, :]

    with jax.named_scope("swap_weights"):
        offsets = jnp.stack([b_enc, threshold])
        sib_offsets = swap_cores(offsets)
        sib_enc = stage(swap_cores(w_enc))
        sib_dec = stage(swap_cores(w_dec))

    with jax.named_scope("gather_resid"):
        quarter = tok_rows // 4
        piece = 2 * (z % 2) + x % 2
        near = exchange(resid, "y", first_bits)
        query_ctx = PREFIX + seq_place * tok_rows + order
        query_col = jnp.broadcast_to(query_ctx[:, None], (tok_rows, tok_rows))
        first_col = jnp.broadcast_to(
            jnp.sum(jnp.where(pick, starts[None, :], 0), axis=1, keepdims=True),
            (tok_rows, tok_rows),
        )
        key_ctx = key_positions(seq_place // NC, core, z, x, cache_key.shape[0], tok_rows)
        near, sib_enc, query_col, first_col, key_ctx = lax.optimization_barrier(
            (near, sib_enc, query_col, first_col, key_ctx)
        )
        mine = lax.dynamic_slice_in_dim(near, piece * quarter, quarter, 0)
        again, mine = lax.optimization_barrier((resid, mine))
        mine = exchange(mine, "y", second_bits)
        far = exchange(again, "y", second_bits)
        near, mine = lax.optimization_barrier((near, mine))
        left, right = mine[:, :part], mine[:, part:]
        left_more = exchange(left, "x", first_bits)
        right_more = exchange(right, "z", first_bits)
        spot = jnp.arange(tok_rows, dtype=jnp.int32)
        spot = (piece ^ (spot // quarter)) * quarter + spot % quarter
        pick_opposite = (order[:, None] == spot[None, :]).astype(BF16)
        pick_rows = pick.astype(BF16)

    with jax.named_scope("clamp"):
        table_pick = (
            clamp_index[:, None] == jnp.arange(clamp_table.shape[0], dtype=jnp.int32)[None, :]
        )
        values = jnp.sum(jnp.where(table_pick, clamp_table[None, :], 0.0), axis=1)
        spread = jnp.arange(lats, dtype=jnp.int32)
        here = jnp.concatenate(
            [
                (seq_place * NZ * NX + lat_place) * lats + spread,
                ((seq_place ^ 1) * NZ * NX + lat_place) * lats + spread,
            ]
        )
        match = here[None, :] == clamp_ids[:, None]
        clamped = jnp.any(match, axis=0).astype(F32)
        level = jnp.sum(jnp.where(match, values[:, None], 0.0), axis=0)
        params = jnp.concatenate(
            [
                jnp.concatenate([offsets, sib_offsets], axis=1),
                clamped[None, :],
                level[None, :],
            ],
            axis=0,
        )

    def terms(codes):
        return (
            decode(codes, w_dec, sib_dec, 0, 128),
            decode(codes, w_dec, sib_dec, 1, 32),
        )

    def first_exchange(terms_z, terms_x):
        return exchange(terms_z[1], "z", first_bits), exchange(terms_x[1], "x", first_bits)

    def halves(terms_z, terms_x, received):
        sum_z = add(terms_z[0], received[0])
        sum_x = add(terms_x[0], received[1])
        return split(sum_z, 32), split(sum_x, 64)

    def second_exchange(halves_z, halves_x):
        return (
            exchange(halves_z[1], "x", first_bits),
            exchange(halves_x[1], "z", first_bits),
        )

    def plane_sums(halves_z, halves_x, received):
        return jnp.concatenate(
            [add(halves_z[0], received[0]), add(halves_x[0], received[1])], axis=1
        )

    with jax.named_scope("early_tokens"):
        early_codes = encode([resid, near], [pick_rows, pick_rows], w_enc, sib_enc, params)
        early_codes, left_more, right_more = lax.optimization_barrier(
            (early_codes, left_more, right_more)
        )
        left = jnp.concatenate([left, left_more])
        right = jnp.concatenate([right, right_more])
        left = jnp.concatenate([left, exchange(left, "z", first_bits)])
        more = exchange(right, "x", first_bits)
        right = jnp.concatenate(
            [right[:quarter], more[:quarter], right[quarter:], more[quarter:]]
        )
        opposite = jnp.concatenate([left, right], axis=1)
        early_terms = terms(early_codes)
        early_received = first_exchange(*early_terms)
        (far, opposite), _ = lax.optimization_barrier(((far, opposite), early_terms))
    with jax.named_scope("late_tokens"):
        late_terms = terms(
            encode([far, opposite], [pick_rows, pick_opposite], w_enc, sib_enc, params)
        )
        late_received = first_exchange(*late_terms)
        (early_received, _) = lax.optimization_barrier((early_received, late_terms))
        early_halves = halves(*early_terms, early_received)
        early_received = second_exchange(*early_halves)
        late_halves = halves(*late_terms, late_received)
        late_received = second_exchange(*late_halves)
        early_received, _ = lax.optimization_barrier((early_received, late_halves))
        early = plane_sums(*early_halves, early_received)
        late = plane_sums(*late_halves, late_received)

    with jax.named_scope("sum_over_chips"):
        quarter = tok_rows // 4
        near_sums = exchange(early[quarter:], "y", first_bits)
        far_sums = exchange(late[:quarter], "y", second_bits)
        opposite_sums = exchange(late[quarter:], "y", lambda core: 2)
        total = early[:quarter].astype(F32) + near_sums.astype(F32)
        total = (total + far_sums.astype(F32) + opposite_sums.astype(F32)).astype(BF16)
        total = add(total, swap_halves(exchange(total, "z", second_bits), 32))
        other = swap_halves(exchange(total, "x", second_bits), 16)
        total = total.astype(F32) + other.astype(F32)
        rest = (total + b_dec).astype(BF16)
        restored = rest[:8]

    with jax.named_scope("gather_restored"):
        rest_z = gather_step(rest[:, :part], "x", first_bits, 16)
        rest_x = gather_step(rest[:, part:], "z", first_bits, 32)
        rest_z = gather_step(rest_z, "z", first_bits, 64)
        rest_x = gather_step(rest_x, "x", first_bits, 16)

    with jax.named_scope("projections"):
        freq = THETA ** (-(jnp.arange(head_size // 2, dtype=F32) * 2.0 / head_size))
        angle = query_ctx.astype(F32)[:, None] * freq[None, :]
        cosine, sine = jnp.cos(angle), jnp.sin(angle)
        cosine = jnp.concatenate([cosine, cosine], axis=1)
        sine = jnp.concatenate([-sine, sine], axis=1)
        query, own_pairs = project(
            rest_z,
            rest_x,
            pre_gain[None, :],
            w_query,
            w_key,
            w_value,
            jnp.stack([q_gain, k_gain]),
            cosine,
            sine,
            cache_key,
            cache_value,
        )

    with jax.named_scope("attention"):
        pairs = jnp.concatenate(
            [
                own_pairs,
                exchange(own_pairs, "y", first_bits),
                exchange(own_pairs, "y", second_bits),
                exchange(own_pairs, "y", lambda place: 2),
            ]
        )
        sib_pairs = swap_cores(pairs)
        keep_z, send_z, keep_x, send_x = attend(
            query, pairs, sib_pairs, key_ctx, query_col, first_col, w_out
        )

    with jax.named_scope("sum_over_heads"):
        out_z = add(keep_z, exchange(send_z, "z", first_bits))
        out_x = add(keep_x, exchange(send_x, "x", first_bits))
        out_z = reduce_step(out_z, "x", first_bits, 32)
        out_x = reduce_step(out_x, "z", first_bits, 64)
        both = jnp.concatenate([out_z, out_x], axis=1)
        mine = both[:8].astype(F32)
        for place, axes in enumerate(("x", "z", "zx")):
            rows = both[8 * place + 8 : 8 * place + 16]
            mine = mine + exchange(rows, axes, second_bits).astype(F32)
        return (restored.astype(F32) + rms_scale(mine, post_gain)).astype(BF16)


def solution(mesh):
    in_specs = (
        P("seq", None),
        P(None, ("seq", "lat")),
        P(("seq", "lat")),
        P(("seq", "lat")),
        P(("seq", "lat"), None),
        P(),
        P(),
        P(),
        P(),
        P(),
        P(None, "lat"),
        P(None, "lat"),
        P(None, "lat"),
        P(),
        P(),
        P("seq", "lat"),
        P("seq", "lat"),
        P("seq"),
        P("lat", None),
        P(),
    )
    out_specs = P(("seq", "lat"), None)
    return jax.shard_map(
        per_device, mesh=mesh, in_specs=in_specs, out_specs=out_specs, check_vma=False
    )
```

```python
import functools

import jax
import jax.numpy as jnp
from jax import lax
from jax.experimental import pallas as pl
from jax.experimental.pallas import tpu as pltpu
from jax.sharding import PartitionSpec as P

WINDOW = 1024
PREFIX = 512
EPS = 1e-06
THETA = 10000.0
QUERY_SCALE = 168.0 ** (-0.5)

NY, NC, NZ, NX = 4, 2, 4, 4
AXES = ("seq", "lat")
TILE = 896
F32, BF16 = jnp.float32, jnp.bfloat16


def first_bits(core):
    return 1 if core == 0 else 3


def second_bits(core):
    return 3 if core == 0 else 1


def exchange(value, dim, bits):
    pairs = []
    for y in range(NY):
        for c in range(NC):
            for z in range(NZ):
                for x in range(NX):
                    to = {"y": y, "c": c, "z": z, "x": x}
                    for axis in dim:
                        to[axis] ^= bits(c)
                    pairs.append(
                        (
                            (y * NC + c) * NZ * NX + z * NX + x,
                            (to["y"] * NC + to["c"]) * NZ * NX + to["z"] * NX + to["x"],
                        )
                    )
    return lax.ppermute(value, AXES, pairs)


def swap_cores(value):
    return exchange(value, "c", lambda core: 1)


def relative(place, core):
    step = jnp.arange(4, dtype=jnp.int32)
    order0 = jnp.where(step == 1, 3, jnp.where(step == 2, 1, jnp.where(step == 3, 2, 0)))
    order1 = jnp.where(step == 1, 1, jnp.where(step == 2, 3, jnp.where(step == 3, 2, 0)))
    return place ^ jnp.where(core == 0, order0, order1)


def row_order(z, x, core):
    zs, xs = relative(z, core), relative(x, core)
    row = (zs[:, None] * NX + xs[None, :])[:, :, None] * 8 + jnp.arange(8, dtype=jnp.int32)
    return row.reshape(-1)


def key_positions(y, core, z, x, old_rows, new_rows):
    block = old_rows + new_rows
    spot = lax.broadcasted_iota(jnp.int32, (1, NC * NY * block), 1)
    side = core ^ (spot // (NY * block))
    first = jnp.where(side == 0, 1, 3)

    def near(index, one, two):
        return jnp.where(index == 0, 0, jnp.where(index == 1, one, jnp.where(index == 2, two, 2)))

    shard = (y ^ near(spot // block % NY, first, first ^ 2)) * NC + side
    within = spot % block
    fresh = within - old_rows
    at_z = z ^ near(fresh // 32, first ^ 2, first)
    at_x = x ^ near(fresh // 8 % 4, first ^ 2, first)
    new = PREFIX + shard * new_rows + (at_z * NX + at_x) * 8 + fresh % 8
    return jnp.where(within < old_rows, shard * old_rows + within, new)


def rms_scale(values, gain):
    return values * lax.rsqrt(jnp.mean(values * values, axis=-1, keepdims=True) + EPS) * gain


def stage_kernel(source_ref, target_ref, sem):
    copy = pltpu.make_async_copy(source_ref, target_ref, sem)
    copy.start()
    copy.wait()


def stage(value):
    return pl.pallas_call(
        stage_kernel,
        name="stage",
        out_shape=jax.ShapeDtypeStruct(value.shape, value.dtype),
        in_specs=[pl.BlockSpec(memory_space=pl.ANY)],
        out_specs=pl.BlockSpec(memory_space=pltpu.VMEM),
        scratch_shapes=[pltpu.SemaphoreType.DMA],
        compiler_params=pltpu.CompilerParams(vmem_limit_bytes=6 * 1024 * 1024),
        cost_estimate=pl.CostEstimate(flops=0, bytes_accessed=2 * value.size, transcendentals=0),
    )(value)


def encode_kernel(count, *refs):
    blocks = refs[:count]
    picks = refs[count : 2 * count]
    own_ref, sib_ref, params_ref, codes_ref, rows_ref = refs[2 * count :]
    size = blocks[0].shape[0]
    lats = own_ref.shape[1]
    for i in range(count):
        rows_ref[i * size : (i + 1) * size, :] = blocks[i][...]
    for side, weights_ref in enumerate((own_ref, sib_ref)):
        there = slice(side * lats, (side + 1) * lats)
        pre = jnp.dot(rows_ref[...], weights_ref[...], preferred_element_type=F32)
        act = jnp.maximum(pre + params_ref[0:1, there] - params_ref[1:2, there], 0.0)
        codes = jnp.where(params_ref[2:3, there] > 0.0, params_ref[3:4, there], act)
        codes = codes.astype(BF16)
        for i in range(count):
            moved = jnp.dot(
                picks[i][...], codes[i * size : (i + 1) * size], preferred_element_type=F32
            )
            codes_ref[i * size : (i + 1) * size, there] = moved.astype(BF16)


def encode(blocks, picks, own, sib, params):
    count = len(blocks)
    size, width = blocks[0].shape
    lats = own.shape[1]
    return pl.pallas_call(
        functools.partial(encode_kernel, count),
        name="encode",
        out_shape=jax.ShapeDtypeStruct((count * size, 2 * lats), BF16),
        scratch_shapes=[pltpu.VMEM((count * size, width), BF16)],
        compiler_params=pltpu.CompilerParams(vmem_limit_bytes=12 * 1024 * 1024),
        cost_estimate=pl.CostEstimate(
            flops=4 * count * size * width * lats,
            bytes_accessed=4 * width * lats + 2 * count * size * (width + 2 * lats),
            transcendentals=0,
        ),
    )(*blocks, *picks, own, sib, params)


def decode_kernel(part, group, codes_ref, own_ref, sib_ref, keep_ref, send_ref):
    size = codes_ref.shape[0]
    lats, width = own_ref.shape
    half = group // 2
    for tile in range(width // 2 // TILE):
        here = slice(tile * TILE, (tile + 1) * TILE)
        there = slice(part * (width // 2) + tile * TILE, part * (width // 2) + (tile + 1) * TILE)
        total = jnp.dot(codes_ref[:, :lats], own_ref[:, there], preferred_element_type=F32)
        total += jnp.dot(codes_ref[:, lats:], sib_ref[:, there], preferred_element_type=F32)
        total = total.astype(BF16)
        for i in range(size // group):
            keep_ref[i * half : (i + 1) * half, here] = total[i * group : i * group + half, :]
            send_ref[i * half : (i + 1) * half, here] = total[i * group + half : (i + 1) * group, :]


def decode(codes, own, sib, part, group):
    size = codes.shape[0]
    lats, width = own.shape
    out = jax.ShapeDtypeStruct((size // 2, width // 2), BF16)
    return pl.pallas_call(
        functools.partial(decode_kernel, part, group),
        name="decode",
        out_shape=(out, out),
        compiler_params=pltpu.CompilerParams(vmem_limit_bytes=12 * 1024 * 1024),
        cost_estimate=pl.CostEstimate(
            flops=2 * size * lats * width,
            bytes_accessed=2 * (lats * width + 2 * size * lats + size * width // 2),
            transcendentals=0,
        ),
    )(codes, own, sib)


def project_kernel(
    left_ref,
    right_ref,
    gain_ref,
    query_w,
    key_w,
    value_w,
    head_gains,
    cosine_ref,
    sine_ref,
    cache_key,
    cache_value,
    query_ref,
    pairs_ref,
    normed_ref,
):
    part = left_ref.shape[1]
    hd = key_w.shape[1]
    left, right = left_ref[...].astype(F32), right_ref[...].astype(F32)
    square = jnp.sum(left * left, axis=-1, keepdims=True) + jnp.sum(
        right * right, axis=-1, keepdims=True
    )
    scale = lax.rsqrt(square / (2 * part) + EPS)
    normed_ref[:, :part] = (left * scale * gain_ref[0:1, :part]).astype(BF16)
    normed_ref[:, part:] = (right * scale * gain_ref[0:1, part:]).astype(BF16)
    normed = normed_ref[...]

    def turn(values, gain):
        values = rms_scale(values, gain)
        return (
            values * cosine_ref[...] + pltpu.roll(values, hd // 2, axis=1) * sine_ref[...]
        ).astype(BF16)

    old = cache_key.shape[0]
    pairs_ref[:old, :hd] = cache_key[...]
    pairs_ref[:old, hd:] = cache_value[...]
    key = jnp.dot(normed, key_w[...], preferred_element_type=F32)
    pairs_ref[old:, :hd] = turn(key, head_gains[1:2, :])
    value = jnp.dot(normed, value_w[...], preferred_element_type=F32)
    pairs_ref[old:, hd:] = value.astype(BF16)
    query = jnp.dot(normed, query_w[...], preferred_element_type=F32)
    for h in range(query_ref.shape[1] // hd):
        query_ref[:, h * hd : (h + 1) * hd] = turn(
            query[:, h * hd : (h + 1) * hd], head_gains[0:1, :]
        )


def project(left, right, gain, query_w, key_w, value_w, gains, cosine, sine, old_key, old_value):
    rows, hd = left.shape[0], key_w.shape[1]
    width = query_w.shape[0]
    return pl.pallas_call(
        project_kernel,
        name="project",
        out_shape=(
            jax.ShapeDtypeStruct((rows, query_w.shape[1]), BF16),
            jax.ShapeDtypeStruct((old_key.shape[0] + rows, 2 * hd), BF16),
        ),
        scratch_shapes=[pltpu.VMEM((rows, width), BF16)],
        compiler_params=pltpu.CompilerParams(vmem_limit_bytes=12 * 1024 * 1024),
        cost_estimate=pl.CostEstimate(
            flops=8 * rows * width * hd,
            bytes_accessed=8 * width * hd + 2 * rows * width,
            transcendentals=0,
        ),
    )(left, right, gain, query_w, key_w, value_w, gains, cosine, sine, old_key, old_value)


def attend_kernel(
    query_ref,
    own_ref,
    sib_ref,
    key_ctx,
    query_ctx,
    first_ctx,
    out_w,
    keep_z,
    send_z,
    keep_x,
    send_x,
    attended_ref,
    pairs_ref,
):
    rows, hd = query_ref.shape[0], pairs_ref.shape[1] // 2
    pairs_ref[: own_ref.shape[0], :] = own_ref[...]
    pairs_ref[own_ref.shape[0] :, :] = sib_ref[...]
    allowed = (
        (key_ctx[...] <= query_ctx[:, 0:1])
        & (key_ctx[...] > query_ctx[:, 0:1] - WINDOW)
        & (key_ctx[...] >= first_ctx[:, 0:1])
    )
    for h in range(query_ref.shape[1] // hd):
        scores = (
            lax.dot_general(
                query_ref[:, h * hd : (h + 1) * hd],
                pairs_ref[:, :hd],
                (((1,), (1,)), ((), ())),
                preferred_element_type=F32,
            )
            * QUERY_SCALE
        )
        scores = jnp.where(allowed, scores, -1e30)
        newest = jnp.max(scores, axis=-1, keepdims=True)
        weights = jnp.where(allowed, jnp.exp(scores - newest), 0.0)
        total = jnp.sum(weights, axis=-1, keepdims=True)
        mixed = jnp.dot(weights.astype(BF16), pairs_ref[:, hd:], preferred_element_type=F32)
        attended_ref[:, h * hd : (h + 1) * hd] = (mixed / total).astype(BF16)
    attended = attended_ref[...]
    part = out_w.shape[1] // 2
    for tile in range(part // TILE):
        here = slice(tile * TILE, (tile + 1) * TILE)
        left = jnp.dot(attended, out_w[:, here], preferred_element_type=F32).astype(BF16)
        keep_z[:, here] = left[: rows // 2]
        send_z[:, here] = left[rows // 2 :]
        there = slice(part + tile * TILE, part + (tile + 1) * TILE)
        right = jnp.dot(attended, out_w[:, there], preferred_element_type=F32).astype(BF16)
        for i in range(4):
            keep_x[i * 16 : (i + 1) * 16, here] = right[i * 32 : i * 32 + 16]
            send_x[i * 16 : (i + 1) * 16, here] = right[i * 32 + 16 : i * 32 + 32]


def attend(query, own, sib, key_ctx, query_ctx, first_ctx, out_w):
    rows, width = query.shape[0], out_w.shape[1]
    out = jax.ShapeDtypeStruct((rows // 2, width // 2), BF16)
    return pl.pallas_call(
        attend_kernel,
        name="attend",
        out_shape=(out, out, out, out),
        scratch_shapes=[
            pltpu.VMEM((rows, query.shape[1]), BF16),
            pltpu.VMEM((2 * own.shape[0], own.shape[1]), BF16),
        ],
        compiler_params=pltpu.CompilerParams(vmem_limit_bytes=12 * 1024 * 1024),
        cost_estimate=pl.CostEstimate(
            flops=2 * rows * query.shape[1] * (4 * own.shape[0] + width),
            bytes_accessed=2 * (query.shape[1] * width + rows * width + 2 * own.size),
            transcendentals=4 * rows * own.shape[0],
        ),
    )(query, own, sib, key_ctx, query_ctx, first_ctx, out_w)


def split(value, group):
    rows, width = value.shape
    grouped = value.reshape(rows // group, group, width)
    half = group // 2
    return (
        grouped[:, :half].reshape(rows // 2, width),
        grouped[:, half:].reshape(rows // 2, width),
    )


def add(left, right):
    return (left.astype(F32) + right.astype(F32)).astype(BF16)


def reduce_step(value, dim, bits, group):
    keep, send = split(value, group)
    return add(keep, exchange(send, dim, bits))


def swap_halves(value, group):
    keep, send = split(value, group)
    rows, width = value.shape
    half = group // 2
    return jnp.concatenate(
        [send.reshape(-1, half, width), keep.reshape(-1, half, width)], axis=1
    ).reshape(rows, width)


def gather_step(value, dim, bits, group):
    other = exchange(value, dim, bits)
    rows, width = value.shape
    return jnp.concatenate(
        [value.reshape(-1, group, width), other.reshape(-1, group, width)], axis=1
    ).reshape(2 * rows, width)


def per_device(
    resid,
    w_enc,
    b_enc,
    threshold,
    w_dec,
    b_dec,
    clamp_ids,
    clamp_index,
    clamp_table,
    pre_gain,
    w_query,
    w_key,
    w_value,
    q_gain,
    k_gain,
    cache_key,
    cache_value,
    starts,
    w_out,
    post_gain,
):
    seq_place = lax.axis_index("seq")
    lat_place = lax.axis_index("lat")
    core = seq_place % NC
    z, x = lat_place // NX, lat_place % NX
    tok_rows, width = resid.shape
    part = width // 2
    lats = w_enc.shape[1]
    head_size = q_gain.shape[0]

    order = row_order(z, x, core)
    pick = order[:, None] == jnp.arange(tok_rows, dtype=jnp.int32)[None, :]

    with jax.named_scope("swap_weights"):
        offsets = jnp.stack([b_enc, threshold])
        sib_offsets = swap_cores(offsets)
        sib_enc = stage(swap_cores(w_enc))
        sib_dec = stage(swap_cores(w_dec))

    with jax.named_scope("gather_resid"):
        quarter = tok_rows // 4
        piece = 2 * (z % 2) + x % 2
        parts = [
            lax.dynamic_slice_in_dim(resid, (piece ^ step) * quarter, quarter, 0)
            for step in range(4)
        ]
        near_first = exchange(parts[0], "y", first_bits)
        rest, sib_offsets = lax.optimization_barrier((jnp.concatenate(parts[1:]), sib_offsets))
        near_rest = exchange(rest, "y", first_bits)
        mine = exchange(near_first, "y", second_bits)
        query_ctx = PREFIX + seq_place * tok_rows + order
        query_col = jnp.broadcast_to(query_ctx[:, None], (tok_rows, tok_rows))
        first_col = jnp.broadcast_to(
            jnp.sum(jnp.where(pick, starts[None, :], 0), axis=1, keepdims=True),
            (tok_rows, tok_rows),
        )
        key_ctx = key_positions(seq_place // NC, core, z, x, cache_key.shape[0], tok_rows)
        near_rest, sib_enc, query_col, first_col, key_ctx = lax.optimization_barrier(
            (near_rest, sib_enc, query_col, first_col, key_ctx)
        )
        again, near_rest = lax.optimization_barrier((resid, near_rest))
        far = exchange(again, "y", second_bits)
        near = jnp.concatenate([near_first, near_rest])
        mine, near = lax.optimization_barrier((mine, near))
        left, right = mine[:, :part], mine[:, part:]
        left = jnp.concatenate([left, exchange(left, "x", first_bits)])
        right = jnp.concatenate([right, exchange(right, "z", first_bits)])
        left = jnp.concatenate([left, exchange(left, "z", first_bits)])
        more = exchange(right, "x", first_bits)
        right = jnp.concatenate(
            [right[:quarter], more[:quarter], right[quarter:], more[quarter:]]
        )
        opposite = jnp.concatenate([left, right], axis=1)
        spot = jnp.arange(tok_rows, dtype=jnp.int32)
        spot = (piece ^ (spot // quarter)) * quarter + spot % quarter
        pick_opposite = (order[:, None] == spot[None, :]).astype(BF16)
        pick_rows = pick.astype(BF16)

    with jax.named_scope("clamp"):
        table_pick = (
            clamp_index[:, None] == jnp.arange(clamp_table.shape[0], dtype=jnp.int32)[None, :]
        )
        values = jnp.sum(jnp.where(table_pick, clamp_table[None, :], 0.0), axis=1)
        spread = jnp.arange(lats, dtype=jnp.int32)
        here = jnp.concatenate(
            [
                (seq_place * NZ * NX + lat_place) * lats + spread,
                ((seq_place ^ 1) * NZ * NX + lat_place) * lats + spread,
            ]
        )
        match = here[None, :] == clamp_ids[:, None]
        clamped = jnp.any(match, axis=0).astype(F32)
        level = jnp.sum(jnp.where(match, values[:, None], 0.0), axis=0)
        params = jnp.concatenate(
            [
                jnp.concatenate([offsets, sib_offsets], axis=1),
                clamped[None, :],
                level[None, :],
            ],
            axis=0,
        )

    def terms(codes):
        return (
            decode(codes, w_dec, sib_dec, 0, 128),
            decode(codes, w_dec, sib_dec, 1, 32),
        )

    def first_exchange(terms_z, terms_x):
        return exchange(terms_z[1], "z", first_bits), exchange(terms_x[1], "x", first_bits)

    def halves(terms_z, terms_x, received):
        sum_z = add(terms_z[0], received[0])
        sum_x = add(terms_x[0], received[1])
        return split(sum_z, 32), split(sum_x, 64)

    def second_exchange(halves_z, halves_x):
        return (
            exchange(halves_z[1], "x", first_bits),
            exchange(halves_x[1], "z", first_bits),
        )

    def plane_sums(halves_z, halves_x, received):
        return jnp.concatenate(
            [add(halves_z[0], received[0]), add(halves_x[0], received[1])], axis=1
        )

    with jax.named_scope("early_tokens"):
        early_codes = encode(
            [near, opposite], [pick_opposite, pick_opposite], w_enc, sib_enc, params
        )
        early_terms = terms(early_codes)
        early_received = first_exchange(*early_terms)
        far, _ = lax.optimization_barrier((far, early_terms))
    with jax.named_scope("late_tokens"):
        late_terms = terms(
            encode([resid, far], [pick_rows, pick_rows], w_enc, sib_enc, params)
        )
        late_received = first_exchange(*late_terms)
        (early_received, _) = lax.optimization_barrier((early_received, late_terms))
        early_halves = halves(*early_terms, early_received)
        early_received = second_exchange(*early_halves)
        late_halves = halves(*late_terms, late_received)
        late_received = second_exchange(*late_halves)
        early_received, _ = lax.optimization_barrier((early_received, late_halves))
        early = plane_sums(*early_halves, early_received)
        late = plane_sums(*late_halves, late_received)

    with jax.named_scope("sum_over_chips"):
        total = add(late, exchange(early, "y", first_bits))
        total = add(total[:quarter], exchange(total[quarter:], "y", second_bits))
        total = add(total, swap_halves(exchange(total, "z", second_bits), 32))
        other = swap_halves(exchange(total, "x", second_bits), 16)
        total = total.astype(F32) + other.astype(F32)
        rest = (total + b_dec).astype(BF16)
        restored = rest[:8]

    with jax.named_scope("gather_restored"):
        rest_z = gather_step(rest[:, :part], "x", first_bits, 16)
        rest_x = gather_step(rest[:, part:], "z", first_bits, 32)
        rest_z = gather_step(rest_z, "z", first_bits, 64)
        rest_x = gather_step(rest_x, "x", first_bits, 16)

    with jax.named_scope("projections"):
        freq = THETA ** (-(jnp.arange(head_size // 2, dtype=F32) * 2.0 / head_size))
        angle = query_ctx.astype(F32)[:, None] * freq[None, :]
        cosine, sine = jnp.cos(angle), jnp.sin(angle)
        cosine = jnp.concatenate([cosine, cosine], axis=1)
        sine = jnp.concatenate([-sine, sine], axis=1)
        query, own_pairs = project(
            rest_z,
            rest_x,
            pre_gain[None, :],
            w_query,
            w_key,
            w_value,
            jnp.stack([q_gain, k_gain]),
            cosine,
            sine,
            cache_key,
            cache_value,
        )

    with jax.named_scope("attention"):
        pairs = jnp.concatenate(
            [
                own_pairs,
                exchange(own_pairs, "y", first_bits),
                exchange(own_pairs, "y", second_bits),
                exchange(own_pairs, "y", lambda place: 2),
            ]
        )
        sib_pairs = swap_cores(pairs)
        keep_z, send_z, keep_x, send_x = attend(
            query, pairs, sib_pairs, key_ctx, query_col, first_col, w_out
        )

    with jax.named_scope("sum_over_heads"):
        out_z = add(keep_z, exchange(send_z, "z", first_bits))
        out_x = add(keep_x, exchange(send_x, "x", first_bits))
        out_z = reduce_step(out_z, "x", first_bits, 32)
        out_x = reduce_step(out_x, "z", first_bits, 64)
        both = jnp.concatenate([out_z, out_x], axis=1)
        mine = both[:8].astype(F32)
        for place, axes in enumerate(("x", "z", "zx")):
            rows = both[8 * place + 8 : 8 * place + 16]
            mine = mine + exchange(rows, axes, second_bits).astype(F32)
        return (restored.astype(F32) + rms_scale(mine, post_gain)).astype(BF16)


def solution(mesh):
    in_specs = (
        P("seq", None),
        P(None, ("seq", "lat")),
        P(("seq", "lat")),
        P(("seq", "lat")),
        P(("seq", "lat"), None),
        P(),
        P(),
        P(),
        P(),
        P(),
        P(None, "lat"),
        P(None, "lat"),
        P(None, "lat"),
        P(),
        P(),
        P("seq", "lat"),
        P("seq", "lat"),
        P("seq"),
        P("lat", None),
        P(),
    )
    out_specs = P(("seq", "lat"), None)
    return jax.shard_map(
        per_device, mesh=mesh, in_specs=in_specs, out_specs=out_specs, check_vma=False
    )
```

```python
import functools

import jax
import jax.numpy as jnp
from jax import lax
from jax.experimental import pallas as pl
from jax.experimental.pallas import tpu as pltpu
from jax.sharding import PartitionSpec as P

WINDOW = 1024
PREFIX = 512
EPS = 1e-06
THETA = 10000.0
QUERY_SCALE = 168.0 ** (-0.5)

NY, NC, NZ, NX = 4, 2, 4, 4
AXES = ("seq", "lat")
TILE = 896
F32, BF16 = jnp.float32, jnp.bfloat16


def first_bits(core):
    return 1 if core == 0 else 3


def second_bits(core):
    return 3 if core == 0 else 1


def exchange(value, dim, bits):
    pairs = []
    for y in range(NY):
        for c in range(NC):
            for z in range(NZ):
                for x in range(NX):
                    to = {"y": y, "c": c, "z": z, "x": x}
                    for axis in dim:
                        to[axis] ^= bits(c)
                    pairs.append(
                        (
                            (y * NC + c) * NZ * NX + z * NX + x,
                            (to["y"] * NC + to["c"]) * NZ * NX + to["z"] * NX + to["x"],
                        )
                    )
    return lax.ppermute(value, AXES, pairs)


def swap_cores(value):
    return exchange(value, "c", lambda core: 1)


def relative(place, core):
    step = jnp.arange(4, dtype=jnp.int32)
    order0 = jnp.where(step == 1, 3, jnp.where(step == 2, 1, jnp.where(step == 3, 2, 0)))
    order1 = jnp.where(step == 1, 1, jnp.where(step == 2, 3, jnp.where(step == 3, 2, 0)))
    return place ^ jnp.where(core == 0, order0, order1)


def row_order(z, x, core):
    zs, xs = relative(z, core), relative(x, core)
    row = (zs[:, None] * NX + xs[None, :])[:, :, None] * 8 + jnp.arange(8, dtype=jnp.int32)
    return row.reshape(-1)


def key_positions(y, core, z, x, old_rows, new_rows):
    block = old_rows + new_rows
    spot = lax.broadcasted_iota(jnp.int32, (1, NC * NY * block), 1)
    side = core ^ (spot // (NY * block))
    first = jnp.where(side == 0, 1, 3)

    def near(index, one, two):
        return jnp.where(index == 0, 0, jnp.where(index == 1, one, jnp.where(index == 2, two, 2)))

    shard = (y ^ near(spot // block % NY, first, first ^ 2)) * NC + side
    within = spot % block
    fresh = within - old_rows
    at_z = z ^ near(fresh // 32, first ^ 2, first)
    at_x = x ^ near(fresh // 8 % 4, first ^ 2, first)
    new = PREFIX + shard * new_rows + (at_z * NX + at_x) * 8 + fresh % 8
    return jnp.where(within < old_rows, shard * old_rows + within, new)


def rms_scale(values, gain):
    return values * lax.rsqrt(jnp.mean(values * values, axis=-1, keepdims=True) + EPS) * gain


def stage_kernel(source_ref, target_ref, sem):
    copy = pltpu.make_async_copy(source_ref, target_ref, sem)
    copy.start()
    copy.wait()


def stage(value):
    return pl.pallas_call(
        stage_kernel,
        name="stage",
        out_shape=jax.ShapeDtypeStruct(value.shape, value.dtype),
        in_specs=[pl.BlockSpec(memory_space=pl.ANY)],
        out_specs=pl.BlockSpec(memory_space=pltpu.VMEM),
        scratch_shapes=[pltpu.SemaphoreType.DMA],
        compiler_params=pltpu.CompilerParams(vmem_limit_bytes=6 * 1024 * 1024),
        cost_estimate=pl.CostEstimate(flops=0, bytes_accessed=2 * value.size, transcendentals=0),
    )(value)


def encode_kernel(count, *refs):
    blocks = refs[:count]
    picks = refs[count : 2 * count]
    own_ref, sib_ref, params_ref, codes_ref, rows_ref = refs[2 * count :]
    size = blocks[0].shape[0]
    lats = own_ref.shape[1]
    for i in range(count):
        rows_ref[i * size : (i + 1) * size, :] = blocks[i][...]
    for side, weights_ref in enumerate((own_ref, sib_ref)):
        there = slice(side * lats, (side + 1) * lats)
        pre = jnp.dot(rows_ref[...], weights_ref[...], preferred_element_type=F32)
        act = jnp.maximum(pre + params_ref[0:1, there] - params_ref[1:2, there], 0.0)
        codes = jnp.where(params_ref[2:3, there] > 0.0, params_ref[3:4, there], act)
        codes = codes.astype(BF16)
        for i in range(count):
            moved = jnp.dot(
                picks[i][...], codes[i * size : (i + 1) * size], preferred_element_type=F32
            )
            codes_ref[i * size : (i + 1) * size, there] = moved.astype(BF16)


def encode(blocks, picks, own, sib, params):
    count = len(blocks)
    size, width = blocks[0].shape
    lats = own.shape[1]
    return pl.pallas_call(
        functools.partial(encode_kernel, count),
        name="encode",
        out_shape=jax.ShapeDtypeStruct((count * size, 2 * lats), BF16),
        scratch_shapes=[pltpu.VMEM((count * size, width), BF16)],
        compiler_params=pltpu.CompilerParams(vmem_limit_bytes=12 * 1024 * 1024),
        cost_estimate=pl.CostEstimate(
            flops=4 * count * size * width * lats,
            bytes_accessed=4 * width * lats + 2 * count * size * (width + 2 * lats),
            transcendentals=0,
        ),
    )(*blocks, *picks, own, sib, params)


def decode_kernel(part, group, codes_ref, own_ref, sib_ref, keep_ref, send_ref):
    size = codes_ref.shape[0]
    lats, width = own_ref.shape
    half = group // 2
    for tile in range(width // 2 // TILE):
        here = slice(tile * TILE, (tile + 1) * TILE)
        there = slice(part * (width // 2) + tile * TILE, part * (width // 2) + (tile + 1) * TILE)
        total = jnp.dot(codes_ref[:, :lats], own_ref[:, there], preferred_element_type=F32)
        total += jnp.dot(codes_ref[:, lats:], sib_ref[:, there], preferred_element_type=F32)
        total = total.astype(BF16)
        for i in range(size // group):
            keep_ref[i * half : (i + 1) * half, here] = total[i * group : i * group + half, :]
            send_ref[i * half : (i + 1) * half, here] = total[i * group + half : (i + 1) * group, :]


def decode(codes, own, sib, part, group):
    size = codes.shape[0]
    lats, width = own.shape
    out = jax.ShapeDtypeStruct((size // 2, width // 2), BF16)
    return pl.pallas_call(
        functools.partial(decode_kernel, part, group),
        name="decode",
        out_shape=(out, out),
        compiler_params=pltpu.CompilerParams(vmem_limit_bytes=12 * 1024 * 1024),
        cost_estimate=pl.CostEstimate(
            flops=2 * size * lats * width,
            bytes_accessed=2 * (lats * width + 2 * size * lats + size * width // 2),
            transcendentals=0,
        ),
    )(codes, own, sib)


def project_kernel(
    left_ref,
    right_ref,
    gain_ref,
    query_w,
    key_w,
    value_w,
    head_gains,
    cosine_ref,
    sine_ref,
    cache_key,
    cache_value,
    query_ref,
    pairs_ref,
    normed_ref,
):
    part = left_ref.shape[1]
    hd = key_w.shape[1]
    left, right = left_ref[...].astype(F32), right_ref[...].astype(F32)
    square = jnp.sum(left * left, axis=-1, keepdims=True) + jnp.sum(
        right * right, axis=-1, keepdims=True
    )
    scale = lax.rsqrt(square / (2 * part) + EPS)
    normed_ref[:, :part] = (left * scale * gain_ref[0:1, :part]).astype(BF16)
    normed_ref[:, part:] = (right * scale * gain_ref[0:1, part:]).astype(BF16)
    normed = normed_ref[...]

    def turn(values, gain):
        values = rms_scale(values, gain)
        return (
            values * cosine_ref[...] + pltpu.roll(values, hd // 2, axis=1) * sine_ref[...]
        ).astype(BF16)

    old = cache_key.shape[0]
    pairs_ref[:old, :hd] = cache_key[...]
    pairs_ref[:old, hd:] = cache_value[...]
    key = jnp.dot(normed, key_w[...], preferred_element_type=F32)
    pairs_ref[old:, :hd] = turn(key, head_gains[1:2, :])
    value = jnp.dot(normed, value_w[...], preferred_element_type=F32)
    pairs_ref[old:, hd:] = value.astype(BF16)
    query = jnp.dot(normed, query_w[...], preferred_element_type=F32)
    for h in range(query_ref.shape[1] // hd):
        query_ref[:, h * hd : (h + 1) * hd] = turn(
            query[:, h * hd : (h + 1) * hd], head_gains[0:1, :]
        )


def project(left, right, gain, query_w, key_w, value_w, gains, cosine, sine, old_key, old_value):
    rows, hd = left.shape[0], key_w.shape[1]
    width = query_w.shape[0]
    return pl.pallas_call(
        project_kernel,
        name="project",
        out_shape=(
            jax.ShapeDtypeStruct((rows, query_w.shape[1]), BF16),
            jax.ShapeDtypeStruct((old_key.shape[0] + rows, 2 * hd), BF16),
        ),
        scratch_shapes=[pltpu.VMEM((rows, width), BF16)],
        compiler_params=pltpu.CompilerParams(vmem_limit_bytes=12 * 1024 * 1024),
        cost_estimate=pl.CostEstimate(
            flops=8 * rows * width * hd,
            bytes_accessed=8 * width * hd + 2 * rows * width,
            transcendentals=0,
        ),
    )(left, right, gain, query_w, key_w, value_w, gains, cosine, sine, old_key, old_value)


def attend_kernel(
    query_ref,
    own_ref,
    sib_ref,
    key_ctx,
    query_ctx,
    first_ctx,
    out_w,
    keep_z,
    send_z,
    keep_x,
    send_x,
    attended_ref,
    pairs_ref,
):
    rows, hd = query_ref.shape[0], pairs_ref.shape[1] // 2
    pairs_ref[: own_ref.shape[0], :] = own_ref[...]
    pairs_ref[own_ref.shape[0] :, :] = sib_ref[...]
    allowed = (
        (key_ctx[...] <= query_ctx[:, 0:1])
        & (key_ctx[...] > query_ctx[:, 0:1] - WINDOW)
        & (key_ctx[...] >= first_ctx[:, 0:1])
    )
    for h in range(query_ref.shape[1] // hd):
        scores = (
            lax.dot_general(
                query_ref[:, h * hd : (h + 1) * hd],
                pairs_ref[:, :hd],
                (((1,), (1,)), ((), ())),
                preferred_element_type=F32,
            )
            * QUERY_SCALE
        )
        scores = jnp.where(allowed, scores, -1e30)
        newest = jnp.max(scores, axis=-1, keepdims=True)
        weights = jnp.where(allowed, jnp.exp(scores - newest), 0.0)
        total = jnp.sum(weights, axis=-1, keepdims=True)
        mixed = jnp.dot(weights.astype(BF16), pairs_ref[:, hd:], preferred_element_type=F32)
        attended_ref[:, h * hd : (h + 1) * hd] = (mixed / total).astype(BF16)
    attended = attended_ref[...]
    part = out_w.shape[1] // 2
    for tile in range(part // TILE):
        here = slice(tile * TILE, (tile + 1) * TILE)
        left = jnp.dot(attended, out_w[:, here], preferred_element_type=F32).astype(BF16)
        keep_z[:, here] = left[: rows // 2]
        send_z[:, here] = left[rows // 2 :]
        there = slice(part + tile * TILE, part + (tile + 1) * TILE)
        right = jnp.dot(attended, out_w[:, there], preferred_element_type=F32).astype(BF16)
        for i in range(4):
            keep_x[i * 16 : (i + 1) * 16, here] = right[i * 32 : i * 32 + 16]
            send_x[i * 16 : (i + 1) * 16, here] = right[i * 32 + 16 : i * 32 + 32]


def attend(query, own, sib, key_ctx, query_ctx, first_ctx, out_w):
    rows, width = query.shape[0], out_w.shape[1]
    out = jax.ShapeDtypeStruct((rows // 2, width // 2), BF16)
    return pl.pallas_call(
        attend_kernel,
        name="attend",
        out_shape=(out, out, out, out),
        scratch_shapes=[
            pltpu.VMEM((rows, query.shape[1]), BF16),
            pltpu.VMEM((2 * own.shape[0], own.shape[1]), BF16),
        ],
        compiler_params=pltpu.CompilerParams(vmem_limit_bytes=12 * 1024 * 1024),
        cost_estimate=pl.CostEstimate(
            flops=2 * rows * query.shape[1] * (4 * own.shape[0] + width),
            bytes_accessed=2 * (query.shape[1] * width + rows * width + 2 * own.size),
            transcendentals=4 * rows * own.shape[0],
        ),
    )(query, own, sib, key_ctx, query_ctx, first_ctx, out_w)


def split(value, group):
    rows, width = value.shape
    grouped = value.reshape(rows // group, group, width)
    half = group // 2
    return (
        grouped[:, :half].reshape(rows // 2, width),
        grouped[:, half:].reshape(rows // 2, width),
    )


def add(left, right):
    return (left.astype(F32) + right.astype(F32)).astype(BF16)


def reduce_step(value, dim, bits, group):
    keep, send = split(value, group)
    return add(keep, exchange(send, dim, bits))


def swap_halves(value, group):
    keep, send = split(value, group)
    rows, width = value.shape
    half = group // 2
    return jnp.concatenate(
        [send.reshape(-1, half, width), keep.reshape(-1, half, width)], axis=1
    ).reshape(rows, width)


def gather_step(value, dim, bits, group):
    other = exchange(value, dim, bits)
    rows, width = value.shape
    return jnp.concatenate(
        [value.reshape(-1, group, width), other.reshape(-1, group, width)], axis=1
    ).reshape(2 * rows, width)


def per_device(
    resid,
    w_enc,
    b_enc,
    threshold,
    w_dec,
    b_dec,
    clamp_ids,
    clamp_index,
    clamp_table,
    pre_gain,
    w_query,
    w_key,
    w_value,
    q_gain,
    k_gain,
    cache_key,
    cache_value,
    starts,
    w_out,
    post_gain,
):
    seq_place = lax.axis_index("seq")
    lat_place = lax.axis_index("lat")
    core = seq_place % NC
    z, x = lat_place // NX, lat_place % NX
    tok_rows, width = resid.shape
    part = width // 2
    lats = w_enc.shape[1]
    head_size = q_gain.shape[0]

    order = row_order(z, x, core)
    pick = order[:, None] == jnp.arange(tok_rows, dtype=jnp.int32)[None, :]

    with jax.named_scope("swap_weights"):
        offsets = jnp.stack([b_enc, threshold])
        sib_offsets = swap_cores(offsets)
        sib_enc = stage(swap_cores(w_enc))
        sib_dec = stage(swap_cores(w_dec))

    with jax.named_scope("gather_resid"):
        quarter = tok_rows // 4
        piece = 2 * (z % 2) + x % 2
        near = exchange(resid, "y", first_bits)
        query_ctx = PREFIX + seq_place * tok_rows + order
        query_col = jnp.broadcast_to(query_ctx[:, None], (tok_rows, tok_rows))
        first_col = jnp.broadcast_to(
            jnp.sum(jnp.where(pick, starts[None, :], 0), axis=1, keepdims=True),
            (tok_rows, tok_rows),
        )
        key_ctx = key_positions(seq_place // NC, core, z, x, cache_key.shape[0], tok_rows)
        near, sib_enc, query_col, first_col, key_ctx = lax.optimization_barrier(
            (near, sib_enc, query_col, first_col, key_ctx)
        )
        mine = lax.dynamic_slice_in_dim(near, piece * quarter, quarter, 0)
        again, mine = lax.optimization_barrier((resid, mine))
        mine = exchange(mine, "y", second_bits)
        far = exchange(again, "y", second_bits)
        near, mine = lax.optimization_barrier((near, mine))
        left, right = mine[:, :part], mine[:, part:]
        left_more = exchange(left, "x", first_bits)
        right_more = exchange(right, "z", first_bits)
        spot = jnp.arange(tok_rows, dtype=jnp.int32)
        spot = (piece ^ (spot // quarter)) * quarter + spot % quarter
        pick_opposite = (order[:, None] == spot[None, :]).astype(BF16)
        pick_rows = pick.astype(BF16)

    with jax.named_scope("clamp"):
        table_pick = (
            clamp_index[:, None] == jnp.arange(clamp_table.shape[0], dtype=jnp.int32)[None, :]
        )
        values = jnp.sum(jnp.where(table_pick, clamp_table[None, :], 0.0), axis=1)
        spread = jnp.arange(lats, dtype=jnp.int32)
        here = jnp.concatenate(
            [
                (seq_place * NZ * NX + lat_place) * lats + spread,
                ((seq_place ^ 1) * NZ * NX + lat_place) * lats + spread,
            ]
        )
        match = here[None, :] == clamp_ids[:, None]
        clamped = jnp.any(match, axis=0).astype(F32)
        level = jnp.sum(jnp.where(match, values[:, None], 0.0), axis=0)
        params = jnp.concatenate(
            [
                jnp.concatenate([offsets, sib_offsets], axis=1),
                clamped[None, :],
                level[None, :],
            ],
            axis=0,
        )

    def terms(codes):
        return (
            decode(codes, w_dec, sib_dec, 0, 128),
            decode(codes, w_dec, sib_dec, 1, 32),
        )

    def first_exchange(terms_z, terms_x):
        return exchange(terms_z[1], "z", first_bits), exchange(terms_x[1], "x", first_bits)

    def halves(terms_z, terms_x, received):
        sum_z = add(terms_z[0], received[0])
        sum_x = add(terms_x[0], received[1])
        return split(sum_z, 32), split(sum_x, 64)

    def second_exchange(halves_z, halves_x):
        return (
            exchange(halves_z[1], "x", first_bits),
            exchange(halves_x[1], "z", first_bits),
        )

    def plane_sums(halves_z, halves_x, received):
        return jnp.concatenate(
            [add(halves_z[0], received[0]), add(halves_x[0], received[1])], axis=1
        )

    with jax.named_scope("early_tokens"):
        early_codes = encode([resid, near], [pick_rows, pick_rows], w_enc, sib_enc, params)
        early_codes, left_more, right_more = lax.optimization_barrier(
            (early_codes, left_more, right_more)
        )
        left = jnp.concatenate([left, left_more])
        right = jnp.concatenate([right, right_more])
        left = jnp.concatenate([left, exchange(left, "z", first_bits)])
        more = exchange(right, "x", first_bits)
        right = jnp.concatenate(
            [right[:quarter], more[:quarter], right[quarter:], more[quarter:]]
        )
        opposite = jnp.concatenate([left, right], axis=1)
        early_terms = terms(early_codes)
        early_received = first_exchange(*early_terms)
        (far, opposite), _ = lax.optimization_barrier(((far, opposite), early_terms))
    with jax.named_scope("late_tokens"):
        late_terms = terms(
            encode([far, opposite], [pick_rows, pick_opposite], w_enc, sib_enc, params)
        )
        late_received = first_exchange(*late_terms)
        (early_received, _) = lax.optimization_barrier((early_received, late_terms))
        early_halves = halves(*early_terms, early_received)
        early_received = second_exchange(*early_halves)
        late_halves = halves(*late_terms, late_received)
        late_received = second_exchange(*late_halves)
        early_received, _ = lax.optimization_barrier((early_received, late_halves))
        early = plane_sums(*early_halves, early_received)
        late = plane_sums(*late_halves, late_received)

    with jax.named_scope("sum_over_chips"):
        quarter = tok_rows // 4
        near_sums = exchange(early[quarter:], "y", first_bits)
        far_sums = exchange(late[:quarter], "y", second_bits)
        opposite_sums = exchange(late[quarter:], "y", lambda core: 2)
        total = early[:quarter].astype(F32) + near_sums.astype(F32)
        total = (total + far_sums.astype(F32) + opposite_sums.astype(F32)).astype(BF16)
        over_x = swap_halves(exchange(total, "x", second_bits), 16)
        over_z = swap_halves(exchange(total, "z", second_bits), 32)
        over_both = swap_halves(swap_halves(exchange(total, "zx", second_bits), 32), 16)
        total = (total.astype(F32) + over_x.astype(F32)) + (
            over_z.astype(F32) + over_both.astype(F32)
        )
        rest = (total + b_dec).astype(BF16)
        restored = rest[:8]

    with jax.named_scope("gather_restored"):
        rest_z = gather_step(rest[:, :part], "x", first_bits, 16)
        rest_x = gather_step(rest[:, part:], "z", first_bits, 32)
        rest_z = gather_step(rest_z, "z", first_bits, 64)
        rest_x = gather_step(rest_x, "x", first_bits, 16)

    with jax.named_scope("projections"):
        freq = THETA ** (-(jnp.arange(head_size // 2, dtype=F32) * 2.0 / head_size))
        angle = query_ctx.astype(F32)[:, None] * freq[None, :]
        cosine, sine = jnp.cos(angle), jnp.sin(angle)
        cosine = jnp.concatenate([cosine, cosine], axis=1)
        sine = jnp.concatenate([-sine, sine], axis=1)
        query, own_pairs = project(
            rest_z,
            rest_x,
            pre_gain[None, :],
            w_query,
            w_key,
            w_value,
            jnp.stack([q_gain, k_gain]),
            cosine,
            sine,
            cache_key,
            cache_value,
        )

    with jax.named_scope("attention"):
        pairs = jnp.concatenate(
            [
                own_pairs,
                exchange(own_pairs, "y", first_bits),
                exchange(own_pairs, "y", second_bits),
                exchange(own_pairs, "y", lambda place: 2),
            ]
        )
        sib_pairs = swap_cores(pairs)
        keep_z, send_z, keep_x, send_x = attend(
            query, pairs, sib_pairs, key_ctx, query_col, first_col, w_out
        )

    with jax.named_scope("sum_over_heads"):
        out_z = add(keep_z, exchange(send_z, "z", first_bits))
        out_x = add(keep_x, exchange(send_x, "x", first_bits))
        out_z = reduce_step(out_z, "x", first_bits, 32)
        out_x = reduce_step(out_x, "z", first_bits, 64)
        both = jnp.concatenate([out_z, out_x], axis=1)
        mine = both[:8].astype(F32)
        for place, axes in enumerate(("x", "z", "zx")):
            rows = both[8 * place + 8 : 8 * place + 16]
            mine = mine + exchange(rows, axes, second_bits).astype(F32)
        return (restored.astype(F32) + rms_scale(mine, post_gain)).astype(BF16)


def solution(mesh):
    in_specs = (
        P("seq", None),
        P(None, ("seq", "lat")),
        P(("seq", "lat")),
        P(("seq", "lat")),
        P(("seq", "lat"), None),
        P(),
        P(),
        P(),
        P(),
        P(),
        P(None, "lat"),
        P(None, "lat"),
        P(None, "lat"),
        P(),
        P(),
        P("seq", "lat"),
        P("seq", "lat"),
        P("seq"),
        P("lat", None),
        P(),
    )
    out_specs = P(("seq", "lat"), None)
    return jax.shard_map(
        per_device, mesh=mesh, in_specs=in_specs, out_specs=out_specs, check_vma=False
    )
```

```python
import functools

import jax
import jax.numpy as jnp
from jax import lax
from jax.experimental import pallas as pl
from jax.experimental.pallas import tpu as pltpu
from jax.sharding import PartitionSpec as P

WINDOW = 1024
PREFIX = 512
EPS = 1e-06
THETA = 10000.0
QUERY_SCALE = 168.0 ** (-0.5)

NY, NC, NZ, NX = 4, 2, 4, 4
AXES = ("seq", "lat")
TILE = 2688
F32, BF16 = jnp.float32, jnp.bfloat16


def first_bits(core):
    return 1 if core == 0 else 3


def second_bits(core):
    return 3 if core == 0 else 1


def exchange(value, dim, bits):
    pairs = []
    for y in range(NY):
        for c in range(NC):
            for z in range(NZ):
                for x in range(NX):
                    to = {"y": y, "c": c, "z": z, "x": x}
                    for axis in dim:
                        to[axis] ^= bits(c)
                    pairs.append(
                        (
                            (y * NC + c) * NZ * NX + z * NX + x,
                            (to["y"] * NC + to["c"]) * NZ * NX + to["z"] * NX + to["x"],
                        )
                    )
    return lax.ppermute(value, AXES, pairs)


def swap_cores(value):
    return exchange(value, "c", lambda core: 1)


def relative(place, core):
    step = jnp.arange(4, dtype=jnp.int32)
    order0 = jnp.where(step == 1, 3, jnp.where(step == 2, 1, jnp.where(step == 3, 2, 0)))
    order1 = jnp.where(step == 1, 1, jnp.where(step == 2, 3, jnp.where(step == 3, 2, 0)))
    return place ^ jnp.where(core == 0, order0, order1)


def row_order(z, x, core):
    zs, xs = relative(z, core), relative(x, core)
    row = (zs[:, None] * NX + xs[None, :])[:, :, None] * 8 + jnp.arange(8, dtype=jnp.int32)
    return row.reshape(-1)


def key_positions(y, core, z, x, old_rows, new_rows):
    block = old_rows + new_rows
    spot = lax.broadcasted_iota(jnp.int32, (1, NC * NY * block), 1)
    side = core ^ (spot // (NY * block))
    first = jnp.where(side == 0, 1, 3)

    def near(index, one, two):
        return jnp.where(index == 0, 0, jnp.where(index == 1, one, jnp.where(index == 2, two, 2)))

    shard = (y ^ near(spot // block % NY, first, first ^ 2)) * NC + side
    within = spot % block
    fresh = within - old_rows
    at_z = z ^ near(fresh // 32, first ^ 2, first)
    at_x = x ^ near(fresh // 8 % 4, first ^ 2, first)
    new = PREFIX + shard * new_rows + (at_z * NX + at_x) * 8 + fresh % 8
    return jnp.where(within < old_rows, shard * old_rows + within, new)


def rms_scale(values, gain):
    return values * lax.rsqrt(jnp.mean(values * values, axis=-1, keepdims=True) + EPS) * gain


def stage_kernel(source_ref, target_ref, sem):
    copy = pltpu.make_async_copy(source_ref, target_ref, sem)
    copy.start()
    copy.wait()


def stage(value):
    return pl.pallas_call(
        stage_kernel,
        name="stage",
        out_shape=jax.ShapeDtypeStruct(value.shape, value.dtype),
        in_specs=[pl.BlockSpec(memory_space=pl.ANY)],
        out_specs=pl.BlockSpec(memory_space=pltpu.VMEM),
        scratch_shapes=[pltpu.SemaphoreType.DMA],
        compiler_params=pltpu.CompilerParams(vmem_limit_bytes=6 * 1024 * 1024),
        cost_estimate=pl.CostEstimate(flops=0, bytes_accessed=2 * value.size, transcendentals=0),
    )(value)


def encode_kernel(count, *refs):
    blocks = refs[:count]
    picks = refs[count : 2 * count]
    own_ref, sib_ref, params_ref, codes_ref, rows_ref = refs[2 * count :]
    size = blocks[0].shape[0]
    lats = own_ref.shape[1]
    for i in range(count):
        rows_ref[i * size : (i + 1) * size, :] = blocks[i][...]
    for side, weights_ref in enumerate((own_ref, sib_ref)):
        there = slice(side * lats, (side + 1) * lats)
        pre = jnp.dot(rows_ref[...], weights_ref[...], preferred_element_type=F32)
        act = jnp.maximum(pre + params_ref[0:1, there] - params_ref[1:2, there], 0.0)
        codes = jnp.where(params_ref[2:3, there] > 0.0, params_ref[3:4, there], act)
        codes = codes.astype(BF16)
        for i in range(count):
            moved = jnp.dot(
                picks[i][...], codes[i * size : (i + 1) * size], preferred_element_type=F32
            )
            codes_ref[i * size : (i + 1) * size, there] = moved.astype(BF16)


def encode(blocks, picks, own, sib, params):
    count = len(blocks)
    size, width = blocks[0].shape
    lats = own.shape[1]
    return pl.pallas_call(
        functools.partial(encode_kernel, count),
        name="encode",
        out_shape=jax.ShapeDtypeStruct((count * size, 2 * lats), BF16),
        scratch_shapes=[pltpu.VMEM((count * size, width), BF16)],
        compiler_params=pltpu.CompilerParams(vmem_limit_bytes=12 * 1024 * 1024),
        cost_estimate=pl.CostEstimate(
            flops=4 * count * size * width * lats,
            bytes_accessed=4 * width * lats + 2 * count * size * (width + 2 * lats),
            transcendentals=0,
        ),
    )(*blocks, *picks, own, sib, params)


def decode_kernel(part, group, codes_ref, own_ref, sib_ref, keep_ref, send_ref):
    size = codes_ref.shape[0]
    lats, width = own_ref.shape
    half = group // 2
    for tile in range(width // 2 // TILE):
        here = slice(tile * TILE, (tile + 1) * TILE)
        there = slice(part * (width // 2) + tile * TILE, part * (width // 2) + (tile + 1) * TILE)
        total = jnp.dot(codes_ref[:, :lats], own_ref[:, there], preferred_element_type=F32)
        total += jnp.dot(codes_ref[:, lats:], sib_ref[:, there], preferred_element_type=F32)
        total = total.astype(BF16)
        for i in range(size // group):
            keep_ref[i * half : (i + 1) * half, here] = total[i * group : i * group + half, :]
            send_ref[i * half : (i + 1) * half, here] = total[i * group + half : (i + 1) * group, :]


def decode(codes, own, sib, part, group):
    size = codes.shape[0]
    lats, width = own.shape
    out = jax.ShapeDtypeStruct((size // 2, width // 2), BF16)
    return pl.pallas_call(
        functools.partial(decode_kernel, part, group),
        name="decode",
        out_shape=(out, out),
        compiler_params=pltpu.CompilerParams(vmem_limit_bytes=12 * 1024 * 1024),
        cost_estimate=pl.CostEstimate(
            flops=2 * size * lats * width,
            bytes_accessed=2 * (lats * width + 2 * size * lats + size * width // 2),
            transcendentals=0,
        ),
    )(codes, own, sib)


def project_kernel(
    left_ref,
    right_ref,
    gain_ref,
    query_w,
    key_w,
    value_w,
    head_gains,
    cosine_ref,
    sine_ref,
    cache_key,
    cache_value,
    query_ref,
    pairs_ref,
    normed_ref,
):
    part = left_ref.shape[1]
    hd = key_w.shape[1]
    left, right = left_ref[...].astype(F32), right_ref[...].astype(F32)
    square = jnp.sum(left * left, axis=-1, keepdims=True) + jnp.sum(
        right * right, axis=-1, keepdims=True
    )
    scale = lax.rsqrt(square / (2 * part) + EPS)
    normed_ref[:, :part] = (left * scale * gain_ref[0:1, :part]).astype(BF16)
    normed_ref[:, part:] = (right * scale * gain_ref[0:1, part:]).astype(BF16)
    normed = normed_ref[...]

    def turn(values, gain):
        values = rms_scale(values, gain)
        return (
            values * cosine_ref[...] + pltpu.roll(values, hd // 2, axis=1) * sine_ref[...]
        ).astype(BF16)

    old = cache_key.shape[0]
    pairs_ref[:old, :hd] = cache_key[...]
    pairs_ref[:old, hd:] = cache_value[...]
    key = jnp.dot(normed, key_w[...], preferred_element_type=F32)
    pairs_ref[old:, :hd] = turn(key, head_gains[1:2, :])
    value = jnp.dot(normed, value_w[...], preferred_element_type=F32)
    pairs_ref[old:, hd:] = value.astype(BF16)
    query = jnp.dot(normed, query_w[...], preferred_element_type=F32)
    for h in range(query_ref.shape[1] // hd):
        query_ref[:, h * hd : (h + 1) * hd] = turn(
            query[:, h * hd : (h + 1) * hd], head_gains[0:1, :]
        )


def project(left, right, gain, query_w, key_w, value_w, gains, cosine, sine, old_key, old_value):
    rows, hd = left.shape[0], key_w.shape[1]
    width = query_w.shape[0]
    return pl.pallas_call(
        project_kernel,
        name="project",
        out_shape=(
            jax.ShapeDtypeStruct((rows, query_w.shape[1]), BF16),
            jax.ShapeDtypeStruct((old_key.shape[0] + rows, 2 * hd), BF16),
        ),
        scratch_shapes=[pltpu.VMEM((rows, width), BF16)],
        compiler_params=pltpu.CompilerParams(vmem_limit_bytes=12 * 1024 * 1024),
        cost_estimate=pl.CostEstimate(
            flops=8 * rows * width * hd,
            bytes_accessed=8 * width * hd + 2 * rows * width,
            transcendentals=0,
        ),
    )(left, right, gain, query_w, key_w, value_w, gains, cosine, sine, old_key, old_value)


def attend_kernel(
    query_ref,
    own_ref,
    sib_ref,
    key_ctx,
    query_ctx,
    first_ctx,
    out_w,
    keep_z,
    send_z,
    keep_x,
    send_x,
    attended_ref,
    pairs_ref,
):
    rows, hd = query_ref.shape[0], pairs_ref.shape[1] // 2
    pairs_ref[: own_ref.shape[0], :] = own_ref[...]
    pairs_ref[own_ref.shape[0] :, :] = sib_ref[...]
    allowed = (
        (key_ctx[...] <= query_ctx[:, 0:1])
        & (key_ctx[...] > query_ctx[:, 0:1] - WINDOW)
        & (key_ctx[...] >= first_ctx[:, 0:1])
    )
    for h in range(query_ref.shape[1] // hd):
        scores = (
            lax.dot_general(
                query_ref[:, h * hd : (h + 1) * hd],
                pairs_ref[:, :hd],
                (((1,), (1,)), ((), ())),
                preferred_element_type=F32,
            )
            * QUERY_SCALE
        )
        scores = jnp.where(allowed, scores, -1e30)
        newest = jnp.max(scores, axis=-1, keepdims=True)
        weights = jnp.where(allowed, jnp.exp(scores - newest), 0.0)
        total = jnp.sum(weights, axis=-1, keepdims=True)
        mixed = jnp.dot(weights.astype(BF16), pairs_ref[:, hd:], preferred_element_type=F32)
        attended_ref[:, h * hd : (h + 1) * hd] = (mixed / total).astype(BF16)
    attended = attended_ref[...]
    part = out_w.shape[1] // 2
    for tile in range(part // TILE):
        here = slice(tile * TILE, (tile + 1) * TILE)
        left = jnp.dot(attended, out_w[:, here], preferred_element_type=F32).astype(BF16)
        keep_z[:, here] = left[: rows // 2]
        send_z[:, here] = left[rows // 2 :]
        there = slice(part + tile * TILE, part + (tile + 1) * TILE)
        right = jnp.dot(attended, out_w[:, there], preferred_element_type=F32).astype(BF16)
        for i in range(4):
            keep_x[i * 16 : (i + 1) * 16, here] = right[i * 32 : i * 32 + 16]
            send_x[i * 16 : (i + 1) * 16, here] = right[i * 32 + 16 : i * 32 + 32]


def attend(query, own, sib, key_ctx, query_ctx, first_ctx, out_w):
    rows, width = query.shape[0], out_w.shape[1]
    out = jax.ShapeDtypeStruct((rows // 2, width // 2), BF16)
    return pl.pallas_call(
        attend_kernel,
        name="attend",
        out_shape=(out, out, out, out),
        scratch_shapes=[
            pltpu.VMEM((rows, query.shape[1]), BF16),
            pltpu.VMEM((2 * own.shape[0], own.shape[1]), BF16),
        ],
        compiler_params=pltpu.CompilerParams(vmem_limit_bytes=12 * 1024 * 1024),
        cost_estimate=pl.CostEstimate(
            flops=2 * rows * query.shape[1] * (4 * own.shape[0] + width),
            bytes_accessed=2 * (query.shape[1] * width + rows * width + 2 * own.size),
            transcendentals=4 * rows * own.shape[0],
        ),
    )(query, own, sib, key_ctx, query_ctx, first_ctx, out_w)


def split(value, group):
    rows, width = value.shape
    grouped = value.reshape(rows // group, group, width)
    half = group // 2
    return (
        grouped[:, :half].reshape(rows // 2, width),
        grouped[:, half:].reshape(rows // 2, width),
    )


def add(left, right):
    return (left.astype(F32) + right.astype(F32)).astype(BF16)


def reduce_step(value, dim, bits, group):
    keep, send = split(value, group)
    return add(keep, exchange(send, dim, bits))


def swap_halves(value, group):
    keep, send = split(value, group)
    rows, width = value.shape
    half = group // 2
    return jnp.concatenate(
        [send.reshape(-1, half, width), keep.reshape(-1, half, width)], axis=1
    ).reshape(rows, width)


def gather_step(value, dim, bits, group):
    other = exchange(value, dim, bits)
    rows, width = value.shape
    return jnp.concatenate(
        [value.reshape(-1, group, width), other.reshape(-1, group, width)], axis=1
    ).reshape(2 * rows, width)


def per_device(
    resid,
    w_enc,
    b_enc,
    threshold,
    w_dec,
    b_dec,
    clamp_ids,
    clamp_index,
    clamp_table,
    pre_gain,
    w_query,
    w_key,
    w_value,
    q_gain,
    k_gain,
    cache_key,
    cache_value,
    starts,
    w_out,
    post_gain,
):
    seq_place = lax.axis_index("seq")
    lat_place = lax.axis_index("lat")
    core = seq_place % NC
    z, x = lat_place // NX, lat_place % NX
    tok_rows, width = resid.shape
    part = width // 2
    lats = w_enc.shape[1]
    head_size = q_gain.shape[0]

    order = row_order(z, x, core)
    pick = order[:, None] == jnp.arange(tok_rows, dtype=jnp.int32)[None, :]

    with jax.named_scope("swap_weights"):
        offsets = jnp.stack([b_enc, threshold])
        sib_offsets = swap_cores(offsets)
        sib_enc = stage(swap_cores(w_enc))
        sib_dec = stage(swap_cores(w_dec))

    with jax.named_scope("gather_resid"):
        quarter = tok_rows // 4
        piece = 2 * (z % 2) + x % 2
        near = exchange(resid, "y", first_bits)
        query_ctx = PREFIX + seq_place * tok_rows + order
        query_col = jnp.broadcast_to(query_ctx[:, None], (tok_rows, tok_rows))
        first_col = jnp.broadcast_to(
            jnp.sum(jnp.where(pick, starts[None, :], 0), axis=1, keepdims=True),
            (tok_rows, tok_rows),
        )
        key_ctx = key_positions(seq_place // NC, core, z, x, cache_key.shape[0], tok_rows)
        near, sib_enc, query_col, first_col, key_ctx = lax.optimization_barrier(
            (near, sib_enc, query_col, first_col, key_ctx)
        )
        mine = lax.dynamic_slice_in_dim(near, piece * quarter, quarter, 0)
        again, mine = lax.optimization_barrier((resid, mine))
        mine = exchange(mine, "y", second_bits)
        far = exchange(again, "y", second_bits)
        near, mine = lax.optimization_barrier((near, mine))
        left, right = mine[:, :part], mine[:, part:]
        left_more = exchange(left, "x", first_bits)
        right_more = exchange(right, "z", first_bits)
        spot = jnp.arange(tok_rows, dtype=jnp.int32)
        spot = (piece ^ (spot // quarter)) * quarter + spot % quarter
        pick_opposite = (order[:, None] == spot[None, :]).astype(BF16)
        pick_rows = pick.astype(BF16)

    with jax.named_scope("clamp"):
        table_pick = (
            clamp_index[:, None] == jnp.arange(clamp_table.shape[0], dtype=jnp.int32)[None, :]
        )
        values = jnp.sum(jnp.where(table_pick, clamp_table[None, :], 0.0), axis=1)
        spread = jnp.arange(lats, dtype=jnp.int32)
        here = jnp.concatenate(
            [
                (seq_place * NZ * NX + lat_place) * lats + spread,
                ((seq_place ^ 1) * NZ * NX + lat_place) * lats + spread,
            ]
        )
        match = here[None, :] == clamp_ids[:, None]
        clamped = jnp.any(match, axis=0).astype(F32)
        level = jnp.sum(jnp.where(match, values[:, None], 0.0), axis=0)
        params = jnp.concatenate(
            [
                jnp.concatenate([offsets, sib_offsets], axis=1),
                clamped[None, :],
                level[None, :],
            ],
            axis=0,
        )

    def terms(codes):
        return (
            decode(codes, w_dec, sib_dec, 0, 128),
            decode(codes, w_dec, sib_dec, 1, 32),
        )

    def first_exchange(terms_z, terms_x):
        return exchange(terms_z[1], "z", first_bits), exchange(terms_x[1], "x", first_bits)

    def halves(terms_z, terms_x, received):
        sum_z = add(terms_z[0], received[0])
        sum_x = add(terms_x[0], received[1])
        return split(sum_z, 32), split(sum_x, 64)

    def second_exchange(halves_z, halves_x):
        return (
            exchange(halves_z[1], "x", first_bits),
            exchange(halves_x[1], "z", first_bits),
        )

    def plane_sums(halves_z, halves_x, received):
        return jnp.concatenate(
            [add(halves_z[0], received[0]), add(halves_x[0], received[1])], axis=1
        )

    with jax.named_scope("early_tokens"):
        early_codes = encode([resid, near], [pick_rows, pick_rows], w_enc, sib_enc, params)
        early_codes, left_more, right_more = lax.optimization_barrier(
            (early_codes, left_more, right_more)
        )
        left = jnp.concatenate([left, left_more])
        right = jnp.concatenate([right, right_more])
        left = jnp.concatenate([left, exchange(left, "z", first_bits)])
        more = exchange(right, "x", first_bits)
        right = jnp.concatenate(
            [right[:quarter], more[:quarter], right[quarter:], more[quarter:]]
        )
        opposite = jnp.concatenate([left, right], axis=1)
        early_terms = terms(early_codes)
        early_received = first_exchange(*early_terms)
        (far, opposite), _ = lax.optimization_barrier(((far, opposite), early_terms))
    with jax.named_scope("late_tokens"):
        late_terms = terms(
            encode([far, opposite], [pick_rows, pick_opposite], w_enc, sib_enc, params)
        )
        late_received = first_exchange(*late_terms)
        (early_received, _) = lax.optimization_barrier((early_received, late_terms))
        early_halves = halves(*early_terms, early_received)
        early_received = second_exchange(*early_halves)
        late_halves = halves(*late_terms, late_received)
        late_received = second_exchange(*late_halves)
        early_received, _ = lax.optimization_barrier((early_received, late_halves))
        early = plane_sums(*early_halves, early_received)
        late = plane_sums(*late_halves, late_received)

    with jax.named_scope("sum_over_chips"):
        quarter = tok_rows // 4
        near_sums = exchange(early[quarter:], "y", first_bits)
        far_sums = exchange(late[:quarter], "y", second_bits)
        opposite_sums = exchange(late[quarter:], "y", lambda core: 2)
        total = early[:quarter].astype(F32) + near_sums.astype(F32)
        total = (total + far_sums.astype(F32) + opposite_sums.astype(F32)).astype(BF16)
        total = add(total, swap_halves(exchange(total, "z", second_bits), 32))
        other = swap_halves(exchange(total, "x", second_bits), 16)
        total = total.astype(F32) + other.astype(F32)
        rest = (total + b_dec).astype(BF16)
        restored = rest[:8]

    with jax.named_scope("gather_restored"):
        rest_z = gather_step(rest[:, :part], "x", first_bits, 16)
        rest_x = gather_step(rest[:, part:], "z", first_bits, 32)
        rest_z = gather_step(rest_z, "z", first_bits, 64)
        rest_x = gather_step(rest_x, "x", first_bits, 16)

    with jax.named_scope("projections"):
        freq = THETA ** (-(jnp.arange(head_size // 2, dtype=F32) * 2.0 / head_size))
        angle = query_ctx.astype(F32)[:, None] * freq[None, :]
        cosine, sine = jnp.cos(angle), jnp.sin(angle)
        cosine = jnp.concatenate([cosine, cosine], axis=1)
        sine = jnp.concatenate([-sine, sine], axis=1)
        query, own_pairs = project(
            rest_z,
            rest_x,
            pre_gain[None, :],
            w_query,
            w_key,
            w_value,
            jnp.stack([q_gain, k_gain]),
            cosine,
            sine,
            cache_key,
            cache_value,
        )

    with jax.named_scope("attention"):
        pairs = jnp.concatenate(
            [
                own_pairs,
                exchange(own_pairs, "y", first_bits),
                exchange(own_pairs, "y", second_bits),
                exchange(own_pairs, "y", lambda place: 2),
            ]
        )
        sib_pairs = swap_cores(pairs)
        keep_z, send_z, keep_x, send_x = attend(
            query, pairs, sib_pairs, key_ctx, query_col, first_col, w_out
        )

    with jax.named_scope("sum_over_heads"):
        out_z = add(keep_z, exchange(send_z, "z", first_bits))
        out_x = add(keep_x, exchange(send_x, "x", first_bits))
        out_z = reduce_step(out_z, "x", first_bits, 32)
        out_x = reduce_step(out_x, "z", first_bits, 64)
        both = jnp.concatenate([out_z, out_x], axis=1)
        mine = both[:8].astype(F32)
        for place, axes in enumerate(("x", "z", "zx")):
            rows = both[8 * place + 8 : 8 * place + 16]
            mine = mine + exchange(rows, axes, second_bits).astype(F32)
        return (restored.astype(F32) + rms_scale(mine, post_gain)).astype(BF16)


def solution(mesh):
    in_specs = (
        P("seq", None),
        P(None, ("seq", "lat")),
        P(("seq", "lat")),
        P(("seq", "lat")),
        P(("seq", "lat"), None),
        P(),
        P(),
        P(),
        P(),
        P(),
        P(None, "lat"),
        P(None, "lat"),
        P(None, "lat"),
        P(),
        P(),
        P("seq", "lat"),
        P("seq", "lat"),
        P("seq"),
        P("lat", None),
        P(),
    )
    out_specs = P(("seq", "lat"), None)
    return jax.shard_map(
        per_device, mesh=mesh, in_specs=in_specs, out_specs=out_specs, check_vma=False
    )
```

```python
import functools

import jax
import jax.numpy as jnp
from jax import lax
from jax.experimental import pallas as pl
from jax.experimental.pallas import tpu as pltpu
from jax.sharding import PartitionSpec as P

WINDOW = 1024
PREFIX = 512
EPS = 1e-06
THETA = 10000.0
QUERY_SCALE = 168.0 ** (-0.5)

NY, NC, NZ, NX = 4, 2, 4, 4
AXES = ("seq", "lat")
TILE = 2688
F32, BF16 = jnp.float32, jnp.bfloat16


def first_bits(core):
    return 1 if core == 0 else 3


def second_bits(core):
    return 3 if core == 0 else 1


def exchange(value, dim, bits):
    pairs = []
    for y in range(NY):
        for c in range(NC):
            for z in range(NZ):
                for x in range(NX):
                    to = {"y": y, "c": c, "z": z, "x": x}
                    for axis in dim:
                        to[axis] ^= bits(c)
                    pairs.append(
                        (
                            (y * NC + c) * NZ * NX + z * NX + x,
                            (to["y"] * NC + to["c"]) * NZ * NX + to["z"] * NX + to["x"],
                        )
                    )
    return lax.ppermute(value, AXES, pairs)


def swap_cores(value):
    return exchange(value, "c", lambda core: 1)


def relative(place, core):
    step = jnp.arange(4, dtype=jnp.int32)
    order0 = jnp.where(step == 1, 3, jnp.where(step == 2, 1, jnp.where(step == 3, 2, 0)))
    order1 = jnp.where(step == 1, 1, jnp.where(step == 2, 3, jnp.where(step == 3, 2, 0)))
    return place ^ jnp.where(core == 0, order0, order1)


def row_order(z, x, core):
    zs, xs = relative(z, core), relative(x, core)
    row = (zs[:, None] * NX + xs[None, :])[:, :, None] * 8 + jnp.arange(8, dtype=jnp.int32)
    return row.reshape(-1)


def key_positions(y, core, z, x, old_rows, new_rows):
    block = old_rows + new_rows
    spot = lax.broadcasted_iota(jnp.int32, (1, NC * NY * block), 1)
    side = core ^ (spot // (NY * block))
    first = jnp.where(side == 0, 1, 3)

    def near(index, one, two):
        return jnp.where(index == 0, 0, jnp.where(index == 1, one, jnp.where(index == 2, two, 2)))

    shard = (y ^ near(spot // block % NY, first, first ^ 2)) * NC + side
    within = spot % block
    fresh = within - old_rows
    at_z = z ^ near(fresh // 32, first ^ 2, first)
    at_x = x ^ near(fresh // 8 % 4, first ^ 2, first)
    new = PREFIX + shard * new_rows + (at_z * NX + at_x) * 8 + fresh % 8
    return jnp.where(within < old_rows, shard * old_rows + within, new)


def rms_scale(values, gain):
    return values * lax.rsqrt(jnp.mean(values * values, axis=-1, keepdims=True) + EPS) * gain


def stage_kernel(source_ref, target_ref, sem):
    copy = pltpu.make_async_copy(source_ref, target_ref, sem)
    copy.start()
    copy.wait()


def stage(value):
    return pl.pallas_call(
        stage_kernel,
        name="stage",
        out_shape=jax.ShapeDtypeStruct(value.shape, value.dtype),
        in_specs=[pl.BlockSpec(memory_space=pl.ANY)],
        out_specs=pl.BlockSpec(memory_space=pltpu.VMEM),
        scratch_shapes=[pltpu.SemaphoreType.DMA],
        compiler_params=pltpu.CompilerParams(vmem_limit_bytes=6 * 1024 * 1024),
        cost_estimate=pl.CostEstimate(flops=0, bytes_accessed=2 * value.size, transcendentals=0),
    )(value)


def encode_kernel(count, *refs):
    blocks = refs[:count]
    picks = refs[count : 2 * count]
    own_ref, sib_ref, params_ref, codes_ref, rows_ref = refs[2 * count :]
    size = blocks[0].shape[0]
    lats = own_ref.shape[1]
    for i in range(count):
        rows_ref[i * size : (i + 1) * size, :] = blocks[i][...]
    for side, weights_ref in enumerate((own_ref, sib_ref)):
        there = slice(side * lats, (side + 1) * lats)
        pre = jnp.dot(rows_ref[...], weights_ref[...], preferred_element_type=F32)
        act = jnp.maximum(pre + params_ref[0:1, there] - params_ref[1:2, there], 0.0)
        codes = jnp.where(params_ref[2:3, there] > 0.0, params_ref[3:4, there], act)
        codes = codes.astype(BF16)
        for i in range(count):
            moved = jnp.dot(
                picks[i][...], codes[i * size : (i + 1) * size], preferred_element_type=F32
            )
            codes_ref[i * size : (i + 1) * size, there] = moved.astype(BF16)


def encode(blocks, picks, own, sib, params):
    count = len(blocks)
    size, width = blocks[0].shape
    lats = own.shape[1]
    return pl.pallas_call(
        functools.partial(encode_kernel, count),
        name="encode",
        out_shape=jax.ShapeDtypeStruct((count * size, 2 * lats), BF16),
        scratch_shapes=[pltpu.VMEM((count * size, width), BF16)],
        compiler_params=pltpu.CompilerParams(vmem_limit_bytes=12 * 1024 * 1024),
        cost_estimate=pl.CostEstimate(
            flops=4 * count * size * width * lats,
            bytes_accessed=4 * width * lats + 2 * count * size * (width + 2 * lats),
            transcendentals=0,
        ),
    )(*blocks, *picks, own, sib, params)


def decode_kernel(part, group, codes_ref, own_ref, sib_ref, keep_ref, send_ref):
    size = codes_ref.shape[0]
    lats, width = own_ref.shape
    half = group // 2
    for tile in range(width // 2 // TILE):
        here = slice(tile * TILE, (tile + 1) * TILE)
        there = slice(part * (width // 2) + tile * TILE, part * (width // 2) + (tile + 1) * TILE)
        total = jnp.dot(codes_ref[:, :lats], own_ref[:, there], preferred_element_type=F32)
        total += jnp.dot(codes_ref[:, lats:], sib_ref[:, there], preferred_element_type=F32)
        total = total.astype(BF16)
        for i in range(size // group):
            keep_ref[i * half : (i + 1) * half, here] = total[i * group : i * group + half, :]
            send_ref[i * half : (i + 1) * half, here] = total[i * group + half : (i + 1) * group, :]


def decode(codes, own, sib, part, group):
    size = codes.shape[0]
    lats, width = own.shape
    out = jax.ShapeDtypeStruct((size // 2, width // 2), BF16)
    return pl.pallas_call(
        functools.partial(decode_kernel, part, group),
        name="decode",
        out_shape=(out, out),
        compiler_params=pltpu.CompilerParams(vmem_limit_bytes=12 * 1024 * 1024),
        cost_estimate=pl.CostEstimate(
            flops=2 * size * lats * width,
            bytes_accessed=2 * (lats * width + 2 * size * lats + size * width // 2),
            transcendentals=0,
        ),
    )(codes, own, sib)


def project_kernel(
    left_ref,
    right_ref,
    gain_ref,
    query_w,
    key_w,
    value_w,
    head_gains,
    cosine_ref,
    sine_ref,
    cache_key,
    cache_value,
    query_ref,
    pairs_ref,
    normed_ref,
):
    part = left_ref.shape[1]
    hd = key_w.shape[1]
    left, right = left_ref[...].astype(F32), right_ref[...].astype(F32)
    square = jnp.sum(left * left, axis=-1, keepdims=True) + jnp.sum(
        right * right, axis=-1, keepdims=True
    )
    scale = lax.rsqrt(square / (2 * part) + EPS)
    normed_ref[:, :part] = (left * scale * gain_ref[0:1, :part]).astype(BF16)
    normed_ref[:, part:] = (right * scale * gain_ref[0:1, part:]).astype(BF16)
    normed = normed_ref[...]

    def turn(values, gain):
        values = rms_scale(values, gain)
        return (
            values * cosine_ref[...] + pltpu.roll(values, hd // 2, axis=1) * sine_ref[...]
        ).astype(BF16)

    old = cache_key.shape[0]
    pairs_ref[:old, :hd] = cache_key[...]
    pairs_ref[:old, hd:] = cache_value[...]
    key = jnp.dot(normed, key_w[...], preferred_element_type=F32)
    pairs_ref[old:, :hd] = turn(key, head_gains[1:2, :])
    value = jnp.dot(normed, value_w[...], preferred_element_type=F32)
    pairs_ref[old:, hd:] = value.astype(BF16)
    query = jnp.dot(normed, query_w[...], preferred_element_type=F32)
    for h in range(query_ref.shape[1] // hd):
        query_ref[:, h * hd : (h + 1) * hd] = turn(
            query[:, h * hd : (h + 1) * hd], head_gains[0:1, :]
        )


def project(left, right, gain, query_w, key_w, value_w, gains, cosine, sine, old_key, old_value):
    rows, hd = left.shape[0], key_w.shape[1]
    width = query_w.shape[0]
    return pl.pallas_call(
        project_kernel,
        name="project",
        out_shape=(
            jax.ShapeDtypeStruct((rows, query_w.shape[1]), BF16),
            jax.ShapeDtypeStruct((old_key.shape[0] + rows, 2 * hd), BF16),
        ),
        scratch_shapes=[pltpu.VMEM((rows, width), BF16)],
        compiler_params=pltpu.CompilerParams(vmem_limit_bytes=12 * 1024 * 1024),
        cost_estimate=pl.CostEstimate(
            flops=8 * rows * width * hd,
            bytes_accessed=8 * width * hd + 2 * rows * width,
            transcendentals=0,
        ),
    )(left, right, gain, query_w, key_w, value_w, gains, cosine, sine, old_key, old_value)


def attend_kernel(
    query_ref,
    own_ref,
    sib_ref,
    key_ctx,
    query_ctx,
    first_ctx,
    out_w,
    keep_z,
    send_z,
    keep_x,
    send_x,
    attended_ref,
    pairs_ref,
):
    rows, hd = query_ref.shape[0], pairs_ref.shape[1] // 2
    pairs_ref[: own_ref.shape[0], :] = own_ref[...]
    pairs_ref[own_ref.shape[0] :, :] = sib_ref[...]
    allowed = (
        (key_ctx[...] <= query_ctx[:, 0:1])
        & (key_ctx[...] > query_ctx[:, 0:1] - WINDOW)
        & (key_ctx[...] >= first_ctx[:, 0:1])
    )
    for h in range(query_ref.shape[1] // hd):
        scores = (
            lax.dot_general(
                query_ref[:, h * hd : (h + 1) * hd],
                pairs_ref[:, :hd],
                (((1,), (1,)), ((), ())),
                preferred_element_type=F32,
            )
            * QUERY_SCALE
        )
        scores = jnp.where(allowed, scores, -1e30)
        newest = jnp.max(scores, axis=-1, keepdims=True)
        weights = jnp.where(allowed, jnp.exp(scores - newest), 0.0)
        total = jnp.sum(weights, axis=-1, keepdims=True)
        mixed = jnp.dot(weights.astype(BF16), pairs_ref[:, hd:], preferred_element_type=F32)
        attended_ref[:, h * hd : (h + 1) * hd] = (mixed / total).astype(BF16)
    attended = attended_ref[...]
    part = out_w.shape[1] // 2
    for tile in range(part // TILE):
        here = slice(tile * TILE, (tile + 1) * TILE)
        left = jnp.dot(attended, out_w[:, here], preferred_element_type=F32).astype(BF16)
        keep_z[:, here] = left[: rows // 2]
        send_z[:, here] = left[rows // 2 :]
        there = slice(part + tile * TILE, part + (tile + 1) * TILE)
        right = jnp.dot(attended, out_w[:, there], preferred_element_type=F32).astype(BF16)
        for i in range(4):
            keep_x[i * 16 : (i + 1) * 16, here] = right[i * 32 : i * 32 + 16]
            send_x[i * 16 : (i + 1) * 16, here] = right[i * 32 + 16 : i * 32 + 32]


def attend(query, own, sib, key_ctx, query_ctx, first_ctx, out_w):
    rows, width = query.shape[0], out_w.shape[1]
    out = jax.ShapeDtypeStruct((rows // 2, width // 2), BF16)
    return pl.pallas_call(
        attend_kernel,
        name="attend",
        out_shape=(out, out, out, out),
        scratch_shapes=[
            pltpu.VMEM((rows, query.shape[1]), BF16),
            pltpu.VMEM((2 * own.shape[0], own.shape[1]), BF16),
        ],
        compiler_params=pltpu.CompilerParams(vmem_limit_bytes=12 * 1024 * 1024),
        cost_estimate=pl.CostEstimate(
            flops=2 * rows * query.shape[1] * (4 * own.shape[0] + width),
            bytes_accessed=2 * (query.shape[1] * width + rows * width + 2 * own.size),
            transcendentals=4 * rows * own.shape[0],
        ),
    )(query, own, sib, key_ctx, query_ctx, first_ctx, out_w)


def split(value, group):
    rows, width = value.shape
    grouped = value.reshape(rows // group, group, width)
    half = group // 2
    return (
        grouped[:, :half].reshape(rows // 2, width),
        grouped[:, half:].reshape(rows // 2, width),
    )


def add(left, right):
    return (left.astype(F32) + right.astype(F32)).astype(BF16)


def reduce_step(value, dim, bits, group):
    keep, send = split(value, group)
    return add(keep, exchange(send, dim, bits))


def swap_halves(value, group):
    keep, send = split(value, group)
    rows, width = value.shape
    half = group // 2
    return jnp.concatenate(
        [send.reshape(-1, half, width), keep.reshape(-1, half, width)], axis=1
    ).reshape(rows, width)


def gather_step(value, dim, bits, group):
    other = exchange(value, dim, bits)
    rows, width = value.shape
    return jnp.concatenate(
        [value.reshape(-1, group, width), other.reshape(-1, group, width)], axis=1
    ).reshape(2 * rows, width)


def per_device(
    resid,
    w_enc,
    b_enc,
    threshold,
    w_dec,
    b_dec,
    clamp_ids,
    clamp_index,
    clamp_table,
    pre_gain,
    w_query,
    w_key,
    w_value,
    q_gain,
    k_gain,
    cache_key,
    cache_value,
    starts,
    w_out,
    post_gain,
):
    seq_place = lax.axis_index("seq")
    lat_place = lax.axis_index("lat")
    core = seq_place % NC
    z, x = lat_place // NX, lat_place % NX
    tok_rows, width = resid.shape
    part = width // 2
    lats = w_enc.shape[1]
    head_size = q_gain.shape[0]

    order = row_order(z, x, core)
    pick = order[:, None] == jnp.arange(tok_rows, dtype=jnp.int32)[None, :]

    with jax.named_scope("swap_weights"):
        offsets = jnp.stack([b_enc, threshold])
        sib_offsets = swap_cores(offsets)
        sib_enc = stage(swap_cores(w_enc))
        sib_dec = stage(swap_cores(w_dec))

    with jax.named_scope("gather_resid"):
        quarter = tok_rows // 4
        piece = 2 * (z % 2) + x % 2
        near = exchange(resid, "y", first_bits)
        query_ctx = PREFIX + seq_place * tok_rows + order
        query_col = jnp.broadcast_to(query_ctx[:, None], (tok_rows, tok_rows))
        first_col = jnp.broadcast_to(
            jnp.sum(jnp.where(pick, starts[None, :], 0), axis=1, keepdims=True),
            (tok_rows, tok_rows),
        )
        key_ctx = key_positions(seq_place // NC, core, z, x, cache_key.shape[0], tok_rows)
        near, sib_enc, query_col, first_col, key_ctx = lax.optimization_barrier(
            (near, sib_enc, query_col, first_col, key_ctx)
        )
        mine = lax.dynamic_slice_in_dim(near, piece * quarter, quarter, 0)
        again, mine = lax.optimization_barrier((resid, mine))
        mine = exchange(mine, "y", second_bits)
        far = exchange(again, "y", second_bits)
        near, mine = lax.optimization_barrier((near, mine))
        left, right = mine[:, :part], mine[:, part:]
        left_more = exchange(left, "x", first_bits)
        right_more = exchange(right, "z", first_bits)
        spot = jnp.arange(tok_rows, dtype=jnp.int32)
        spot = (piece ^ (spot // quarter)) * quarter + spot % quarter
        pick_opposite = (order[:, None] == spot[None, :]).astype(BF16)
        pick_rows = pick.astype(BF16)

    with jax.named_scope("clamp"):
        table_pick = (
            clamp_index[:, None] == jnp.arange(clamp_table.shape[0], dtype=jnp.int32)[None, :]
        )
        values = jnp.sum(jnp.where(table_pick, clamp_table[None, :], 0.0), axis=1)
        spread = jnp.arange(lats, dtype=jnp.int32)
        here = jnp.concatenate(
            [
                (seq_place * NZ * NX + lat_place) * lats + spread,
                ((seq_place ^ 1) * NZ * NX + lat_place) * lats + spread,
            ]
        )
        match = here[None, :] == clamp_ids[:, None]
        clamped = jnp.any(match, axis=0).astype(F32)
        level = jnp.sum(jnp.where(match, values[:, None], 0.0), axis=0)
        params = jnp.concatenate(
            [
                jnp.concatenate([offsets, sib_offsets], axis=1),
                clamped[None, :],
                level[None, :],
            ],
            axis=0,
        )

    def terms(codes):
        return (
            decode(codes, w_dec, sib_dec, 0, 128),
            decode(codes, w_dec, sib_dec, 1, 32),
        )

    def first_exchange(terms_z, terms_x):
        return exchange(terms_z[1], "z", first_bits), exchange(terms_x[1], "x", first_bits)

    def halves(terms_z, terms_x, received):
        sum_z = add(terms_z[0], received[0])
        sum_x = add(terms_x[0], received[1])
        return split(sum_z, 32), split(sum_x, 64)

    def second_exchange(halves_z, halves_x):
        return (
            exchange(halves_z[1], "x", first_bits),
            exchange(halves_x[1], "z", first_bits),
        )

    def plane_sums(halves_z, halves_x, received):
        return jnp.concatenate(
            [add(halves_z[0], received[0]), add(halves_x[0], received[1])], axis=1
        )

    with jax.named_scope("early_tokens"):
        early_codes = encode([resid, near], [pick_rows, pick_rows], w_enc, sib_enc, params)
        early_codes, left_more, right_more = lax.optimization_barrier(
            (early_codes, left_more, right_more)
        )
        left = jnp.concatenate([left, left_more])
        right = jnp.concatenate([right, right_more])
        left = jnp.concatenate([left, exchange(left, "z", first_bits)])
        more = exchange(right, "x", first_bits)
        right = jnp.concatenate(
            [right[:quarter], more[:quarter], right[quarter:], more[quarter:]]
        )
        opposite = jnp.concatenate([left, right], axis=1)
        early_terms = terms(early_codes)
        early_received = first_exchange(*early_terms)
        (far, opposite), _ = lax.optimization_barrier(((far, opposite), early_terms))
    with jax.named_scope("late_tokens"):
        late_terms = terms(
            encode([far, opposite], [pick_rows, pick_opposite], w_enc, sib_enc, params)
        )
        late_received = first_exchange(*late_terms)
        (early_received, _) = lax.optimization_barrier((early_received, late_terms))
        early_halves = halves(*early_terms, early_received)
        early_received = second_exchange(*early_halves)
        late_halves = halves(*late_terms, late_received)
        late_received = second_exchange(*late_halves)
        early_received, _ = lax.optimization_barrier((early_received, late_halves))
        early = plane_sums(*early_halves, early_received)
        late = plane_sums(*late_halves, late_received)

    with jax.named_scope("sum_over_chips"):
        quarter = tok_rows // 4
        near_sums = exchange(early[quarter:], "y", first_bits)
        far_sums = exchange(late[:quarter], "y", second_bits)
        opposite_sums = exchange(late[quarter:], "y", lambda core: 2)
        total = early[:quarter].astype(F32) + near_sums.astype(F32)
        total = (total + far_sums.astype(F32) + opposite_sums.astype(F32)).astype(BF16)
        over_x = swap_halves(exchange(total, "x", second_bits), 16)
        over_z = swap_halves(exchange(total, "z", second_bits), 32)
        over_both = swap_halves(swap_halves(exchange(total, "zx", second_bits), 32), 16)
        total = (total.astype(F32) + over_x.astype(F32)) + (
            over_z.astype(F32) + over_both.astype(F32)
        )
        rest = (total + b_dec).astype(BF16)
        restored = rest[:8]

    with jax.named_scope("gather_restored"):
        rest_z = gather_step(rest[:, :part], "x", first_bits, 16)
        rest_x = gather_step(rest[:, part:], "z", first_bits, 32)
        rest_z = gather_step(rest_z, "z", first_bits, 64)
        rest_x = gather_step(rest_x, "x", first_bits, 16)

    with jax.named_scope("projections"):
        freq = THETA ** (-(jnp.arange(head_size // 2, dtype=F32) * 2.0 / head_size))
        angle = query_ctx.astype(F32)[:, None] * freq[None, :]
        cosine, sine = jnp.cos(angle), jnp.sin(angle)
        cosine = jnp.concatenate([cosine, cosine], axis=1)
        sine = jnp.concatenate([-sine, sine], axis=1)
        query, own_pairs = project(
            rest_z,
            rest_x,
            pre_gain[None, :],
            w_query,
            w_key,
            w_value,
            jnp.stack([q_gain, k_gain]),
            cosine,
            sine,
            cache_key,
            cache_value,
        )

    with jax.named_scope("attention"):
        pairs = jnp.concatenate(
            [
                own_pairs,
                exchange(own_pairs, "y", first_bits),
                exchange(own_pairs, "y", second_bits),
                exchange(own_pairs, "y", lambda place: 2),
            ]
        )
        sib_pairs = swap_cores(pairs)
        keep_z, send_z, keep_x, send_x = attend(
            query, pairs, sib_pairs, key_ctx, query_col, first_col, w_out
        )

    with jax.named_scope("sum_over_heads"):
        out_z = add(keep_z, exchange(send_z, "z", first_bits))
        out_x = add(keep_x, exchange(send_x, "x", first_bits))
        out_z = reduce_step(out_z, "x", first_bits, 32)
        out_x = reduce_step(out_x, "z", first_bits, 64)
        both = jnp.concatenate([out_z, out_x], axis=1)
        mine = both[:8].astype(F32)
        for place, axes in enumerate(("x", "z", "zx")):
            rows = both[8 * place + 8 : 8 * place + 16]
            mine = mine + exchange(rows, axes, second_bits).astype(F32)
        return (restored.astype(F32) + rms_scale(mine, post_gain)).astype(BF16)


def solution(mesh):
    in_specs = (
        P("seq", None),
        P(None, ("seq", "lat")),
        P(("seq", "lat")),
        P(("seq", "lat")),
        P(("seq", "lat"), None),
        P(),
        P(),
        P(),
        P(),
        P(),
        P(None, "lat"),
        P(None, "lat"),
        P(None, "lat"),
        P(),
        P(),
        P("seq", "lat"),
        P("seq", "lat"),
        P("seq"),
        P("lat", None),
        P(),
    )
    out_specs = P(("seq", "lat"), None)
    return jax.shard_map(
        per_device, mesh=mesh, in_specs=in_specs, out_specs=out_specs, check_vma=False
    )
```
